32 devices in a mesh: rep: 2 (over y), dp: 4 (over x, core), tensor: 4 (over z).
Axes of the slice: x: 2, y: 2, z: 4, core: 2. Of those that a mesh axis runs over, the one named last changes fastest.
Arguments:
- activations: bfloat16 [12288, 8192], P(('rep', 'dp'), 'tensor'), parts along dimension 0, may hold values from -6 to 6
- output_gradient: bfloat16 [12288, 2048], P(('rep', 'dp'), 'tensor'), parts along dimension 0, may hold values from -6 to 6
- row_tenant: int32 [12288, 1], P(('rep', 'dp')), parts along dimension 0, may hold values from 0 to 15; in each aligned block of 1536 rows (0 to 1535, 1536 to 3071, ...) at most 192 rows name the same one
- group_row_count: int32 [8], P(('rep', 'dp')), parts along dimension 0, may hold values from 384 to 1536
- tenant_storage_entry: int32 [16], replicated, may hold values from 0 to 15, each once
- key_value_weight: bfloat16 [8192, 2048], P('tensor'), may hold values from -0.125 to 0.125
- adapter_down_maps: bfloat16 [16, 8192, 64], P('dp', 'tensor'), may hold values from -0.23925781 to 0.23925781
- adapter_up_maps: bfloat16 [16, 64, 2048], P('dp', None, 'tensor'), may hold values from -0.125 to 0.125
- down_row_factor: float32 [16, 8192], P('dp', 'tensor'), may hold values from 2 to 60
- down_column_factor: float32 [16, 64], P('dp'), may hold values from 2 to 60
- up_row_factor: float32 [16, 64], P('dp'), may hold values from 0.02 to 0.6
- up_column_factor: float32 [16, 2048], P('dp', 'tensor'), may hold values from 20 to 600
Outputs:
- input_grad: bfloat16 [12288, 8192], P(('rep', 'dp'), 'tensor'), parts along dimension 0
- down_rows: float32 [32, 8192], P(('rep', 'dp'), 'tensor'), parts along dimension 0
- down_cols: float32 [32, 64], P(('rep', 'dp')), parts along dimension 0
- up_rows: float32 [32, 64], P(('rep', 'dp')), parts along dimension 0
- up_cols: float32 [32, 2048], P(('rep', 'dp'), 'tensor'), parts along dimension 0
- down_update: float32 [32, 8192, 64], P(('rep', 'dp'), 'tensor'), parts along dimension 0
- up_update: float32 [32, 64, 2048], P(('rep', 'dp'), None, 'tensor'), parts along dimension 0
The draws below stay inside these ranges and needn't reach their ends.
There are 2 independent parts, one for each index of `rep`. The reference program is written for one: setup_inputs(seed, part) draws one part's arguments, and reference() takes and returns one part's arrays. A program takes and returns all parts, laid end to end along the dimension named above; an argument that names none is the same for every part. Nothing has to cross between parts.
Inputs may be any that keep to these rules, and one draw needn't show every extreme that they name: `row_tenant`: within the rows of one group (aligned blocks of 1536 rows, padding rows included) no tenant is named by more than 192 rows, a bound that some block reaches. Row 1536 g + i is live for i < group_row_count[g]; the other rows of the group are padding. A permutation: tenant t's adapters and factors are stored at entry tenant_storage_entry[t] of the adapter and factor arrays.
All inputs are finite; a program needn't handle non-finite values.
Results may differ from the reference program's by a relative error of at most 0.0029.
Values may be sent and summed in bfloat16 or wider, within the bound.
A program may use at most 128 MiB of HBM per device.

```python
import math
import jax
import jax.numpy as jnp
import numpy as np
from jax import lax

MODEL_WIDTH = 8192
ADAPTER_RANK = 64
TOK = 1536
KEY_VALUE_WIDTH = 2048
TOKENS = 6144
TENANT_TOTAL = 16
TENANT_ROW_LIMIT = 192
N_DP = 4


def plant(drawn, own_key, low, top_value):
    longest = drawn.shape.index(max(drawn.shape))
    spots = []
    for shift in (0, 1):
        where = [jax.random.randint(jax.random.fold_in(own_key, axis), (), 0, length) for axis, length in enumerate(drawn.shape)]
        where[longest] = (where[longest] + shift) % drawn.shape[longest]
        spots.append(tuple(where))
    return drawn.at[spots[0]].set(low).at[spots[1]].set(top_value)


def block_levels(stream_key, extent, split, smallest, high):
    def one(dim, parts):
        draws = jax.random.uniform(jax.random.fold_in(jax.random.fold_in(stream_key, 6), dim), (parts,), jnp.float32, smallest / len(split), high / len(split))
        return jnp.repeat(jnp.exp(draws), extent[dim] // parts).reshape((-1,) + (1,) * (len(extent) - dim - 1))

    loudness = one(*split[0])
    for cut in split[1:]:
        loudness = loudness * one(*cut)
    return loudness


def shared_out(own_key, own, number, rows, count, top, most, lean):
    ranking = jax.random.permutation(own_key, count)
    heavy_load, ordinary = load_shares(count, rows * top, most, lean, True), load_shares(count, rows * top, most, lean, False)
    places = jnp.arange(count)

    def named(tallies, turn):
        used = int((tallies > 0).sum())
        fixed = max(1, used // 4)
        moved = fixed + (places - fixed + turn * (used - fixed)) % max(1, count - fixed)
        return jnp.zeros((count,), jnp.int32).at[ranking[jnp.where(places < fixed, places, moved)]].set(jnp.asarray(tallies, jnp.int32))

    tallies = jnp.where(number % 4 == 0, named(heavy_load, number // 4), named(ordinary, number - number // 4 - 1))
    mixed = jax.random.permutation(jax.random.fold_in(own, 3), count)
    source_of, taker = mixed[0:count // 2 * 2:2], mixed[1:count // 2 * 2:2]
    margin = jnp.minimum(tallies[source_of] - 1, most - tallies[taker]) // 2
    margin = jnp.where((source_of == ranking[0]) | (taker == ranking[0]) | (tallies[taker] == 0), 0, jnp.maximum(margin, 0))
    moved = jax.random.randint(jax.random.fold_in(own, 4), (count // 2,), 0, 1 << 20) % (margin + 1)
    tallies = tallies.at[source_of].add(-moved).at[taker].add(moved)
    members = jnp.searchsorted(jnp.cumsum(tallies), jnp.arange(rows * top), side="right").astype(jnp.int32)
    table = members.reshape(top, rows).T
    table = table[jax.random.permutation(jax.random.fold_in(own, 1), rows)]
    turn = jax.random.randint(jax.random.fold_in(own, 2), (rows, 1), 0, top)
    return jnp.take_along_axis(table, (jnp.arange(top)[None, :] + turn) % top, axis=1)


def load_shares(number_of, total, limit, skew, full):
    portions = [(1 << 20) // math.isqrt(rank ** skew) + 1 for rank in range(1, number_of + 1)]
    largest = limit if full else min(limit, max(-(-total // number_of), total * portions[0] // sum(portions)))
    least = 1 if total - largest >= number_of - 1 else 0
    given, spare = [largest] + [least] * (number_of - 1), total - largest - least * (number_of - 1)
    while spare > 0:
        free = [i for i in range(1, number_of) if given[i] < largest] or [i for i in range(1, number_of) if given[i] < limit]
        whole, remaining = sum([portions[i] for i in free]), spare
        for i in free:
            more = min(limit - given[i], max(1, remaining * portions[i] // whole), spare)
            given[i] = given[i] + more
            spare = spare - more
    return np.array(given)


def bell_draw(rng, dims, spread, bound, shards=(), kind=jnp.bfloat16):
    drawn = jax.random.normal(rng, dims, jnp.float32) * spread
    if len(shards) > 0:
        drawn = block_levels(rng, dims, shards, -0.22, 0.18) * drawn
    return jnp.clip(drawn, min=-bound, max=bound).astype(kind)


def setup_inputs(seed: int = 0, part: int = 0) -> dict:
    splits = jax.random.split(jax.random.key(seed), 13)
    part_keys = jax.random.split(jax.random.fold_in(splits[12], part), 13)
    activations = bell_draw(part_keys[0], (TOKENS, MODEL_WIDTH), 1.0, 6.0, ((0, 4), (1, 4)))
    output_gradient = bell_draw(part_keys[1], (TOKENS, KEY_VALUE_WIDTH), 1.0, 6.0, ((0, 4), (1, 4)))
    row_tenant_keys = jax.random.split(jax.random.fold_in(part_keys[2], 1), TOKENS // TOK)
    row_tenant_turns = jax.random.permutation(jax.random.fold_in(part_keys[2], 3), TOKENS // TOK)
    row_tenant = jax.vmap(lambda own, number: shared_out(jax.random.fold_in(part_keys[2], 2), own, number, TOK, TENANT_TOTAL, 1, TENANT_ROW_LIMIT, 2))(row_tenant_keys, row_tenant_turns).reshape((TOKENS, 1))
    group_row_count = plant(jax.random.randint(part_keys[3], (N_DP,), TOK // 4, TOK + 1), jax.random.fold_in(part_keys[3], 1), TOK // 4, TOK).astype(jnp.int32)
    tenant_storage_entry = jax.random.permutation(splits[4], TENANT_TOTAL).astype(jnp.int32)
    key_value_weight = bell_draw(splits[5], (MODEL_WIDTH, KEY_VALUE_WIDTH), KEY_VALUE_WIDTH ** -0.5, 0.125, ((0, 4),))
    adapter_down_maps = bell_draw(splits[6], (TENANT_TOTAL, MODEL_WIDTH, ADAPTER_RANK), 0.04, 0.23925781, ((0, 4), (1, 4)))
    adapter_up_maps = bell_draw(splits[7], (TENANT_TOTAL, ADAPTER_RANK, KEY_VALUE_WIDTH), KEY_VALUE_WIDTH ** -0.5, 0.125, ((0, 4), (2, 4)))
    down_row_factor = jnp.clip(jnp.exp(math.log(60.0) - 3.4011974 * jax.random.uniform(splits[8], (TENANT_TOTAL, MODEL_WIDTH), jnp.float32) ** block_levels(splits[8], (TENANT_TOTAL, MODEL_WIDTH), ((0, 4), (1, 4)), -0.2, 0.2)), 2.0, 60.0)
    down_column_factor = jnp.clip(jnp.exp(math.log(60.0) - 3.4011974 * jax.random.uniform(splits[9], (TENANT_TOTAL, ADAPTER_RANK), jnp.float32) ** block_levels(splits[9], (TENANT_TOTAL, ADAPTER_RANK), ((0, 4),), -0.2, 0.2)), 2.0, 60.0)
    up_row_factor = jnp.clip(jnp.exp(math.log(0.6) - 3.4011974 * jax.random.uniform(splits[10], (TENANT_TOTAL, ADAPTER_RANK), jnp.float32) ** block_levels(splits[10], (TENANT_TOTAL, ADAPTER_RANK), ((0, 4),), -0.2, 0.2)), 0.02, 0.6)
    up_column_factor = jnp.clip(jnp.exp(math.log(600.0) - 3.4011974 * jax.random.uniform(splits[11], (TENANT_TOTAL, KEY_VALUE_WIDTH), jnp.float32) ** block_levels(splits[11], (TENANT_TOTAL, KEY_VALUE_WIDTH), ((0, 4), (1, 4)), -0.2, 0.2)), 20.0, 600.0)
    return dict(activations=activations, output_gradient=output_gradient, row_tenant=row_tenant, group_row_count=group_row_count, tenant_storage_entry=tenant_storage_entry, key_value_weight=key_value_weight, adapter_down_maps=adapter_down_maps, adapter_up_maps=adapter_up_maps, down_row_factor=down_row_factor, down_column_factor=down_column_factor, up_row_factor=up_row_factor, up_column_factor=up_column_factor)


adapter_scale = 0.25
decay_rate = 0.9
tiny_floor = 1e-30

def slot_layout(tenant_col, tenant_storage_entry, row_limit):
    tenants = tenant_col[:, 0]
    count_rows = tenants.shape[0]
    entries = tenant_storage_entry.shape[0]
    onehot = (tenants[:, None] == jnp.arange(entries, dtype=jnp.int32)[None, :]).astype(jnp.int32)
    position = jnp.cumsum(onehot, axis=0) - onehot
    within = lax.optimization_barrier(jnp.sum(position * onehot, axis=1)).astype(jnp.int32)
    entry_of = lax.optimization_barrier(jnp.sum(onehot * tenant_storage_entry[None, :], axis=1)).astype(jnp.int32)
    target = (entry_of * row_limit + within).astype(jnp.int32)
    lookup = jnp.full((entries * row_limit,), count_rows, jnp.int32).at[target].set(jnp.arange(count_rows, dtype=jnp.int32))
    return (target, lookup)

def reference(activations, output_gradient, row_tenant, group_row_count, tenant_storage_entry, key_value_weight, adapter_down_maps, adapter_up_maps, down_row_factor, down_column_factor, up_row_factor, up_column_factor):
    live_mask = (jnp.arange(TOK, dtype=jnp.int32)[None, :] < group_row_count[:, None]).reshape(TOKENS, 1)
    masked = jnp.where(live_mask, output_gradient, jnp.zeros_like(output_gradient))
    frozen = jnp.dot(masked, key_value_weight.T, preferred_element_type=jnp.float32)
    target, lookup = jax.vmap(lambda column: slot_layout(column, tenant_storage_entry, TENANT_ROW_LIMIT))(row_tenant.reshape(N_DP, TOK, 1))
    padded_x = jnp.concatenate([activations.reshape(N_DP, TOK, MODEL_WIDTH), jnp.zeros((N_DP, 1, MODEL_WIDTH), activations.dtype)], axis=1)
    padded_g = jnp.concatenate([masked.reshape(N_DP, TOK, KEY_VALUE_WIDTH), jnp.zeros((N_DP, 1, KEY_VALUE_WIDTH), masked.dtype)], axis=1)
    group_numbers = jnp.arange(N_DP, dtype=jnp.int32)[:, None]

    def per_entry(written_rows, entry_number):
        storage_index = lax.dynamic_slice_in_dim(lookup, entry_number * TENANT_ROW_LIMIT, TENANT_ROW_LIMIT, 1)
        picked_input = padded_x[group_numbers, storage_index].reshape(N_DP * TENANT_ROW_LIMIT, MODEL_WIDTH)
        picked_gradient = padded_g[group_numbers, storage_index].reshape(N_DP * TENANT_ROW_LIMIT, KEY_VALUE_WIDTH)
        down_entry_map = adapter_down_maps[entry_number]
        up_entry_map = adapter_up_maps[entry_number]
        proj_down = jnp.dot(picked_input, down_entry_map, preferred_element_type=jnp.float32)
        proj_up = jnp.dot(picked_gradient, up_entry_map.T, preferred_element_type=jnp.float32)
        rounded_down = proj_down.astype(jnp.bfloat16)
        rounded_up = proj_up.astype(jnp.bfloat16)
        down_gradient = adapter_scale * jnp.dot(picked_input.T, rounded_up, preferred_element_type=jnp.float32)
        up_gradient = adapter_scale * jnp.dot(rounded_down.T, picked_gradient, preferred_element_type=jnp.float32)
        adapter_branch = (adapter_scale * jnp.dot(rounded_up, down_entry_map.T, preferred_element_type=jnp.float32)).astype(jnp.bfloat16)
        written_rows = written_rows.at[group_numbers, storage_index].set(adapter_branch.reshape(N_DP, TENANT_ROW_LIMIT, MODEL_WIDTH))
        return (written_rows, (down_gradient, up_gradient))
    blank_rows = jnp.zeros((N_DP, TOK + 1, MODEL_WIDTH), jnp.bfloat16)
    side_all, grads = lax.scan(per_entry, blank_rows, jnp.arange(TENANT_TOTAL, dtype=jnp.int32))
    down_gradient, up_gradient = grads
    side_rows = side_all[:, :TOK, :].reshape(TOKENS, MODEL_WIDTH)
    input_grad = (frozen + side_rows.astype(jnp.float32)).astype(jnp.bfloat16)
    square_down = down_gradient * down_gradient + tiny_floor
    square_up = up_gradient * up_gradient + tiny_floor
    down_rows = decay_rate * down_row_factor + (1.0 - decay_rate) * lax.optimization_barrier(jnp.mean(square_down, axis=2))
    down_cols = decay_rate * down_column_factor + (1.0 - decay_rate) * lax.optimization_barrier(jnp.mean(square_down, axis=1))
    up_rows = decay_rate * up_row_factor + (1.0 - decay_rate) * lax.optimization_barrier(jnp.mean(square_up, axis=2))
    up_cols = decay_rate * up_column_factor + (1.0 - decay_rate) * lax.optimization_barrier(jnp.mean(square_up, axis=1))
    second_down = down_rows[:, :, None] * down_cols[:, None, :] / lax.optimization_barrier(jnp.mean(down_rows, axis=1))[:, None, None]
    second_up = up_rows[:, :, None] * up_cols[:, None, :] / lax.optimization_barrier(jnp.mean(up_rows, axis=1))[:, None, None]
    down_update = down_gradient * lax.rsqrt(second_down)
    up_update = up_gradient * lax.rsqrt(second_up)
    return (input_grad, down_rows, down_cols, up_rows, up_cols, down_update, up_update)
```

```python
import jax
import jax.numpy as jnp
from jax import lax
from jax.sharding import PartitionSpec as P

adapter_scale = 0.25
decay_rate = 0.9
tiny_floor = 1e-30
f32 = jnp.float32
bf16 = jnp.bfloat16
CORES = 2


def dot(a, b, ca, cb):
    return lax.dot_general(a, b, (((ca,), (cb,)), ((), ())), preferred_element_type=f32)


def chip_shift(value, groups, step):
    chips = groups // CORES
    pairs = [(d, (d // CORES + step) % chips * CORES + d % CORES) for d in range(groups)]
    return lax.ppermute(value, "dp", pairs)


def core_swap(value, groups):
    return lax.ppermute(value, "dp", [(d, d ^ 1) for d in range(groups)])


def ring_shift(value, size, step):
    return lax.ppermute(value, "tensor", [(t, (t + step) % size) for t in range(size)])


PAIRS = ((0, 1), (1, 0), (2, 3), (3, 2))
CROSS = ((1, 2), (2, 1))
OUTWARD = ((1, 0), (2, 3))


def hop(value, pairs):
    return lax.ppermute(value, "tensor", list(pairs))


def total_small(value, size):
    if size > 8:
        return lax.psum(value, "tensor")
    me = lax.axis_index("tensor")
    parts = jnp.zeros((size,) + value.shape, value.dtype)
    parts = lax.dynamic_update_index_in_dim(parts, value, me, 0)
    for step in range(1, size):
        got = ring_shift(value, size, step)
        parts = lax.dynamic_update_index_in_dim(parts, got, (me - step) % size, 0)
    return jnp.sum(parts, axis=0)


def total_rows(value, size):
    if size > 8:
        return lax.psum(value, "tensor").astype(bf16)
    me = lax.axis_index("tensor")
    rows = value.shape[0] // size

    def piece(index):
        return lax.dynamic_slice_in_dim(value, index % size * rows, rows, 0)

    total = piece(me)
    for step in range(1, size):
        total = total + ring_shift(piece(me + step), size, step)
    mine = total.astype(bf16)
    out = jnp.zeros(value.shape, bf16)
    out = lax.dynamic_update_slice_in_dim(out, mine, me * rows, 0)
    for step in range(1, size):
        got = ring_shift(mine, size, step)
        out = lax.dynamic_update_slice_in_dim(out, got, (me - step) % size * rows, 0)
    return out


def shards(
    activations,
    output_gradient,
    row_tenant,
    group_row_count,
    tenant_storage_entry,
    key_value_weight,
    adapter_down_maps,
    adapter_up_maps,
    down_row_factor,
    down_column_factor,
    up_row_factor,
    up_column_factor,
):
    groups = lax.axis_size("dp")
    size = lax.axis_size("tensor")
    chips = groups // CORES
    owned, depth, rank = adapter_down_maps.shape
    width = adapter_up_maps.shape[2]
    entries = owned * groups
    count_rows = activations.shape[0]
    full_width = depth * size
    pair_width = key_value_weight.shape[1]
    here = lax.axis_index("dp")
    chip, core = here // CORES, here % CORES
    line = size == 4
    spot = lax.axis_index("tensor")
    if line:
        middle = (spot == 1) | (spot == 2)
        near = hop(output_gradient, PAIRS)
        across = hop(output_gradient, CROSS)
    else:
        gathered = lax.all_gather(output_gradient, "tensor", axis=1, tiled=True)
    own_maps = jnp.concatenate(
        [adapter_down_maps.transpose(0, 2, 1), adapter_up_maps], axis=2
    ).reshape(owned * rank, depth + width)
    blocks = []
    for s in range(chips):
        column = own_maps if s == 0 else chip_shift(own_maps, groups, s)
        blocks.append(jnp.concatenate([column, core_swap(column, groups)], axis=0))
    live = jnp.arange(count_rows, dtype=jnp.int32)[:, None] < group_row_count[0]
    masked = jnp.where(live, output_gradient, jnp.zeros_like(output_gradient))
    tse = tenant_storage_entry
    owner = tse // owned
    place = (
        (chip - owner // CORES) % chips * CORES + (owner % CORES != core).astype(jnp.int32)
    ) * owned + tse % owned
    tenants = row_tenant[:, 0]
    place_of = jnp.sum(
        jnp.where(
            tenants[:, None] == jnp.arange(entries, dtype=jnp.int32)[None, :], place[None, :], 0
        ),
        axis=1,
    )
    span = CORES * owned * rank
    pair = 2 * rank
    lanes = jnp.arange(span, dtype=jnp.int32)[None, :] // rank

    def wide(s):
        return place_of[:, None] == lanes + s * CORES * owned

    def pick(s, product):
        kept = jnp.where(wide(s), product, 0.0)
        both = kept[:, :pair]
        for i in range(1, span // pair):
            both = both + kept[:, i * pair : (i + 1) * pair]
        return both

    picked_down = picked_up = 0.0
    for s in range(chips):
        picked_down += pick(s, dot(activations, blocks[s][:, :depth], 1, 1))
        picked_up += pick(s, dot(masked, blocks[s][:, depth:], 1, 1))
    partial = jnp.concatenate(
        [
            picked_down[:, :rank] + picked_down[:, rank:],
            picked_up[:, :rank] + picked_up[:, rank:],
        ],
        axis=1,
    )
    if line:
        partial, near, across = lax.optimization_barrier((partial, near, across))
    rounded = total_rows(partial, size)
    if line:
        rounded, near, across = lax.optimization_barrier((rounded, near, across))
        second = hop(near, CROSS) + hop(across, OUTWARD)
        third = jnp.where(middle, across, hop(second, OUTWARD))
        shards_of = (output_gradient, near, second, third)
    zero = jnp.zeros((), bf16)
    repeat_down = jnp.tile(rounded[:, :rank], (1, span // rank))
    repeat_up = jnp.tile(rounded[:, rank:], (1, span // rank))
    half = owned * rank
    spreads = [jnp.where(wide(s), repeat_up, zero) for s in range(chips)]
    pieces = []
    for s in list(range(1, chips)) + [0]:
        spread_down = jnp.where(wide(s), repeat_down, zero)
        terms = [
            adapter_scale
            * jnp.concatenate(
                [
                    dot(spreads[s][:, k : k + half], activations, 0, 0),
                    dot(spread_down[:, k : k + half], masked, 0, 0),
                ],
                axis=1,
            )
            for k in (half, 0)
        ]
        summed = terms[1] + core_swap(terms[0], groups)
        pieces.append(chip_shift(summed.astype(bf16), groups, -s) if s else summed)
    side = lax.optimization_barrier(
        (
            adapter_scale
            * dot(
                jnp.concatenate(spreads, axis=1),
                jnp.concatenate([b[:, :depth] for b in blocks], axis=0),
                1,
                0,
            )
        ).astype(bf16)
    )
    if line:
        frozen = 0.0
        for k, piece in enumerate(shards_of):
            columns = lax.dynamic_slice_in_dim(
                key_value_weight, (spot ^ k) * width, width, 1
            )
            frozen = frozen + dot(piece, columns, 1, 1)
        frozen = jnp.where(live, frozen, 0.0)
    else:
        frozen = jnp.where(live, dot(gathered, key_value_weight, 1, 1), 0.0)
    input_grad = (frozen + side.astype(f32)).astype(bf16)
    pieces, input_grad = lax.optimization_barrier((pieces, input_grad))
    grads = sum(p.astype(f32) for p in pieces)
    grads = grads.reshape(owned, rank, depth + width)
    down_gradient, up_gradient = grads[:, :, :depth], grads[:, :, depth:]
    square_down = down_gradient * down_gradient + tiny_floor
    square_up = up_gradient * up_gradient + tiny_floor
    down_rows = decay_rate * down_row_factor + (1.0 - decay_rate) * jnp.mean(square_down, axis=1)
    up_cols = decay_rate * up_column_factor + (1.0 - decay_rate) * jnp.mean(square_up, axis=1)
    stats = jnp.concatenate(
        [
            jnp.sum(square_down, axis=2),
            jnp.sum(square_up, axis=2),
            jnp.broadcast_to(jnp.sum(down_rows, axis=1)[:, None], (owned, pair)),
        ],
        axis=1,
    )
    stats = total_small(stats, size)
    column_total, row_total = stats[:, :rank], stats[:, rank:pair]
    rows_sum = stats[:, pair]
    down_cols = decay_rate * down_column_factor + (1.0 - decay_rate) * (column_total / full_width)
    up_rows = decay_rate * up_row_factor + (1.0 - decay_rate) * (row_total / pair_width)
    second_down = (
        down_rows[:, None, :] * down_cols[:, :, None] / (rows_sum / full_width)[:, None, None]
    )
    second_up = up_rows[:, :, None] * up_cols[:, None, :] / jnp.mean(up_rows, axis=1)[:, None, None]
    down_update = (down_gradient * lax.rsqrt(second_down)).transpose(0, 2, 1)
    up_update = up_gradient * lax.rsqrt(second_up)
    return (input_grad, down_rows, down_cols, up_rows, up_cols, down_update, up_update)


def solution(mesh):
    in_specs = (
        P(("rep", "dp"), "tensor"),
        P(("rep", "dp"), "tensor"),
        P(("rep", "dp"), None),
        P(("rep", "dp")),
        P(),
        P("tensor", None),
        P("dp", "tensor", None),
        P("dp", None, "tensor"),
        P("dp", "tensor"),
        P("dp", None),
        P("dp", None),
        P("dp", "tensor"),
    )
    out_specs = (
        P(("rep", "dp"), "tensor"),
        P(("rep", "dp"), "tensor"),
        P(("rep", "dp"), None),
        P(("rep", "dp"), None),
        P(("rep", "dp"), "tensor"),
        P(("rep", "dp"), "tensor", None),
        P(("rep", "dp"), None, "tensor"),
    )
    return jax.shard_map(shards, mesh=mesh, in_specs=in_specs, out_specs=out_specs, check_vma=False)
```

```python
import functools

import jax
import jax.numpy as jnp
from jax import lax
from jax.experimental import pallas as pl
from jax.experimental.pallas import tpu as pltpu
from jax.sharding import PartitionSpec as P

adapter_scale = 0.25
decay_rate = 0.9
tiny_floor = 1e-30
f32 = jnp.float32
bf16 = jnp.bfloat16
CORES = 2
VMEM_LIMIT = 66_000_000
MESH = pl.DeviceIdType.MESH


def dot_nt(a, b):
    return lax.dot_general(a, b, (((1,), (1,)), ((), ())), preferred_element_type=jnp.float32)


def dot_nn(a, b):
    return lax.dot_general(a, b, (((1,), (0,)), ((), ())), preferred_element_type=jnp.float32)


def fused_kernel(
    rank,
    x_hbm,
    g_hbm,
    w_hbm,
    down_hbm,
    up_hbm,
    place_col,
    place_row,
    row_factor,
    column_factor,
    small_factor,
    grad_out,
    rows_out,
    columns_out,
    small_out,
    down_out,
    up_out,
    xv,
    gv,
    wv,
    bd,
    bu,
    acc,
    part,
    far_in,
    near_in,
    cross_in,
    cross_out,
    rounded,
    turned,
    spread,
    side_lhs,
    pair_out,
    pair_in,
    far_out,
    far_got,
    total,
    stage,
    stat_all,
    load_sem,
    ag_send,
    ag_recv,
    own_send,
    own_recv,
    x_send,
    x_recv,
    y_send,
    y_recv,
    c_send,
    c_recv,
    rs_send,
    rs_recv,
    pair_send,
    pair_recv,
    far_send,
    far_recv,
    stat_send,
    stat_recv,
    out_sem,
    upd_sem,
):
    z = lax.axis_index("tensor")
    d = lax.axis_index("dp")
    rep = lax.axis_index("rep")
    middle = (z == 1) | (z == 2)
    end = (z == 0) | (z == 3)
    rows, depth = xv.shape
    width = gv.shape[2]
    span = bd.shape[1]
    owned = span // rank
    chunks = ag_recv.shape[1]
    size = rows // chunks
    half = rows // 2
    tile = rows // 4
    cols = 512 if depth % 512 == 0 else depth
    wide = depth // cols
    pieces = total.shape[0]
    piece = total.shape[2]
    quarter = x_recv.shape[0]
    step = span // 2 // quarter
    near_at = pl.multiple_of(z // 2 * half, half)
    far_at = pl.multiple_of((1 - z // 2) * half, half)

    def remote(src, dst, ss, rs, **where):
        return pltpu.make_async_remote_copy(
            src_ref=src, dst_ref=dst, send_sem=ss, recv_sem=rs, device_id=where, device_id_type=MESH
        )

    def local(src, dst, sem):
        return pltpu.make_async_copy(src, dst, sem)

    loads = [
        local(g_hbm, gv.at[0], load_sem.at[0]),
        local(down_hbm, bd.at[0], load_sem.at[1]),
        local(up_hbm, bu.at[0], load_sem.at[2]),
        local(x_hbm, xv, load_sem.at[3]),
    ]
    for k in range(4):
        at = pl.multiple_of((z ^ k) * width, width)
        loads.append(local(w_hbm.at[:, pl.ds(at, width)], wv.at[k], load_sem.at[4 + k]))
    for copy in loads:
        copy.start()

    barrier = pltpu.get_barrier_semaphore()
    peers = [
        {"tensor": z ^ 1},
        {"tensor": z ^ 2},
        {"tensor": z ^ 3},
        {"dp": d ^ 1},
        {"dp": d ^ 2},
        {"rep": rep ^ 1},
    ]
    for peer in peers:
        pl.semaphore_signal(barrier, inc=1, device_id=peer, device_id_type=MESH)
    pl.semaphore_wait(barrier, len(peers))

    def chunk(i):
        return pl.ds(i * size, size)

    def to_pair(i):
        return remote(
            g_hbm.at[chunk(i)], gv.at[1, chunk(i)], ag_send.at[0, i], ag_recv.at[0, i], tensor=z ^ 1
        )

    def to_cross(i):
        return remote(
            g_hbm.at[chunk(i)], gv.at[3, chunk(i)], ag_send.at[1, i], ag_recv.at[2, i], tensor=z ^ 3
        )

    def relay_cross(i):
        return remote(
            gv.at[1, chunk(i)], gv.at[2, chunk(i)], ag_send.at[2, i], ag_recv.at[1, i], tensor=z ^ 3
        )

    def relay_end(i):
        return remote(
            gv.at[3, chunk(i)], gv.at[2, chunk(i)], ag_send.at[3, i], ag_recv.at[1, i], tensor=z ^ 1
        )

    def relay_last(i):
        return remote(
            gv.at[2, chunk(i)], gv.at[3, chunk(i)], ag_send.at[4, i], ag_recv.at[2, i], tensor=z ^ 1
        )

    def arrive(slot, i):
        remote(
            gv.at[slot, chunk(i)], gv.at[slot, chunk(i)], ag_send.at[0, i], ag_recv.at[slot - 1, i], tensor=z ^ 1
        ).wait_recv()

    for i in range(chunks):
        to_pair(i).start()

        @pl.when(middle)
        def _():
            to_cross(i).start()

    maps = ((down_hbm, bd), (up_hbm, bu))

    def own(m):
        src, dst = maps[m]
        return remote(src, dst.at[1], own_send.at[m], own_recv.at[m], dp=d ^ 1)

    mine = rep * (span // 2)
    other = (1 - rep) * (span // 2)

    def part_rows(base, q):
        return pl.ds(pl.multiple_of(base + q * step, step), step)

    def over_x(q, m):
        src, dst = maps[m]
        at = part_rows(mine, q)
        return remote(src.at[at], dst.at[2, at], x_send.at[q, m], x_recv.at[q, m], dp=d ^ 2)

    def over_y(q, m):
        dst = maps[m][1]
        at = part_rows(mine, q)
        return remote(dst.at[2, at], dst.at[2, at], y_send.at[q, m], y_recv.at[q, m], rep=rep ^ 1)

    def over_core(q, m, base, k):
        dst = maps[m][1]
        at = part_rows(base, q)
        return remote(dst.at[2, at], dst.at[3, at], c_send.at[k, q, m], c_recv.at[k, q, m], dp=d ^ 1)

    for q in range(quarter):
        for m in range(2):
            over_x(q, m).start()
    for m in range(2):
        own(m).start()

    lane = lax.broadcasted_iota(jnp.int32, (tile, span), 1) // rank
    low = lax.broadcasted_iota(jnp.int32, (tile, 2 * rank), 1) < rank

    def project(b):
        def body(i, _):
            at = pl.ds(pl.multiple_of(i * tile, tile), tile)
            hit = place_col[at, :] == lane + b * owned

            def fold(product):
                kept = jnp.where(hit, product, 0.0)
                both = kept[:, : 2 * rank]
                for j in range(1, span // (2 * rank)):
                    both = both + kept[:, j * 2 * rank : (j + 1) * 2 * rank]
                return both + pltpu.roll(both, rank, axis=1)

            new = jnp.where(
                low,
                fold(dot_nt(xv[at, :], bd[b])),
                fold(dot_nt(gv[0, at, :], bu[b])),
            )
            part[at, :] = new if b == 0 else part[at, :] + new
            return 0

        lax.fori_loop(0, rows // tile, body, 0)

    def frozen(k, first, start, count):
        def body(t, _):
            i, j = t // wide, t % wide
            at = pl.ds(pl.multiple_of(i * tile, tile), tile)
            over = pl.ds(pl.multiple_of(j * cols, cols), cols)
            new = dot_nt(gv[k, at, :], wv[k, over, :])
            acc[at, over] = new if first else acc[at, over] + new
            return 0

        lax.fori_loop(start * wide, (start + count) * wide, body, 0)

    for k in range(4):
        loads[k].wait()
    project(0)
    for m in range(2):
        own(m).wait_recv()
    loads[4].wait()
    for q in range(quarter):
        if q == quarter - 2:
            project(1)
        else:
            frozen(0, True, min(q, 2), 1)
        for m in range(2):
            over_x(q, m).wait_recv()
            over_y(q, m).start()
            over_core(q, m, mine, 0).start()
    for q in range(quarter):
        for m in range(2):
            dst = maps[m][1]
            at = part_rows(other, q)
            remote(dst.at[2, at], dst.at[2, at], y_send.at[q, m], y_recv.at[q, m], rep=rep ^ 1).wait_recv()
            over_core(q, m, other, 1).start()
        if q == 0:
            frozen(0, True, 3, 1)
    project(2)
    for k in range(2):
        for q in range(quarter):
            for m in range(2):
                at = part_rows(mine if k == 0 else other, q)
                dst = maps[m][1]
                remote(dst.at[2, at], dst.at[3, at], c_send.at[k, q, m], c_recv.at[k, q, m], dp=d ^ 1).wait_recv()
    project(3)

    near = pl.ds(near_at, half)
    far = pl.ds(far_at, half)
    send_far = remote(part.at[far], far_in, rs_send.at[0], rs_recv.at[0], tensor=z ^ 1)
    send_near = remote(part.at[near], near_in, rs_send.at[1], rs_recv.at[1], tensor=z ^ 1)
    send_cross = remote(cross_out, cross_in, rs_send.at[2], rs_recv.at[2], tensor=z ^ 3)
    near_end = remote(rounded.at[near], rounded.at[near], rs_send.at[3], rs_recv.at[3], tensor=z ^ 1)
    near_cross = remote(rounded.at[near], rounded.at[near], rs_send.at[4], rs_recv.at[4], tensor=z ^ 3)
    far_end = remote(rounded.at[far], rounded.at[far], rs_send.at[5], rs_recv.at[4], tensor=z ^ 1)

    def forward(i):
        @pl.when(middle)
        def _():
            arrive(3, i)
            relay_end(i).start()
            arrive(1, i)
            relay_cross(i).start()

    @pl.when(end)
    def _():
        send_far.start()
        send_near.start()

    for i in range(chunks // 3):
        forward(i)

    @pl.when(middle)
    def _():
        send_far.wait_recv()
        cross_out[...] = part[far, :] + far_in[...]
        send_cross.start()

    loads[5].wait()

    @pl.when(middle)
    def _():
        send_near.wait_recv()
        send_cross.wait_recv()
        rounded[near, :] = ((part[near, :] + near_in[...]) + cross_in[...]).astype(jnp.bfloat16)
        near_cross.start()
        near_end.start()
        remote(rounded.at[far], rounded.at[far], rs_send.at[4], rs_recv.at[4], tensor=z ^ 3).wait_recv()
        far_end.start()

    for i in range(chunks // 3, chunks):
        forward(i)

    @pl.when(end)
    def _():
        for i in range(chunks):
            arrive(1, i)

    frozen(1, False, 0, 4)

    @pl.when(end)
    def _():
        remote(rounded.at[near], rounded.at[near], rs_send.at[3], rs_recv.at[3], tensor=z ^ 1).wait_recv()
        remote(rounded.at[far], rounded.at[far], rs_send.at[4], rs_recv.at[4], tensor=z ^ 1).wait_recv()

    def turn(i, _):
        at = pl.ds(pl.multiple_of(i * 128, 128), 128)
        turned[:, at] = rounded[at, :].astype(jnp.float32).T.astype(jnp.bfloat16)
        return 0

    lax.fori_loop(0, rows // 128, turn, 0)

    head = lax.broadcasted_iota(jnp.int32, (span, 128), 0) // rank

    def fill(b):
        def body(i, _):
            at = pl.ds(pl.multiple_of(i * 128, 128), 128)
            hit = place_row[:, at] == head + b * owned
            both = turned[:, at].astype(jnp.float32)
            for which, lines in ((0, both[rank:]), (1, both[:rank])):
                lines = jnp.concatenate([lines] * owned, axis=0)
                spread[which, :, at] = jnp.where(hit, lines, 0.0).astype(jnp.bfloat16)
            return 0

        lax.fori_loop(0, rows // 128, body, 0)

    def product(j):
        if j < pieces - 1:
            return 0.25 * dot_nn(spread[0], xv[:, j * piece : (j + 1) * piece])
        return 0.25 * dot_nn(spread[1], gv[0])

    def to_core(k, j):
        return remote(
            pair_out.at[k, j], pair_in.at[k, j], pair_send.at[k, j], pair_recv.at[k, j], dp=d ^ 1
        )

    def to_chip(j):
        return remote(far_out.at[j], far_got.at[j], far_send.at[j], far_recv.at[j], dp=d ^ 2)

    fill(3)
    for j in range(pieces):
        pair_out[0, j] = product(j)
        to_core(0, j).start()
    fill(2)
    for j in range(pieces):
        ours = product(j)
        to_core(0, j).wait_recv()
        far_out[j] = (ours + pair_in[0, j]).astype(jnp.bfloat16)
        to_chip(j).start()

    def last(i):
        @pl.when(middle)
        def _():
            arrive(2, i)
            relay_last(i).start()

    for i in range(chunks // 2):
        last(i)
    fill(1)
    for j in range(pieces):
        pair_out[1, j] = product(j)
        to_core(1, j).start()
    fill(0)
    for j in range(pieces):
        ours = product(j)
        to_core(1, j).wait_recv()
        total[j] = ours + pair_in[1, j]
    for i in range(chunks // 2, chunks):
        last(i)

    @pl.when(end)
    def _():
        for i in range(chunks):
            arrive(2, i)

    loads[6].wait()
    frozen(2, False, 0, 4)

    lane_side = lax.broadcasted_iota(jnp.int32, (tile, 2 * rank), 1) // rank

    def add_side(i, _):
        at = pl.ds(pl.multiple_of(i * tile, tile), tile)
        both = rounded[at, :].astype(jnp.float32)
        both = jnp.where(low, pltpu.roll(both, rank, axis=1), both)
        owner = place_col[at, :]
        for t in range(side_lhs.shape[1] // (2 * rank)):
            side_lhs[:, t * 2 * rank : (t + 1) * 2 * rank] = jnp.where(
                owner == lane_side + 2 * t, both, 0.0
            ).astype(jnp.bfloat16)

        def column(j, _):
            over = pl.ds(pl.multiple_of(j * cols, cols), cols)
            right = bd[:, :, over].reshape(4 * span, cols)
            acc[at, over] = acc[at, over] + 0.25 * dot_nn(side_lhs[...], right)
            return 0

        lax.fori_loop(0, wide, column, 0)
        return 0

    lax.fori_loop(0, rows // tile, add_side, 0)

    share = 1.0 - decay_rate
    line = jnp.zeros((span, 1), jnp.float32)
    upper = jnp.zeros((span, 1), jnp.float32)
    rows_sum = jnp.zeros((owned, 1), jnp.float32)
    for j in range(pieces):
        to_chip(j).wait_recv()
        value = total[j] + far_got[j].astype(jnp.float32)
        total[j] = value
        square = value * value + tiny_floor
        mean = jnp.sum(square.reshape(owned, rank, piece), axis=1) / rank
        if j < pieces - 1:
            over = slice(j * piece, (j + 1) * piece)
            fresh = decay_rate * row_factor[:, over] + share * mean
            rows_out[:, over] = fresh
            rows_sum = rows_sum + jnp.sum(fresh, axis=1, keepdims=True)
            line = line + jnp.sum(square, axis=1, keepdims=True)
        else:
            columns_out[...] = decay_rate * column_factor[...] + share * mean
            upper = jnp.sum(square, axis=1, keepdims=True)
    place = lax.broadcasted_iota(jnp.int32, (span, 128), 1)
    spread_sum = jnp.broadcast_to(rows_sum[:, None, :], (owned, rank, 1)).reshape(span, 1)
    packed = jnp.where(place == 0, line, jnp.where(place == 1, upper, spread_sum))
    stat_all[z] = packed.T[:8, :]

    def to_line(k):
        return remote(
            stat_all.at[z], stat_all.at[z], stat_send.at[k - 1], stat_recv.at[k - 1], tensor=z ^ k
        )

    for k in (1, 2, 3):
        to_line(k).start()
    for k in (1, 2, 3):
        remote(
            stat_all.at[z ^ k], stat_all.at[z ^ k], stat_send.at[k - 1], stat_recv.at[k - 1], tensor=z ^ k
        ).wait_recv()
    summed = (stat_all[0] + stat_all[1]) + (stat_all[2] + stat_all[3])
    full_width = depth * 4
    pair_width = width * 4
    down_cols = decay_rate * small_factor[0:1, :] + share * (summed[0:1, :] / full_width)
    up_rows = decay_rate * small_factor[1:2, :] + share * (summed[1:2, :] / pair_width)
    small_out[0:1, :] = down_cols
    small_out[1:2, :] = up_rows
    ratio = down_cols / (summed[2:3, :] / full_width)
    index = lax.broadcasted_iota(jnp.int32, (128, span), 0)
    back = jnp.where(index == 0, ratio, up_rows).T
    down_scale = lax.rsqrt(back[:, 0:1])
    up_column = back[:, 1:2].reshape(owned, rank, 1)
    up_mean = jnp.sum(up_column, axis=1, keepdims=True) / rank
    up_scale = lax.rsqrt(up_column / up_mean).reshape(span, 1)

    def write(j):
        if j < pieces - 1:
            return local(total.at[j], down_out.at[:, pl.ds(j * piece, piece)], upd_sem.at[j])
        return local(total.at[j], up_out, upd_sem.at[j])

    for j in range(pieces):
        if j < pieces - 1:
            row_scale = lax.rsqrt(rows_out[:, j * piece : (j + 1) * piece])
            column_scale = down_scale
        else:
            row_scale = lax.rsqrt(columns_out[...])
            column_scale = up_scale
        row_scale = jnp.broadcast_to(row_scale[:, None, :], (owned, rank, piece)).reshape(span, piece)
        total[j] = total[j] * row_scale * column_scale
        write(j).start()

    loads[7].wait()

    def put(i):
        return local(stage.at[i % 2], grad_out.at[chunk(i)], out_sem.at[i % 2])

    for i in range(chunks):
        @pl.when(end)
        def _():
            arrive(3, i)

        if i >= 2:
            put(i - 2).wait()
        alive = place_col[chunk(i), :] >= 0

        def column(j, _):
            over = pl.ds(pl.multiple_of(j * cols, cols), cols)
            value = acc[chunk(i), over] + dot_nt(gv[3, chunk(i), :], wv[3, over, :])
            stage[i % 2, :, over] = jnp.where(alive, value, 0.0).astype(jnp.bfloat16)
            return 0

        lax.fori_loop(0, wide, column, 0)
        put(i).start()
    put(chunks - 2).wait()
    put(chunks - 1).wait()
    for j in range(pieces):
        write(j).wait()

    for i in range(chunks):
        to_pair(i).wait_send()

        @pl.when(middle)
        def _():
            to_cross(i).wait_send()
            relay_cross(i).wait_send()
            relay_end(i).wait_send()
            relay_last(i).wait_send()

    for m in range(2):
        own(m).wait_send()
        for q in range(quarter):
            over_x(q, m).wait_send()
            over_y(q, m).wait_send()
            over_core(q, m, mine, 0).wait_send()
            over_core(q, m, other, 1).wait_send()

    @pl.when(end)
    def _():
        send_far.wait_send()
        send_near.wait_send()

    @pl.when(middle)
    def _():
        send_cross.wait_send()
        near_end.wait_send()
        near_cross.wait_send()
        far_end.wait_send()

    for j in range(pieces):
        for k in range(2):
            to_core(k, j).wait_send()
        to_chip(j).wait_send()
    for k in (1, 2, 3):
        to_line(k).wait_send()


def fused(activations, output_gradient, place_of, weight, down_maps, up_maps, factors):
    row_factor, column_factor, small_factor = factors
    rows, depth = activations.shape
    width = output_gradient.shape[1]
    owned, _, rank = down_maps.shape
    span = owned * rank
    chunks, quarter = 6, 4
    piece = width
    pieces = depth // piece + 1
    half = rows // 2
    any_spec = pl.BlockSpec(memory_space=pl.ANY)
    vmem = pl.BlockSpec(memory_space=pltpu.VMEM)
    dma = pltpu.SemaphoreType.DMA
    scratch = [
        pltpu.VMEM((rows, depth), bf16),
        pltpu.VMEM((4, rows, width), bf16),
        pltpu.VMEM((4, depth, width), bf16),
        pltpu.VMEM((4, span, depth), bf16),
        pltpu.VMEM((4, span, width), bf16),
        pltpu.VMEM((rows, depth), f32),
        pltpu.VMEM((rows, 2 * rank), f32),
        pltpu.VMEM((half, 2 * rank), f32),
        pltpu.VMEM((half, 2 * rank), f32),
        pltpu.VMEM((half, 2 * rank), f32),
        pltpu.VMEM((half, 2 * rank), f32),
        pltpu.VMEM((rows, 2 * rank), bf16),
        pltpu.VMEM((2 * rank, rows), bf16),
        pltpu.VMEM((2, span, rows), bf16),
        pltpu.VMEM((rows // 4, 4 * span), bf16),
        pltpu.VMEM((2, pieces, span, piece), f32),
        pltpu.VMEM((2, pieces, span, piece), f32),
        pltpu.VMEM((pieces, span, piece), bf16),
        pltpu.VMEM((pieces, span, piece), bf16),
        pltpu.VMEM((pieces, span, piece), f32),
        pltpu.VMEM((2, rows // chunks, depth), bf16),
        pltpu.VMEM((4, 8, span), f32),
        dma((8,)),
        dma((5, chunks)),
        dma((3, chunks)),
        dma((2,)),
        dma((2,)),
        dma((quarter, 2)),
        dma((quarter, 2)),
        dma((quarter, 2)),
        dma((quarter, 2)),
        dma((2, quarter, 2)),
        dma((2, quarter, 2)),
        dma((6,)),
        dma((5,)),
        dma((2, pieces)),
        dma((2, pieces)),
        dma((pieces,)),
        dma((pieces,)),
        dma((3,)),
        dma((3,)),
        dma((2,)),
        dma((pieces,)),
    ]
    return pl.pallas_call(
        functools.partial(fused_kernel, rank),
        out_shape=(
            jax.ShapeDtypeStruct((rows, depth), bf16),
            jax.ShapeDtypeStruct((owned, depth), f32),
            jax.ShapeDtypeStruct((owned, width), f32),
            jax.ShapeDtypeStruct((2, span), f32),
            jax.ShapeDtypeStruct((span, depth), f32),
            jax.ShapeDtypeStruct((span, width), f32),
        ),
        in_specs=[any_spec] * 5 + [vmem] * 5,
        out_specs=(any_spec, vmem, vmem, vmem, any_spec, any_spec),
        scratch_shapes=scratch,
        compiler_params=pltpu.CompilerParams(
            collective_id=0, has_side_effects=True, vmem_limit_bytes=VMEM_LIMIT
        ),
        name="fused",
    )(
        activations,
        output_gradient,
        weight,
        down_maps.transpose(0, 2, 1).reshape(span, depth),
        up_maps.reshape(span, width),
        place_of[:, None],
        place_of[None, :],
        row_factor,
        column_factor,
        small_factor,
    )


def fits(activations, output_gradient, down_maps):
    rows, depth = activations.shape
    width = output_gradient.shape[1]
    owned, _, rank = down_maps.shape
    return (
        lax.axis_size("tensor") == 4
        and lax.axis_size("dp") == 4
        and lax.axis_size("rep") == 2
        and rank == 64
        and owned % 2 == 0
        and owned * rank // 8 % 16 == 0
        and rows % 768 == 0
        and width % 128 == 0
        and depth % width == 0
    )


def dot(a, b, ca, cb):
    return lax.dot_general(a, b, (((ca,), (cb,)), ((), ())), preferred_element_type=f32)


def chip_shift(value, groups, step):
    chips = groups // CORES
    pairs = [(d, (d // CORES + step) % chips * CORES + d % CORES) for d in range(groups)]
    return lax.ppermute(value, "dp", pairs)


def core_swap(value, groups):
    return lax.ppermute(value, "dp", [(d, d ^ 1) for d in range(groups)])


def ring_shift(value, size, step):
    return lax.ppermute(value, "tensor", [(t, (t + step) % size) for t in range(size)])


def total_small(value, size):
    if size > 8:
        return lax.psum(value, "tensor")
    me = lax.axis_index("tensor")
    parts = jnp.zeros((size,) + value.shape, value.dtype)
    parts = lax.dynamic_update_index_in_dim(parts, value, me, 0)
    for step in range(1, size):
        got = ring_shift(value, size, step)
        parts = lax.dynamic_update_index_in_dim(parts, got, (me - step) % size, 0)
    return jnp.sum(parts, axis=0)


def total_rows(value, size):
    if size > 8:
        return lax.psum(value, "tensor").astype(bf16)
    me = lax.axis_index("tensor")
    rows = value.shape[0] // size

    def piece(index):
        return lax.dynamic_slice_in_dim(value, index % size * rows, rows, 0)

    total = piece(me)
    for step in range(1, size):
        total = total + ring_shift(piece(me + step), size, step)
    mine = total.astype(bf16)
    out = jnp.zeros(value.shape, bf16)
    out = lax.dynamic_update_slice_in_dim(out, mine, me * rows, 0)
    for step in range(1, size):
        got = ring_shift(mine, size, step)
        out = lax.dynamic_update_slice_in_dim(out, got, (me - step) % size * rows, 0)
    return out


def shards(
    activations,
    output_gradient,
    row_tenant,
    group_row_count,
    tenant_storage_entry,
    key_value_weight,
    adapter_down_maps,
    adapter_up_maps,
    down_row_factor,
    down_column_factor,
    up_row_factor,
    up_column_factor,
):
    groups = lax.axis_size("dp")
    size = lax.axis_size("tensor")
    chips = groups // CORES
    owned, depth, rank = adapter_down_maps.shape
    width = adapter_up_maps.shape[2]
    entries = owned * groups
    count_rows = activations.shape[0]
    full_width = depth * size
    pair_width = key_value_weight.shape[1]
    here = lax.axis_index("dp")
    chip, core = here // CORES, here % CORES
    live = jnp.arange(count_rows, dtype=jnp.int32)[:, None] < group_row_count[0]
    tse = tenant_storage_entry
    owner = tse // owned
    place = (
        (chip - owner // CORES) % chips * CORES + (owner % CORES != core).astype(jnp.int32)
    ) * owned + tse % owned
    tenants = row_tenant[:, 0]
    place_of = jnp.sum(
        jnp.where(
            tenants[:, None] == jnp.arange(entries, dtype=jnp.int32)[None, :], place[None, :], 0
        ),
        axis=1,
    )
    if fits(activations, output_gradient, adapter_down_maps):
        span = owned * rank
        small = jnp.stack([down_column_factor.reshape(span), up_row_factor.reshape(span)])
        input_grad, down_rows, up_cols, small, down_update, up_update = fused(
            activations,
            output_gradient,
            jnp.where(live[:, 0], place_of, -1),
            key_value_weight,
            adapter_down_maps,
            adapter_up_maps,
            (down_row_factor, up_column_factor, small),
        )
        return (
            input_grad,
            down_rows,
            small[0].reshape(owned, rank),
            small[1].reshape(owned, rank),
            up_cols,
            down_update.reshape(owned, rank, depth).transpose(0, 2, 1),
            up_update.reshape(owned, rank, width),
        )
    gathered = lax.all_gather(output_gradient, "tensor", axis=1, tiled=True)
    own_maps = jnp.concatenate(
        [adapter_down_maps.transpose(0, 2, 1), adapter_up_maps], axis=2
    ).reshape(owned * rank, depth + width)
    blocks = []
    for s in range(chips):
        column = own_maps if s == 0 else chip_shift(own_maps, groups, s)
        blocks.append(jnp.concatenate([column, core_swap(column, groups)], axis=0))
    masked = jnp.where(live, output_gradient, jnp.zeros_like(output_gradient))
    span = CORES * owned * rank
    pair = 2 * rank
    lanes = jnp.arange(span, dtype=jnp.int32)[None, :] // rank

    def wide(s):
        return place_of[:, None] == lanes + s * CORES * owned

    def pick(s, product):
        kept = jnp.where(wide(s), product, 0.0)
        both = kept[:, :pair]
        for i in range(1, span // pair):
            both = both + kept[:, i * pair : (i + 1) * pair]
        return both

    picked_down = picked_up = 0.0
    for s in range(chips):
        picked_down += pick(s, dot(activations, blocks[s][:, :depth], 1, 1))
        picked_up += pick(s, dot(masked, blocks[s][:, depth:], 1, 1))
    partial = jnp.concatenate(
        [
            picked_down[:, :rank] + picked_down[:, rank:],
            picked_up[:, :rank] + picked_up[:, rank:],
        ],
        axis=1,
    )
    rounded = total_rows(partial, size)
    zero = jnp.zeros((), bf16)
    repeat_down = jnp.tile(rounded[:, :rank], (1, span // rank))
    repeat_up = jnp.tile(rounded[:, rank:], (1, span // rank))
    half = owned * rank
    spreads = [jnp.where(wide(s), repeat_up, zero) for s in range(chips)]
    pieces = []
    for s in list(range(1, chips)) + [0]:
        spread_down = jnp.where(wide(s), repeat_down, zero)
        terms = [
            adapter_scale
            * jnp.concatenate(
                [
                    dot(spreads[s][:, k : k + half], activations, 0, 0),
                    dot(spread_down[:, k : k + half], masked, 0, 0),
                ],
                axis=1,
            )
            for k in (half, 0)
        ]
        summed = terms[1] + core_swap(terms[0], groups)
        pieces.append(chip_shift(summed.astype(bf16), groups, -s) if s else summed)
    side = lax.optimization_barrier(
        (
            adapter_scale
            * dot(
                jnp.concatenate(spreads, axis=1),
                jnp.concatenate([b[:, :depth] for b in blocks], axis=0),
                1,
                0,
            )
        ).astype(bf16)
    )
    frozen = jnp.where(live, dot(gathered, key_value_weight, 1, 1), 0.0)
    input_grad = (frozen + side.astype(f32)).astype(bf16)
    pieces, input_grad = lax.optimization_barrier((pieces, input_grad))
    grads = sum(p.astype(f32) for p in pieces)
    grads = grads.reshape(owned, rank, depth + width)
    down_gradient, up_gradient = grads[:, :, :depth], grads[:, :, depth:]
    square_down = down_gradient * down_gradient + tiny_floor
    square_up = up_gradient * up_gradient + tiny_floor
    down_rows = decay_rate * down_row_factor + (1.0 - decay_rate) * jnp.mean(square_down, axis=1)
    up_cols = decay_rate * up_column_factor + (1.0 - decay_rate) * jnp.mean(square_up, axis=1)
    stats = jnp.concatenate(
        [
            jnp.sum(square_down, axis=2),
            jnp.sum(square_up, axis=2),
            jnp.broadcast_to(jnp.sum(down_rows, axis=1)[:, None], (owned, pair)),
        ],
        axis=1,
    )
    stats = total_small(stats, size)
    column_total, row_total = stats[:, :rank], stats[:, rank:pair]
    rows_sum = stats[:, pair]
    down_cols = decay_rate * down_column_factor + (1.0 - decay_rate) * (column_total / full_width)
    up_rows = decay_rate * up_row_factor + (1.0 - decay_rate) * (row_total / pair_width)
    second_down = (
        down_rows[:, None, :] * down_cols[:, :, None] / (rows_sum / full_width)[:, None, None]
    )
    second_up = up_rows[:, :, None] * up_cols[:, None, :] / jnp.mean(up_rows, axis=1)[:, None, None]
    down_update = (down_gradient * lax.rsqrt(second_down)).transpose(0, 2, 1)
    up_update = up_gradient * lax.rsqrt(second_up)
    return (input_grad, down_rows, down_cols, up_rows, up_cols, down_update, up_update)


def solution(mesh):
    in_specs = (
        P(("rep", "dp"), "tensor"),
        P(("rep", "dp"), "tensor"),
        P(("rep", "dp"), None),
        P(("rep", "dp")),
        P(),
        P("tensor", None),
        P("dp", "tensor", None),
        P("dp", None, "tensor"),
        P("dp", "tensor"),
        P("dp", None),
        P("dp", None),
        P("dp", "tensor"),
    )
    out_specs = (
        P(("rep", "dp"), "tensor"),
        P(("rep", "dp"), "tensor"),
        P(("rep", "dp"), None),
        P(("rep", "dp"), None),
        P(("rep", "dp"), "tensor"),
        P(("rep", "dp"), "tensor", None),
        P(("rep", "dp"), None, "tensor"),
    )
    return jax.shard_map(shards, mesh=mesh, in_specs=in_specs, out_specs=out_specs, check_vma=False)
```

```python
import functools

import jax
import jax.numpy as jnp
from jax import lax
from jax.experimental import pallas as pl
from jax.experimental.pallas import tpu as pltpu
from jax.sharding import PartitionSpec as P

adapter_scale = 0.25
decay_rate = 0.9
tiny_floor = 1e-30
f32 = jnp.float32
bf16 = jnp.bfloat16
CORES = 2
VMEM_LIMIT = 66_000_000
MESH = pl.DeviceIdType.MESH
EARLY = 3
BEFORE = 3
HEADS = 2


def dot_nt(a, b):
    return lax.dot_general(a, b, (((1,), (1,)), ((), ())), preferred_element_type=jnp.float32)


def dot_nn(a, b):
    return lax.dot_general(a, b, (((1,), (0,)), ((), ())), preferred_element_type=jnp.float32)


def fused_kernel(
    rank,
    x_hbm,
    g_hbm,
    w_hbm,
    down_hbm,
    up_hbm,
    tenants,
    live_count,
    entry_of,
    row_factor,
    column_factor,
    line_factor,
    upper_factor,
    grad_out,
    rows_out,
    columns_out,
    line_out,
    upper_out,
    down_out,
    up_out,
    place_col,
    place_row,
    xv,
    gv,
    wv,
    bd,
    bu,
    acc,
    part,
    far_in,
    near_in,
    cross_in,
    rounded,
    turned,
    spread,
    side_lhs,
    pair_out,
    pair_in,
    far_out,
    far_got,
    total,
    stage,
    stat_all,
    load_sem,
    ag_send,
    ag_recv,
    own_send,
    own_recv,
    x_send,
    x_recv,
    y_send,
    y_recv,
    c_send,
    c_recv,
    rs_send,
    rs_recv,
    pair_send,
    pair_recv,
    far_send,
    far_recv,
    stat_send,
    stat_recv,
    out_sem,
    upd_sem,
    credit,
):
    z = lax.axis_index("tensor")
    d = lax.axis_index("dp")
    rep = lax.axis_index("rep")
    middle = (z == 1) | (z == 2)
    end = (z == 0) | (z == 3)
    rows, depth = xv.shape
    width = gv.shape[2]
    span = bd.shape[1]
    owned = span // rank
    chunks = ag_recv.shape[1]
    size = rows // chunks
    half = rows // 2
    tile = rows // 4
    cols = 512 if depth % 512 == 0 else depth
    wide = depth // cols
    pieces = total.shape[0]
    piece = total.shape[2]
    quarter = x_recv.shape[0]
    step = span // 2 // quarter
    near_at = pl.multiple_of(z // 2 * half, half)
    far_at = pl.multiple_of((1 - z // 2) * half, half)

    def remote(src, dst, ss, rs, **where):
        return pltpu.make_async_remote_copy(
            src_ref=src, dst_ref=dst, send_sem=ss, recv_sem=rs, device_id=where, device_id_type=MESH
        )

    def local(src, dst, sem):
        return pltpu.make_async_copy(src, dst, sem)

    loads = [
        local(g_hbm, gv.at[0], load_sem.at[0]),
        local(down_hbm, bd.at[0], load_sem.at[1]),
        local(up_hbm, bu.at[0], load_sem.at[2]),
        local(x_hbm, xv, load_sem.at[3]),
    ]
    for k in range(4):
        at = pl.multiple_of((z ^ k) * width, width)
        loads.append(local(w_hbm.at[:, pl.ds(at, width)], wv.at[k], load_sem.at[4 + k]))
    for copy in loads:
        copy.start()

    barrier = pltpu.get_barrier_semaphore()
    peers = [
        {"tensor": z ^ 1},
        {"tensor": z ^ 2},
        {"tensor": z ^ 3},
        {"dp": d ^ 1},
        {"dp": d ^ 2},
        {"rep": rep ^ 1},
    ]
    for peer in peers:
        pl.semaphore_signal(barrier, inc=1, device_id=peer, device_id_type=MESH)
    pl.semaphore_wait(barrier, len(peers))

    def chunk(i):
        return pl.ds(i * size, size)

    def to_pair(i):
        return remote(
            g_hbm.at[chunk(i)], gv.at[1, chunk(i)], ag_send.at[0, i], ag_recv.at[0, i], tensor=z ^ 1
        )

    def to_cross(i):
        return remote(
            g_hbm.at[chunk(i)], gv.at[3, chunk(i)], ag_send.at[1, i], ag_recv.at[2, i], tensor=z ^ 3
        )

    def relay_cross(i):
        return remote(
            gv.at[1, chunk(i)], gv.at[2, chunk(i)], ag_send.at[2, i], ag_recv.at[1, i], tensor=z ^ 3
        )

    def relay_end(i):
        return remote(
            gv.at[3, chunk(i)], gv.at[2, chunk(i)], ag_send.at[3, i], ag_recv.at[1, i], tensor=z ^ 1
        )

    def relay_last(i):
        return remote(
            gv.at[2, chunk(i)], gv.at[3, chunk(i)], ag_send.at[4, i], ag_recv.at[2, i], tensor=z ^ 1
        )

    def arrive(slot, i):
        remote(
            gv.at[slot, chunk(i)], gv.at[slot, chunk(i)], ag_send.at[0, i], ag_recv.at[slot - 1, i], tensor=z ^ 1
        ).wait_recv()

    for i in range(chunks - 1):
        to_pair(i).start()

    @pl.when(middle)
    def _():
        to_pair(chunks - 1).start()
        for i in range(chunks):
            to_cross(i).start()

    maps = ((down_hbm, bd), (up_hbm, bu))

    def own(m):
        src, dst = maps[m]
        return remote(src, dst.at[1], own_send.at[m], own_recv.at[m], dp=d ^ 1)

    mine = rep * (span // 2)
    other = (1 - rep) * (span // 2)

    def part_rows(base, q):
        return pl.ds(pl.multiple_of(base + q * step, step), step)

    def over_x(q, m):
        src, dst = maps[m]
        at = part_rows(mine, q)
        return remote(src.at[at], dst.at[2, at], x_send.at[q, m], x_recv.at[q, m], dp=d ^ 2)

    def over_y(q, m):
        dst = maps[m][1]
        at = part_rows(mine, q)
        return remote(dst.at[2, at], dst.at[2, at], y_send.at[q, m], y_recv.at[q, m], rep=rep ^ 1)

    def over_core(q, m, base, k):
        dst = maps[m][1]
        at = part_rows(base, q)
        return remote(dst.at[2, at], dst.at[3, at], c_send.at[k, q, m], c_recv.at[k, q, m], dp=d ^ 1)

    for q in range(quarter):
        for m in range(2):
            over_x(q, m).start()
    for m in range(2):
        own(m).start()

    named = tenants[...]
    found = jnp.zeros((1, rows), jnp.int32)
    for t in range(entry_of.shape[0]):
        entry = entry_of[t]
        owner = lax.div(entry, owned)
        away = (owner // 2 != d // 2).astype(jnp.int32) * 2 + (owner % 2 != d % 2).astype(jnp.int32)
        found = jnp.where(named == t, away * owned + lax.rem(entry, owned), found)
    alive = lax.broadcasted_iota(jnp.int32, (1, rows), 1) < live_count[0]
    place_row[...] = jnp.where(alive, found, -1)

    def stand(i, _):
        at = pl.ds(pl.multiple_of(i * 128, 128), 128)
        lines = jnp.broadcast_to(place_row[:, at].astype(jnp.float32), (128, 128))
        place_col[at, :] = lines.T.astype(jnp.int32)
        return 0

    lax.fori_loop(0, rows // 128, stand, 0)

    def place_wide(at, lanes):
        return jnp.concatenate([place_col[at, :]] * (lanes // 128), axis=1)

    lane = lax.broadcasted_iota(jnp.int32, (tile, span), 1) // rank
    low = lax.broadcasted_iota(jnp.int32, (tile, 2 * rank), 1) < rank

    def project(b, base=0, count=rows // tile):
        def body(i, _):
            at = pl.ds(pl.multiple_of(base + i * tile, tile), tile)
            hit = place_wide(at, span) == lane + b * owned

            def fold(product):
                kept = jnp.where(hit, product, 0.0)
                both = kept[:, : 2 * rank]
                for j in range(1, span // (2 * rank)):
                    both = both + kept[:, j * 2 * rank : (j + 1) * 2 * rank]
                return both + pltpu.roll(both, rank, axis=1)

            new = jnp.where(
                low,
                fold(dot_nt(xv[at, :], bd[b])),
                fold(dot_nt(gv[0, at, :], bu[b])),
            )
            part[at, :] = new if b == 0 else part[at, :] + new
            return 0

        lax.fori_loop(0, count, body, 0)

    def frozen(k, first, start, count):
        def body(t, _):
            i, j = t // wide, t % wide
            at = pl.ds(pl.multiple_of(i * tile, tile), tile)
            over = pl.ds(pl.multiple_of(j * cols, cols), cols)
            new = dot_nt(gv[k, at, :], wv[k, over, :])
            acc[at, over] = new if first else acc[at, over] + new
            return 0

        lax.fori_loop(start * wide, (start + count) * wide, body, 0)

    for k in range(4):
        loads[k].wait()
    project(0)
    for m in range(2):
        own(m).wait_recv()
    loads[4].wait()
    for q in range(quarter):
        if q == quarter - 2:
            project(1)
        else:
            frozen(0, True, min(q, 2), 1)
        for m in range(2):
            over_x(q, m).wait_recv()
            over_y(q, m).start()
            over_core(q, m, mine, 0).start()
    for q in range(quarter):
        for m in range(2):
            dst = maps[m][1]
            at = part_rows(other, q)
            remote(dst.at[2, at], dst.at[2, at], y_send.at[q, m], y_recv.at[q, m], rep=rep ^ 1).wait_recv()
            over_core(q, m, other, 1).start()
        if q == 0:
            frozen(0, True, 3, 1)
    project(2)
    for k in range(2):
        for q in range(quarter):
            for m in range(2):
                at = part_rows(mine if k == 0 else other, q)
                dst = maps[m][1]
                remote(dst.at[2, at], dst.at[3, at], c_send.at[k, q, m], c_recv.at[k, q, m], dp=d ^ 1).wait_recv()
    project(3, far_at, rows // tile // 2)

    near = pl.ds(near_at, half)
    far = pl.ds(far_at, half)
    send_far = remote(part.at[far], far_in, rs_send.at[0], rs_recv.at[0], tensor=z ^ 1)
    send_near = remote(part.at[near], near_in, rs_send.at[1], rs_recv.at[1], tensor=z ^ 1)
    send_cross = remote(far_in, cross_in, rs_send.at[2], rs_recv.at[2], tensor=z ^ 3)
    near_end = remote(rounded.at[near], rounded.at[near], rs_send.at[3], rs_recv.at[3], tensor=z ^ 1)
    near_cross = remote(rounded.at[near], rounded.at[near], rs_send.at[4], rs_recv.at[4], tensor=z ^ 3)
    far_end = remote(rounded.at[far], rounded.at[far], rs_send.at[5], rs_recv.at[4], tensor=z ^ 1)

    def seen(t):
        return -(-t * tile // size)

    def outward(i):
        arrive(3, i)
        relay_end(i).start()

    def across(i):
        arrive(1, i)
        relay_cross(i).start()

    @pl.when(end)
    def _():
        send_far.start()

    project(3, near_at, rows // tile // 2)

    def gather(slot, tiles):
        for t in tiles:
            for i in range(seen(t), seen(t + 1)):
                arrive(slot, i)

    for k in (5, 6, 7):
        loads[k].wait()

    @pl.when(end)
    def _():
        send_near.start()
        to_pair(chunks - 1).start()
        gather(1, range(4))
        frozen(1, False, 0, 4)
        for t in range(HEADS):
            gather(2, (t,))
            frozen(2, False, t, 1)
        remote(rounded.at[near], rounded.at[near], rs_send.at[3], rs_recv.at[3], tensor=z ^ 1).wait_recv()
        remote(rounded.at[far], rounded.at[far], rs_send.at[4], rs_recv.at[4], tensor=z ^ 1).wait_recv()

    @pl.when(middle)
    def _():
        for i in range(EARLY):
            outward(i)
        across(0)
        send_far.wait_recv()
        far_in[...] = part[far, :] + far_in[...]
        send_cross.start()
        for i in range(1, seen(3)):
            arrive(1, i)
        frozen(1, False, 0, 3)
        send_near.wait_recv()
        send_cross.wait_recv()
        rounded[near, :] = ((part[near, :] + near_in[...]) + cross_in[...]).astype(jnp.bfloat16)
        near_cross.start()
        near_end.start()
        for i in range(seen(3), chunks):
            arrive(1, i)
        for i in range(1, chunks):
            relay_cross(i).start()
        remote(rounded.at[far], rounded.at[far], rs_send.at[4], rs_recv.at[4], tensor=z ^ 3).wait_recv()
        far_end.start()
        for i in range(EARLY, chunks):
            outward(i)

    def turn(i, _):
        at = pl.ds(pl.multiple_of(i * 128, 128), 128)
        turned[:, at] = rounded[at, :].astype(jnp.float32).T.astype(jnp.bfloat16)
        return 0

    lax.fori_loop(0, rows // 128, turn, 0)

    head = lax.broadcasted_iota(jnp.int32, (span, 128), 0) // rank

    def fill(b, put_in):
        def body(i, _):
            at = pl.ds(pl.multiple_of(i * 128, 128), 128)
            hit = place_row[:, at] == head + b * owned
            both = turned[:, at].astype(jnp.float32)
            for which, lines in ((0, both[rank:]), (1, both[:rank])):
                lines = jnp.concatenate([lines] * owned, axis=0)
                spread[put_in, which, :, at] = jnp.where(hit, lines, 0.0).astype(jnp.bfloat16)
            return 0

        lax.fori_loop(0, rows // 128, body, 0)

    def product(j, taken):
        if j < pieces - 1:
            return 0.25 * dot_nn(spread[taken, 0], xv[:, j * piece : (j + 1) * piece])
        return 0.25 * dot_nn(spread[taken, 1], gv[0])

    def to_core(k, j):
        return remote(
            pair_out.at[j], pair_in.at[j], pair_send.at[k, j], pair_recv.at[k, j], dp=d ^ 1
        )

    def to_chip(j):
        return remote(far_out.at[j], far_got.at[j], far_send.at[j], far_recv.at[j], dp=d ^ 2)

    def last(i):
        @pl.when(middle)
        def _():
            arrive(2, i)
            relay_last(i).start()

    def last(i):
        @pl.when(middle)
        def _():
            arrive(2, i)
            relay_last(i).start()

    def exchange(k, use):
        def offer(j):
            if k == 1:
                to_core(0, j).wait_send()
            pair_out[j] = product(j, 0)
            to_core(k, j).start()

        offer(0)
        for j in range(pieces):
            if j + 1 < pieces:
                offer(j + 1)
            ours = product(j, 1)
            to_core(k, j).wait_recv()
            use(j, ours + pair_in[j])

    def send_chip(j, value):
        far_out[j] = value.astype(jnp.bfloat16)
        to_chip(j).start()

    def keep(j, value):
        total[j] = value

    fill(3, 0)
    fill(2, 1)
    with jax.named_scope("EX0"):
        exchange(0, send_chip)
    pl.semaphore_signal(credit, inc=1, device_id={"dp": d ^ 1}, device_id_type=MESH)
    for i in range(chunks // 3):
        last(i)
    fill(1, 0)
    fill(0, 1)
    pl.semaphore_wait(credit, 1)
    with jax.named_scope("EX1"):
        exchange(1, keep)
    for i in range(chunks // 3, chunks - 2):
        last(i)

    @pl.when(end)
    def _():
        for t in range(HEADS, 4):
            gather(2, (t,))
            frozen(2, False, t, 1)

    @pl.when(middle)
    def _():
        frozen(1, False, 3, 1)

    lane_side = lax.broadcasted_iota(jnp.int32, (tile, 2 * rank), 1) // rank

    def add_side(i, _):
        at = pl.ds(pl.multiple_of(i * tile, tile), tile)
        both = rounded[at, :].astype(jnp.float32)
        both = jnp.where(low, pltpu.roll(both, rank, axis=1), both)
        owner = place_col[at, :]
        for t in range(side_lhs.shape[1] // (2 * rank)):
            side_lhs[:, t * 2 * rank : (t + 1) * 2 * rank] = jnp.where(
                owner == lane_side + 2 * t, both, 0.0
            ).astype(jnp.bfloat16)

        def column(j, _):
            over = pl.ds(pl.multiple_of(j * cols, cols), cols)
            right = bd[:, :, over].reshape(4 * span, cols)
            acc[at, over] = acc[at, over] + 0.25 * dot_nn(side_lhs[...], right)
            return 0

        lax.fori_loop(0, wide, column, 0)
        return 0

    lax.fori_loop(0, rows // tile, add_side, 0)
    last(chunks - 2)

    @pl.when(middle)
    def _():
        arrive(2, chunks - 1)
        frozen(2, False, 0, 4)


    def put(i):
        return local(stage.at[i % 2], grad_out.at[chunk(i)], out_sem.at[i % 2])

    def finish(i):
        @pl.when(end)
        def _():
            arrive(3, i)

        if i >= 2:
            put(i - 2).wait()
        alive = place_wide(chunk(i), cols) >= 0

        def column(j, _):
            over = pl.ds(pl.multiple_of(j * cols, cols), cols)
            value = acc[chunk(i), over] + dot_nt(gv[3, chunk(i), :], wv[3, over, :])
            stage[i % 2, :, over] = jnp.where(alive, value, 0.0).astype(jnp.bfloat16)
            return 0

        lax.fori_loop(0, wide, column, 0)
        put(i).start()

    for i in range(BEFORE):
        finish(i)

    share = 1.0 - decay_rate
    line = jnp.zeros((span, 1), jnp.float32)
    upper = jnp.zeros((span, 1), jnp.float32)
    rows_sum = jnp.zeros((owned, 1), jnp.float32)
    for j in range(pieces):
        to_chip(j).wait_recv()
        value = total[j] + far_got[j].astype(jnp.float32)
        total[j] = value
        square = value * value + tiny_floor
        mean = jnp.sum(square.reshape(owned, rank, piece), axis=1) / rank
        if j < pieces - 1:
            over = slice(j * piece, (j + 1) * piece)
            fresh = decay_rate * row_factor[:, over] + share * mean
            rows_out[:, over] = fresh
            rows_sum = rows_sum + jnp.sum(fresh, axis=1, keepdims=True)
            line = line + jnp.sum(square, axis=1, keepdims=True)
        else:
            columns_out[...] = decay_rate * column_factor[...] + share * mean
            upper = jnp.sum(square, axis=1, keepdims=True)
    place = lax.broadcasted_iota(jnp.int32, (span, 128), 1)
    spread_sum = jnp.broadcast_to(rows_sum[:, None, :], (owned, rank, 1)).reshape(span, 1)
    packed = jnp.where(place == 0, line, jnp.where(place == 1, upper, spread_sum))
    stat_all[z] = packed.T[:8, :]

    def to_line(k):
        return remote(
            stat_all.at[z], stat_all.at[z], stat_send.at[k - 1], stat_recv.at[k - 1], tensor=z ^ k
        )

    for k in (1, 2, 3):
        to_line(k).start()

    @pl.when(middle)
    def _():
        relay_last(chunks - 1).start()

    for i in range(BEFORE, chunks - 2):
        finish(i)
    for k in (1, 2, 3):
        remote(
            stat_all.at[z ^ k], stat_all.at[z ^ k], stat_send.at[k - 1], stat_recv.at[k - 1], tensor=z ^ k
        ).wait_recv()
    summed = (stat_all[0] + stat_all[1]) + (stat_all[2] + stat_all[3])
    full_width = depth * 4
    pair_width = width * 4

    def in_line(ref):
        return jnp.concatenate([ref[e : e + 1, :] for e in range(owned)], axis=1)

    down_cols = decay_rate * in_line(line_factor) + share * (summed[0:1, :] / full_width)
    up_rows = decay_rate * in_line(upper_factor) + share * (summed[1:2, :] / pair_width)
    for e in range(owned):
        line_out[e : e + 1, :] = down_cols[:, e * rank : (e + 1) * rank]
        upper_out[e : e + 1, :] = up_rows[:, e * rank : (e + 1) * rank]
    ratio = down_cols / (summed[2:3, :] / full_width)
    index = lax.broadcasted_iota(jnp.int32, (128, span), 0)
    back = jnp.where(index == 0, ratio, up_rows).T
    down_scale = lax.rsqrt(back[:, 0:1])
    up_column = back[:, 1:2].reshape(owned, rank, 1)
    up_mean = jnp.sum(up_column, axis=1, keepdims=True) / rank
    up_scale = lax.rsqrt(up_column / up_mean).reshape(span, 1)

    def write(j):
        if j < pieces - 1:
            return local(total.at[j], down_out.at[:, pl.ds(j * piece, piece)], upd_sem.at[j])
        return local(total.at[j], up_out, upd_sem.at[j])

    for j in range(pieces):
        if j < pieces - 1:
            row_scale = lax.rsqrt(rows_out[:, j * piece : (j + 1) * piece])
            column_scale = down_scale
        else:
            row_scale = lax.rsqrt(columns_out[...])
            column_scale = up_scale
        row_scale = jnp.broadcast_to(row_scale[:, None, :], (owned, rank, piece)).reshape(span, piece)
        total[j] = total[j] * row_scale * column_scale
        write(j).start()

    for i in range(chunks - 2, chunks):
        finish(i)
    put(chunks - 2).wait()
    put(chunks - 1).wait()
    for j in range(pieces):
        write(j).wait()

    for i in range(chunks):
        to_pair(i).wait_send()

        @pl.when(middle)
        def _():
            to_cross(i).wait_send()
            relay_cross(i).wait_send()
            relay_end(i).wait_send()
            relay_last(i).wait_send()

    for m in range(2):
        own(m).wait_send()
        for q in range(quarter):
            over_x(q, m).wait_send()
            over_y(q, m).wait_send()
            over_core(q, m, mine, 0).wait_send()
            over_core(q, m, other, 1).wait_send()

    @pl.when(end)
    def _():
        send_far.wait_send()
        send_near.wait_send()

    @pl.when(middle)
    def _():
        send_cross.wait_send()
        near_end.wait_send()
        near_cross.wait_send()
        far_end.wait_send()

    for j in range(pieces):
        to_core(1, j).wait_send()
        to_chip(j).wait_send()
    for k in (1, 2, 3):
        to_line(k).wait_send()


def hand_over_kernel(count, steps, *refs):
    sources, targets, buffers = refs[:count], refs[count : 2 * count], refs[2 * count : 3 * count]
    in_sem, out_sem = refs[3 * count :]
    moves = []
    for k in range(count):
        rows = sources[k].shape[0] // steps[k]
        for i in range(steps[k]):
            at = pl.ds(i * rows, rows)
            n = len(moves)
            moves.append(
                (
                    pltpu.make_async_copy(sources[k].at[at], buffers[k].at[at], in_sem.at[n]),
                    pltpu.make_async_copy(buffers[k].at[at], targets[k].at[at], out_sem.at[n]),
                )
            )
    for inward, _ in moves:
        inward.start()
    for inward, outward in moves:
        inward.wait()
        outward.start()
    for _, outward in moves:
        outward.wait()


def hand_over(arrays):
    count = len(arrays)
    steps = [8 if a.shape[0] % 128 == 0 else 1 for a in arrays]
    any_spec = pl.BlockSpec(memory_space=pl.ANY)
    return pl.pallas_call(
        functools.partial(hand_over_kernel, count, steps),
        out_shape=tuple(jax.ShapeDtypeStruct(a.shape, a.dtype) for a in arrays),
        in_specs=[any_spec] * count,
        out_specs=(any_spec,) * count,
        scratch_shapes=[pltpu.VMEM(a.shape, a.dtype) for a in arrays]
        + [pltpu.SemaphoreType.DMA((sum(steps),)), pltpu.SemaphoreType.DMA((sum(steps),))],
        name="hand_over",
    )(*arrays)


def fused(activations, output_gradient, tenants, live_count, entry_of, weight, down_maps, up_maps, factors):
    rows, depth = activations.shape
    width = output_gradient.shape[1]
    owned, _, rank = down_maps.shape
    span = owned * rank
    chunks, quarter = 6, 4
    piece = width
    pieces = depth // piece + 1
    half = rows // 2
    any_spec = pl.BlockSpec(memory_space=pl.ANY)
    vmem = pl.BlockSpec(memory_space=pltpu.VMEM)
    dma = pltpu.SemaphoreType.DMA
    smem = pl.BlockSpec(memory_space=pltpu.SMEM)
    scratch = [
        pltpu.VMEM((rows, 128), jnp.int32),
        pltpu.VMEM((1, rows), jnp.int32),
        pltpu.VMEM((rows, depth), bf16),
        pltpu.VMEM((4, rows, width), bf16),
        pltpu.VMEM((4, depth, width), bf16),
        pltpu.VMEM((4, span, depth), bf16),
        pltpu.VMEM((4, span, width), bf16),
        pltpu.VMEM((rows, depth), f32),
        pltpu.VMEM((rows, 2 * rank), f32),
        pltpu.VMEM((half, 2 * rank), f32),
        pltpu.VMEM((half, 2 * rank), f32),
        pltpu.VMEM((half, 2 * rank), f32),
        pltpu.VMEM((rows, 2 * rank), bf16),
        pltpu.VMEM((2 * rank, rows), bf16),
        pltpu.VMEM((2, 2, span, rows), bf16),
        pltpu.VMEM((rows // 4, 4 * span), bf16),
        pltpu.VMEM((pieces, span, piece), f32),
        pltpu.VMEM((pieces, span, piece), f32),
        pltpu.VMEM((pieces, span, piece), bf16),
        pltpu.VMEM((pieces, span, piece), bf16),
        pltpu.VMEM((pieces, span, piece), f32),
        pltpu.VMEM((2, rows // chunks, depth), bf16),
        pltpu.VMEM((4, 8, span), f32),
        dma((8,)),
        dma((5, chunks)),
        dma((3, chunks)),
        dma((2,)),
        dma((2,)),
        dma((quarter, 2)),
        dma((quarter, 2)),
        dma((quarter, 2)),
        dma((quarter, 2)),
        dma((2, quarter, 2)),
        dma((2, quarter, 2)),
        dma((6,)),
        dma((5,)),
        dma((2, pieces)),
        dma((2, pieces)),
        dma((pieces,)),
        dma((pieces,)),
        dma((3,)),
        dma((3,)),
        dma((2,)),
        dma((pieces,)),
        pltpu.SemaphoreType.REGULAR,
    ]
    results = pl.pallas_call(
        functools.partial(fused_kernel, rank),
        out_shape=(
            jax.ShapeDtypeStruct((rows, depth), bf16),
            jax.ShapeDtypeStruct((owned, depth), f32),
            jax.ShapeDtypeStruct((owned, width), f32),
            jax.ShapeDtypeStruct((owned, rank), f32),
            jax.ShapeDtypeStruct((owned, rank), f32),
            jax.ShapeDtypeStruct((span, depth), f32),
            jax.ShapeDtypeStruct((span, width), f32),
        ),
        in_specs=[any_spec] * 5 + [vmem, smem, smem] + [vmem] * 4,
        out_specs=(any_spec, vmem, vmem, vmem, vmem, any_spec, any_spec),
        scratch_shapes=scratch,
        compiler_params=pltpu.CompilerParams(
            collective_id=0, has_side_effects=True, vmem_limit_bytes=VMEM_LIMIT
        ),
        name="fused",
    )(
        activations,
        output_gradient,
        weight,
        down_maps.transpose(0, 2, 1).reshape(span, depth),
        up_maps.reshape(span, width),
        tenants,
        live_count,
        entry_of,
        *factors,
    )
    return hand_over(results)


def fits(activations, output_gradient, down_maps):
    rows, depth = activations.shape
    width = output_gradient.shape[1]
    owned, _, rank = down_maps.shape
    return (
        lax.axis_size("tensor") == 4
        and lax.axis_size("dp") == 4
        and lax.axis_size("rep") == 2
        and rank == 64
        and owned % 2 == 0
        and owned * rank // 8 % 16 == 0
        and rows % 768 == 0
        and width % 128 == 0
        and depth % width == 0
    )


def dot(a, b, ca, cb):
    return lax.dot_general(a, b, (((ca,), (cb,)), ((), ())), preferred_element_type=f32)


def chip_shift(value, groups, step):
    chips = groups // CORES
    pairs = [(d, (d // CORES + step) % chips * CORES + d % CORES) for d in range(groups)]
    return lax.ppermute(value, "dp", pairs)


def core_swap(value, groups):
    return lax.ppermute(value, "dp", [(d, d ^ 1) for d in range(groups)])


def ring_shift(value, size, step):
    return lax.ppermute(value, "tensor", [(t, (t + step) % size) for t in range(size)])


def total_small(value, size):
    if size > 8:
        return lax.psum(value, "tensor")
    me = lax.axis_index("tensor")
    parts = jnp.zeros((size,) + value.shape, value.dtype)
    parts = lax.dynamic_update_index_in_dim(parts, value, me, 0)
    for step in range(1, size):
        got = ring_shift(value, size, step)
        parts = lax.dynamic_update_index_in_dim(parts, got, (me - step) % size, 0)
    return jnp.sum(parts, axis=0)


def total_rows(value, size):
    if size > 8:
        return lax.psum(value, "tensor").astype(bf16)
    me = lax.axis_index("tensor")
    rows = value.shape[0] // size

    def piece(index):
        return lax.dynamic_slice_in_dim(value, index % size * rows, rows, 0)

    total = piece(me)
    for step in range(1, size):
        total = total + ring_shift(piece(me + step), size, step)
    mine = total.astype(bf16)
    out = jnp.zeros(value.shape, bf16)
    out = lax.dynamic_update_slice_in_dim(out, mine, me * rows, 0)
    for step in range(1, size):
        got = ring_shift(mine, size, step)
        out = lax.dynamic_update_slice_in_dim(out, got, (me - step) % size * rows, 0)
    return out


def shards(
    activations,
    output_gradient,
    row_tenant,
    group_row_count,
    tenant_storage_entry,
    key_value_weight,
    adapter_down_maps,
    adapter_up_maps,
    down_row_factor,
    down_column_factor,
    up_row_factor,
    up_column_factor,
):
    groups = lax.axis_size("dp")
    size = lax.axis_size("tensor")
    chips = groups // CORES
    owned, depth, rank = adapter_down_maps.shape
    width = adapter_up_maps.shape[2]
    entries = owned * groups
    count_rows = activations.shape[0]
    full_width = depth * size
    pair_width = key_value_weight.shape[1]
    here = lax.axis_index("dp")
    chip, core = here // CORES, here % CORES
    if fits(activations, output_gradient, adapter_down_maps):
        input_grad, down_rows, up_cols, down_cols, up_rows, down_update, up_update = fused(
            activations,
            output_gradient,
            row_tenant.reshape(1, count_rows),
            group_row_count,
            tenant_storage_entry,
            key_value_weight,
            adapter_down_maps,
            adapter_up_maps,
            (down_row_factor, up_column_factor, down_column_factor, up_row_factor),
        )
        return (
            input_grad,
            down_rows,
            down_cols,
            up_rows,
            up_cols,
            down_update.reshape(owned, rank, depth).transpose(0, 2, 1),
            up_update.reshape(owned, rank, width),
        )
    gathered = lax.all_gather(output_gradient, "tensor", axis=1, tiled=True)
    own_maps = jnp.concatenate(
        [adapter_down_maps.transpose(0, 2, 1), adapter_up_maps], axis=2
    ).reshape(owned * rank, depth + width)
    blocks = []
    for s in range(chips):
        column = own_maps if s == 0 else chip_shift(own_maps, groups, s)
        blocks.append(jnp.concatenate([column, core_swap(column, groups)], axis=0))
    live = jnp.arange(count_rows, dtype=jnp.int32)[:, None] < group_row_count[0]
    masked = jnp.where(live, output_gradient, jnp.zeros_like(output_gradient))
    tse = tenant_storage_entry
    owner = tse // owned
    place = (
        (chip - owner // CORES) % chips * CORES + (owner % CORES != core).astype(jnp.int32)
    ) * owned + tse % owned
    tenants = row_tenant[:, 0]
    place_of = jnp.sum(
        jnp.where(
            tenants[:, None] == jnp.arange(entries, dtype=jnp.int32)[None, :], place[None, :], 0
        ),
        axis=1,
    )
    span = CORES * owned * rank
    pair = 2 * rank
    lanes = jnp.arange(span, dtype=jnp.int32)[None, :] // rank

    def wide(s):
        return place_of[:, None] == lanes + s * CORES * owned

    def pick(s, product):
        kept = jnp.where(wide(s), product, 0.0)
        both = kept[:, :pair]
        for i in range(1, span // pair):
            both = both + kept[:, i * pair : (i + 1) * pair]
        return both

    picked_down = picked_up = 0.0
    for s in range(chips):
        picked_down += pick(s, dot(activations, blocks[s][:, :depth], 1, 1))
        picked_up += pick(s, dot(masked, blocks[s][:, depth:], 1, 1))
    partial = jnp.concatenate(
        [
            picked_down[:, :rank] + picked_down[:, rank:],
            picked_up[:, :rank] + picked_up[:, rank:],
        ],
        axis=1,
    )
    rounded = total_rows(partial, size)
    zero = jnp.zeros((), bf16)
    repeat_down = jnp.tile(rounded[:, :rank], (1, span // rank))
    repeat_up = jnp.tile(rounded[:, rank:], (1, span // rank))
    half = owned * rank
    spreads = [jnp.where(wide(s), repeat_up, zero) for s in range(chips)]
    pieces = []
    for s in list(range(1, chips)) + [0]:
        spread_down = jnp.where(wide(s), repeat_down, zero)
        terms = [
            adapter_scale
            * jnp.concatenate(
                [
                    dot(spreads[s][:, k : k + half], activations, 0, 0),
                    dot(spread_down[:, k : k + half], masked, 0, 0),
                ],
                axis=1,
            )
            for k in (half, 0)
        ]
        summed = terms[1] + core_swap(terms[0], groups)
        pieces.append(chip_shift(summed.astype(bf16), groups, -s) if s else summed)
    side = lax.optimization_barrier(
        (
            adapter_scale
            * dot(
                jnp.concatenate(spreads, axis=1),
                jnp.concatenate([b[:, :depth] for b in blocks], axis=0),
                1,
                0,
            )
        ).astype(bf16)
    )
    frozen = jnp.where(live, dot(gathered, key_value_weight, 1, 1), 0.0)
    input_grad = (frozen + side.astype(f32)).astype(bf16)
    pieces, input_grad = lax.optimization_barrier((pieces, input_grad))
    grads = sum(p.astype(f32) for p in pieces)
    grads = grads.reshape(owned, rank, depth + width)
    down_gradient, up_gradient = grads[:, :, :depth], grads[:, :, depth:]
    square_down = down_gradient * down_gradient + tiny_floor
    square_up = up_gradient * up_gradient + tiny_floor
    down_rows = decay_rate * down_row_factor + (1.0 - decay_rate) * jnp.mean(square_down, axis=1)
    up_cols = decay_rate * up_column_factor + (1.0 - decay_rate) * jnp.mean(square_up, axis=1)
    stats = jnp.concatenate(
        [
            jnp.sum(square_down, axis=2),
            jnp.sum(square_up, axis=2),
            jnp.broadcast_to(jnp.sum(down_rows, axis=1)[:, None], (owned, pair)),
        ],
        axis=1,
    )
    stats = total_small(stats, size)
    column_total, row_total = stats[:, :rank], stats[:, rank:pair]
    rows_sum = stats[:, pair]
    down_cols = decay_rate * down_column_factor + (1.0 - decay_rate) * (column_total / full_width)
    up_rows = decay_rate * up_row_factor + (1.0 - decay_rate) * (row_total / pair_width)
    second_down = (
        down_rows[:, None, :] * down_cols[:, :, None] / (rows_sum / full_width)[:, None, None]
    )
    second_up = up_rows[:, :, None] * up_cols[:, None, :] / jnp.mean(up_rows, axis=1)[:, None, None]
    down_update = (down_gradient * lax.rsqrt(second_down)).transpose(0, 2, 1)
    up_update = up_gradient * lax.rsqrt(second_up)
    return (input_grad, down_rows, down_cols, up_rows, up_cols, down_update, up_update)


def solution(mesh):
    in_specs = (
        P(("rep", "dp"), "tensor"),
        P(("rep", "dp"), "tensor"),
        P(("rep", "dp"), None),
        P(("rep", "dp")),
        P(),
        P("tensor", None),
        P("dp", "tensor", None),
        P("dp", None, "tensor"),
        P("dp", "tensor"),
        P("dp", None),
        P("dp", None),
        P("dp", "tensor"),
    )
    out_specs = (
        P(("rep", "dp"), "tensor"),
        P(("rep", "dp"), "tensor"),
        P(("rep", "dp"), None),
        P(("rep", "dp"), None),
        P(("rep", "dp"), "tensor"),
        P(("rep", "dp"), "tensor", None),
        P(("rep", "dp"), None, "tensor"),
    )
    return jax.shard_map(shards, mesh=mesh, in_specs=in_specs, out_specs=out_specs, check_vma=False)
```

```python
import functools

import jax
import jax.numpy as jnp
from jax import lax
from jax.experimental import pallas as pl
from jax.experimental.pallas import tpu as pltpu
from jax.sharding import PartitionSpec as P

HAND_LIMIT = 4_000_000
adapter_scale = 0.25
decay_rate = 0.9
tiny_floor = 1e-30
f32 = jnp.float32
bf16 = jnp.bfloat16
CORES = 2
VMEM_LIMIT = 57_000_000
MESH = pl.DeviceIdType.MESH
EARLY = 3
BEFORE = 3
PARTS = 1
HEADS = 2


def dot_nt(a, b):
    return lax.dot_general(a, b, (((1,), (1,)), ((), ())), preferred_element_type=jnp.float32)


def dot_nn(a, b):
    return lax.dot_general(a, b, (((1,), (0,)), ((), ())), preferred_element_type=jnp.float32)


def fused_kernel(
    rank,
    x_hbm,
    g_hbm,
    w_hbm,
    down_hbm,
    up_hbm,
    tenants,
    live_count,
    entry_of,
    row_factor,
    column_factor,
    line_factor,
    upper_factor,
    xv,
    new_rows,
    new_columns,
    new_line,
    new_upper,
    total_down,
    total_up,
    place_col,
    place_row,
    gv,
    wv,
    bd,
    bu,
    acc,
    part,
    far_in,
    near_in,
    cross_in,
    rounded,
    turned,
    spread,
    side_lhs,
    pair_out,
    pair_in,
    far_out,
    far_got,
    stat_all,
    load_sem,
    ag_send,
    ag_recv,
    own_send,
    own_recv,
    x_send,
    x_recv,
    y_send,
    y_recv,
    c_send,
    c_recv,
    rs_send,
    rs_recv,
    pair_send,
    pair_recv,
    far_send,
    far_recv,
    stat_send,
    stat_recv,
    credit,
):
    z = lax.axis_index("tensor")
    d = lax.axis_index("dp")
    rep = lax.axis_index("rep")
    middle = (z == 1) | (z == 2)
    end = (z == 0) | (z == 3)
    rows, depth = xv.shape
    width = gv.shape[2]
    span = bd.shape[1]
    owned = span // rank
    chunks = ag_recv.shape[1]
    size = rows // chunks
    part_size = size // PARTS
    half = rows // 2
    tile = rows // 4
    cols = 512 if depth % 512 == 0 else depth
    wide = depth // cols
    piece = width
    pieces = depth // piece + 1
    quarter = x_recv.shape[0]
    step = span // 2 // quarter
    near_at = pl.multiple_of(z // 2 * half, half)
    far_at = pl.multiple_of((1 - z // 2) * half, half)

    def total_part(j):
        if j < pieces - 1:
            return total_down.at[:, j * piece : (j + 1) * piece]
        return total_up

    def remote(src, dst, ss, rs, **where):
        return pltpu.make_async_remote_copy(
            src_ref=src, dst_ref=dst, send_sem=ss, recv_sem=rs, device_id=where, device_id_type=MESH
        )

    def local(src, dst, sem):
        return pltpu.make_async_copy(src, dst, sem)

    loads = [
        local(g_hbm, gv.at[0], load_sem.at[0]),
        local(down_hbm, bd.at[0], load_sem.at[1]),
        local(up_hbm, bu.at[0], load_sem.at[2]),
        local(x_hbm, xv, load_sem.at[3]),
    ]
    for k in range(4):
        at = pl.multiple_of((z ^ k) * width, width)
        loads.append(local(w_hbm.at[:, pl.ds(at, width)], wv.at[k], load_sem.at[4 + k]))
    for copy in loads:
        copy.start()

    barrier = pltpu.get_barrier_semaphore()
    peers = [
        {"tensor": z ^ 1},
        {"tensor": z ^ 2},
        {"tensor": z ^ 3},
        {"dp": d ^ 1},
        {"dp": d ^ 2},
        {"rep": rep ^ 1},
    ]
    for peer in peers:
        pl.semaphore_signal(barrier, inc=1, device_id=peer, device_id_type=MESH)
    pl.semaphore_wait(barrier, len(peers))

    def chunk(i):
        return pl.ds(i * size, size)

    def to_pair(i):
        return remote(
            g_hbm.at[chunk(i)], gv.at[1, chunk(i)], ag_send.at[0, i], ag_recv.at[0, i], tensor=z ^ 1
        )

    def to_cross(i):
        return remote(
            g_hbm.at[chunk(i)], gv.at[3, chunk(i)], ag_send.at[1, i], ag_recv.at[2, i], tensor=z ^ 3
        )

    def relay_cross(i):
        return remote(
            gv.at[1, chunk(i)], gv.at[2, chunk(i)], ag_send.at[2, i], ag_recv.at[1, i], tensor=z ^ 3
        )

    def relay_end(i):
        return remote(
            gv.at[3, chunk(i)], gv.at[2, chunk(i)], ag_send.at[3, i], ag_recv.at[1, i], tensor=z ^ 1
        )

    def relay_last(i):
        return remote(
            gv.at[2, chunk(i)], gv.at[3, chunk(i)], ag_send.at[4, i], ag_recv.at[2, i], tensor=z ^ 1
        )

    def arrive(slot, i):
        remote(
            gv.at[slot, chunk(i)], gv.at[slot, chunk(i)], ag_send.at[0, i], ag_recv.at[slot - 1, i], tensor=z ^ 1
        ).wait_recv()

    for i in range(chunks - 1):
        to_pair(i).start()

    @pl.when(middle)
    def _():
        to_pair(chunks - 1).start()
        for i in range(chunks):
            to_cross(i).start()

    maps = ((down_hbm, bd), (up_hbm, bu))

    def own(m):
        src, dst = maps[m]
        return remote(src, dst.at[1], own_send.at[m], own_recv.at[m], dp=d ^ 1)

    mine = rep * (span // 2)
    other = (1 - rep) * (span // 2)

    def part_rows(base, q):
        return pl.ds(pl.multiple_of(base + q * step, step), step)

    def over_x(q, m):
        src, dst = maps[m]
        at = part_rows(mine, q)
        return remote(src.at[at], dst.at[2, at], x_send.at[q, m], x_recv.at[q, m], dp=d ^ 2)

    def over_y(q, m):
        dst = maps[m][1]
        at = part_rows(mine, q)
        return remote(dst.at[2, at], dst.at[2, at], y_send.at[q, m], y_recv.at[q, m], rep=rep ^ 1)

    def over_core(q, m, base, k):
        dst = maps[m][1]
        at = part_rows(base, q)
        return remote(dst.at[2, at], dst.at[3, at], c_send.at[k, q, m], c_recv.at[k, q, m], dp=d ^ 1)

    for q in range(quarter):
        for m in range(2):
            over_x(q, m).start()
    for m in range(2):
        own(m).start()

    named = tenants[...]
    found = jnp.zeros((1, rows), jnp.int32)
    for t in range(entry_of.shape[0]):
        entry = entry_of[t]
        owner = lax.div(entry, owned)
        away = (owner // 2 != d // 2).astype(jnp.int32) * 2 + (owner % 2 != d % 2).astype(jnp.int32)
        found = jnp.where(named == t, away * owned + lax.rem(entry, owned), found)
    alive = lax.broadcasted_iota(jnp.int32, (1, rows), 1) < live_count[0]
    place_row[...] = jnp.where(alive, found, -1)

    def stand(i, _):
        at = pl.ds(pl.multiple_of(i * 128, 128), 128)
        lines = jnp.broadcast_to(place_row[:, at].astype(jnp.float32), (128, 128))
        place_col[at, :] = lines.T.astype(jnp.int32)
        return 0

    lax.fori_loop(0, rows // 128, stand, 0)

    def place_wide(at, lanes):
        return jnp.concatenate([place_col[at, :]] * (lanes // 128), axis=1)

    lane = lax.broadcasted_iota(jnp.int32, (tile, span), 1) // rank
    low = lax.broadcasted_iota(jnp.int32, (tile, 2 * rank), 1) < rank

    def project(b, base=0, count=rows // tile):
        def body(i, _):
            at = pl.ds(pl.multiple_of(base + i * tile, tile), tile)
            hit = place_wide(at, span) == lane + b * owned

            def fold(product):
                kept = jnp.where(hit, product, 0.0)
                both = kept[:, : 2 * rank]
                for j in range(1, span // (2 * rank)):
                    both = both + kept[:, j * 2 * rank : (j + 1) * 2 * rank]
                return both + pltpu.roll(both, rank, axis=1)

            new = jnp.where(
                low,
                fold(dot_nt(xv[at, :], bd[b])),
                fold(dot_nt(gv[0, at, :], bu[b])),
            )
            part[at, :] = new if b == 0 else part[at, :] + new
            return 0

        lax.fori_loop(0, count, body, 0)

    def frozen(k, first, start, count):
        def body(t, _):
            i, j = t // wide, t % wide
            at = pl.ds(pl.multiple_of(i * tile, tile), tile)
            over = pl.ds(pl.multiple_of(j * cols, cols), cols)
            new = dot_nt(gv[k, at, :], wv[k, over, :])
            acc[at, over] = new if first else acc[at, over] + new
            return 0

        lax.fori_loop(start * wide, (start + count) * wide, body, 0)

    for k in range(4):
        loads[k].wait()
    project(0)
    for m in range(2):
        own(m).wait_recv()
    loads[4].wait()
    for q in range(quarter):
        if q == quarter - 2:
            project(1)
        else:
            frozen(0, True, min(q, 2), 1)
        for m in range(2):
            over_x(q, m).wait_recv()
            over_y(q, m).start()
            over_core(q, m, mine, 0).start()
    for q in range(quarter):
        for m in range(2):
            dst = maps[m][1]
            at = part_rows(other, q)
            remote(dst.at[2, at], dst.at[2, at], y_send.at[q, m], y_recv.at[q, m], rep=rep ^ 1).wait_recv()
            over_core(q, m, other, 1).start()
        if q == 0:
            frozen(0, True, 3, 1)
    project(2)
    for k in range(2):
        for q in range(quarter):
            for m in range(2):
                at = part_rows(mine if k == 0 else other, q)
                dst = maps[m][1]
                remote(dst.at[2, at], dst.at[3, at], c_send.at[k, q, m], c_recv.at[k, q, m], dp=d ^ 1).wait_recv()
    project(3, far_at, rows // tile // 2)

    near = pl.ds(near_at, half)
    far = pl.ds(far_at, half)
    send_far = remote(part.at[far], far_in, rs_send.at[0], rs_recv.at[0], tensor=z ^ 1)
    send_near = remote(part.at[near], near_in, rs_send.at[1], rs_recv.at[1], tensor=z ^ 1)
    send_cross = remote(far_in, cross_in, rs_send.at[2], rs_recv.at[2], tensor=z ^ 3)
    near_end = remote(rounded.at[near], rounded.at[near], rs_send.at[3], rs_recv.at[3], tensor=z ^ 1)
    near_cross = remote(rounded.at[near], rounded.at[near], rs_send.at[4], rs_recv.at[4], tensor=z ^ 3)
    far_end = remote(rounded.at[far], rounded.at[far], rs_send.at[5], rs_recv.at[4], tensor=z ^ 1)

    def seen(t):
        return -(-t * tile // size)

    def outward(i):
        arrive(3, i)
        relay_end(i).start()

    def across(i):
        arrive(1, i)
        relay_cross(i).start()

    @pl.when(end)
    def _():
        send_far.start()

    project(3, near_at, rows // tile // 2)

    def gather(slot, tiles):
        for t in tiles:
            for i in range(seen(t), seen(t + 1)):
                arrive(slot, i)

    for k in (5, 6, 7):
        loads[k].wait()

    @pl.when(end)
    def _():
        send_near.start()
        to_pair(chunks - 1).start()
        gather(1, range(4))
        frozen(1, False, 0, 4)
        for t in range(HEADS):
            gather(2, (t,))
            frozen(2, False, t, 1)
        remote(rounded.at[near], rounded.at[near], rs_send.at[3], rs_recv.at[3], tensor=z ^ 1).wait_recv()
        remote(rounded.at[far], rounded.at[far], rs_send.at[4], rs_recv.at[4], tensor=z ^ 1).wait_recv()

    @pl.when(middle)
    def _():
        for i in range(EARLY):
            outward(i)
        across(0)
        send_far.wait_recv()
        far_in[...] = part[far, :] + far_in[...]
        send_cross.start()
        for i in range(1, seen(3)):
            arrive(1, i)
        frozen(1, False, 0, 3)
        send_near.wait_recv()
        send_cross.wait_recv()
        rounded[near, :] = ((part[near, :] + near_in[...]) + cross_in[...]).astype(jnp.bfloat16)
        near_cross.start()
        near_end.start()
        for i in range(seen(3), chunks):
            arrive(1, i)
        for i in range(1, chunks):
            relay_cross(i).start()
        remote(rounded.at[far], rounded.at[far], rs_send.at[4], rs_recv.at[4], tensor=z ^ 3).wait_recv()
        far_end.start()
        for i in range(EARLY, chunks):
            outward(i)

    def turn(i, _):
        at = pl.ds(pl.multiple_of(i * 128, 128), 128)
        turned[:, at] = rounded[at, :].astype(jnp.float32).T.astype(jnp.bfloat16)
        return 0

    lax.fori_loop(0, rows // 128, turn, 0)

    head = lax.broadcasted_iota(jnp.int32, (span, 128), 0) // rank

    def fill(b, put_in):
        def body(i, _):
            at = pl.ds(pl.multiple_of(i * 128, 128), 128)
            hit = place_row[:, at] == head + b * owned
            both = turned[:, at].astype(jnp.float32)
            for which, lines in ((0, both[rank:]), (1, both[:rank])):
                lines = jnp.concatenate([lines] * owned, axis=0)
                spread[put_in, which, :, at] = jnp.where(hit, lines, 0.0).astype(jnp.bfloat16)
            return 0

        lax.fori_loop(0, rows // 128, body, 0)

    def product(j, taken):
        if j < pieces - 1:
            return 0.25 * dot_nn(spread[taken, 0], xv[:, j * piece : (j + 1) * piece])
        return 0.25 * dot_nn(spread[taken, 1], gv[0])

    def to_core(k, j):
        return remote(
            pair_out.at[j], pair_in.at[j], pair_send.at[k, j], pair_recv.at[k, j], dp=d ^ 1
        )

    def to_chip(j):
        return remote(far_out.at[j], far_got.at[j], far_send.at[j], far_recv.at[j], dp=d ^ 2)

    def last(i):
        @pl.when(middle)
        def _():
            arrive(2, i)
            relay_last(i).start()

    def last(i):
        @pl.when(middle)
        def _():
            arrive(2, i)
            relay_last(i).start()

    def exchange(k, use):
        def offer(j):
            if k == 1:
                to_core(0, j).wait_send()
            pair_out[j] = product(j, 0)
            to_core(k, j).start()

        offer(0)
        for j in range(pieces):
            if j + 1 < pieces:
                offer(j + 1)
            ours = product(j, 1)
            to_core(k, j).wait_recv()
            use(j, ours + pair_in[j])

    def send_chip(j, value):
        far_out[j] = value.astype(jnp.bfloat16)
        to_chip(j).start()

    def keep(j, value):
        total_part(j)[...] = value

    fill(3, 0)
    fill(2, 1)
    with jax.named_scope("EX0"):
        exchange(0, send_chip)
    pl.semaphore_signal(credit, inc=1, device_id={"dp": d ^ 1}, device_id_type=MESH)
    for i in range(chunks // 3):
        last(i)
    fill(1, 0)
    fill(0, 1)
    pl.semaphore_wait(credit, 1)
    with jax.named_scope("EX1"):
        exchange(1, keep)
    for i in range(chunks // 3, chunks - 2):
        last(i)

    @pl.when(end)
    def _():
        for t in range(HEADS, 4):
            gather(2, (t,))
            frozen(2, False, t, 1)

    @pl.when(middle)
    def _():
        frozen(1, False, 3, 1)

    lane_side = lax.broadcasted_iota(jnp.int32, (tile, 2 * rank), 1) // rank

    def add_side(i, _):
        at = pl.ds(pl.multiple_of(i * tile, tile), tile)
        both = rounded[at, :].astype(jnp.float32)
        both = jnp.where(low, pltpu.roll(both, rank, axis=1), both)
        owner = place_col[at, :]
        for t in range(side_lhs.shape[1] // (2 * rank)):
            side_lhs[:, t * 2 * rank : (t + 1) * 2 * rank] = jnp.where(
                owner == lane_side + 2 * t, both, 0.0
            ).astype(jnp.bfloat16)

        def column(j, _):
            over = pl.ds(pl.multiple_of(j * cols, cols), cols)
            right = bd[:, :, over].reshape(4 * span, cols)
            acc[at, over] = acc[at, over] + 0.25 * dot_nn(side_lhs[...], right)
            return 0

        lax.fori_loop(0, wide, column, 0)
        return 0

    lax.fori_loop(0, rows // tile, add_side, 0)
    last(chunks - 2)

    @pl.when(middle)
    def _():
        arrive(2, chunks - 1)
        frozen(2, False, 0, 4)


    def finish(i):
        @pl.when(end)
        def _():
            arrive(3, i)

        for n in range(i * PARTS, (i + 1) * PARTS):
            at = pl.ds(n * part_size, part_size)
            alive = place_wide(at, cols) >= 0

            def column(j, _):
                over = pl.ds(pl.multiple_of(j * cols, cols), cols)
                value = acc[at, over] + dot_nt(gv[3, at, :], wv[3, over, :])
                xv[at, over] = jnp.where(alive, value, 0.0).astype(jnp.bfloat16)
                return 0

            lax.fori_loop(0, wide, column, 0)

    for i in range(BEFORE):
        finish(i)

    share = 1.0 - decay_rate
    line = jnp.zeros((span, 1), jnp.float32)
    upper = jnp.zeros((span, 1), jnp.float32)
    rows_sum = jnp.zeros((owned, 1), jnp.float32)
    for j in range(pieces):
        to_chip(j).wait_recv()
        value = total_part(j)[...] + far_got[j].astype(jnp.float32)
        total_part(j)[...] = value
        square = value * value + tiny_floor
        mean = jnp.sum(square.reshape(owned, rank, piece), axis=1) / rank
        if j < pieces - 1:
            over = slice(j * piece, (j + 1) * piece)
            fresh = decay_rate * row_factor[:, over] + share * mean
            new_rows[:, over] = fresh
            rows_sum = rows_sum + jnp.sum(fresh, axis=1, keepdims=True)
            line = line + jnp.sum(square, axis=1, keepdims=True)
        else:
            new_columns[...] = decay_rate * column_factor[...] + share * mean
            upper = jnp.sum(square, axis=1, keepdims=True)
    place = lax.broadcasted_iota(jnp.int32, (span, 128), 1)
    spread_sum = jnp.broadcast_to(rows_sum[:, None, :], (owned, rank, 1)).reshape(span, 1)
    packed = jnp.where(place == 0, line, jnp.where(place == 1, upper, spread_sum))
    stat_all[z] = packed.T[:8, :]

    def to_line(k):
        return remote(
            stat_all.at[z], stat_all.at[z], stat_send.at[k - 1], stat_recv.at[k - 1], tensor=z ^ k
        )

    for k in (1, 2, 3):
        to_line(k).start()

    @pl.when(middle)
    def _():
        relay_last(chunks - 1).start()

    for i in range(BEFORE, chunks - 2):
        finish(i)
    for k in (1, 2, 3):
        remote(
            stat_all.at[z ^ k], stat_all.at[z ^ k], stat_send.at[k - 1], stat_recv.at[k - 1], tensor=z ^ k
        ).wait_recv()
    summed = (stat_all[0] + stat_all[1]) + (stat_all[2] + stat_all[3])
    full_width = depth * 4
    pair_width = width * 4

    def in_line(ref):
        return jnp.concatenate([ref[e : e + 1, :] for e in range(owned)], axis=1)

    down_cols = decay_rate * in_line(line_factor) + share * (summed[0:1, :] / full_width)
    up_rows = decay_rate * in_line(upper_factor) + share * (summed[1:2, :] / pair_width)
    for e in range(owned):
        new_line[e : e + 1, :] = down_cols[:, e * rank : (e + 1) * rank]
        new_upper[e : e + 1, :] = up_rows[:, e * rank : (e + 1) * rank]
    ratio = down_cols / (summed[2:3, :] / full_width)
    index = lax.broadcasted_iota(jnp.int32, (128, span), 0)
    back = jnp.where(index == 0, ratio, up_rows).T
    down_scale = lax.rsqrt(back[:, 0:1])
    up_column = back[:, 1:2].reshape(owned, rank, 1)
    up_mean = jnp.sum(up_column, axis=1, keepdims=True) / rank
    up_scale = lax.rsqrt(up_column / up_mean).reshape(span, 1)

    for j in range(pieces):
        if j < pieces - 1:
            row_scale = lax.rsqrt(new_rows[:, j * piece : (j + 1) * piece])
            column_scale = down_scale
        else:
            row_scale = lax.rsqrt(new_columns[...])
            column_scale = up_scale
        row_scale = jnp.broadcast_to(row_scale[:, None, :], (owned, rank, piece)).reshape(span, piece)
        total_part(j)[...] = total_part(j)[...] * row_scale * column_scale

    for i in range(chunks - 2, chunks):
        finish(i)

    for i in range(chunks):
        to_pair(i).wait_send()

        @pl.when(middle)
        def _():
            to_cross(i).wait_send()
            relay_cross(i).wait_send()
            relay_end(i).wait_send()
            relay_last(i).wait_send()

    for m in range(2):
        own(m).wait_send()
        for q in range(quarter):
            over_x(q, m).wait_send()
            over_y(q, m).wait_send()
            over_core(q, m, mine, 0).wait_send()
            over_core(q, m, other, 1).wait_send()

    @pl.when(end)
    def _():
        send_far.wait_send()
        send_near.wait_send()

    @pl.when(middle)
    def _():
        send_cross.wait_send()
        near_end.wait_send()
        near_cross.wait_send()
        far_end.wait_send()

    for j in range(pieces):
        to_core(1, j).wait_send()
        to_chip(j).wait_send()
    for k in (1, 2, 3):
        to_line(k).wait_send()


def hand_over_kernel(count, steps, *refs):
    sources, targets, sem = refs[:count], refs[count : 2 * count], refs[2 * count]
    copies = []
    for k in range(count):
        rows = sources[k].shape[0] // steps[k]
        for i in range(steps[k]):
            at = pl.ds(i * rows, rows)
            copies.append(
                pltpu.make_async_copy(sources[k].at[at], targets[k].at[at], sem.at[len(copies)])
            )
    for copy in copies:
        copy.start()
    for copy in copies:
        copy.wait()


def hand_over(results):
    count = len(results)
    steps = [4 if r.shape[0] % 64 == 0 else 1 for r in results]
    return pl.pallas_call(
        functools.partial(hand_over_kernel, count, steps),
        out_shape=tuple(jax.ShapeDtypeStruct(r.shape, r.dtype) for r in results),
        in_specs=[pl.BlockSpec(memory_space=pltpu.VMEM)] * count,
        out_specs=(pl.BlockSpec(memory_space=pl.ANY),) * count,
        scratch_shapes=[pltpu.SemaphoreType.DMA((sum(steps),))],
        compiler_params=pltpu.CompilerParams(vmem_limit_bytes=HAND_LIMIT),
        name="hand_over",
    )(*[pltpu.with_memory_space_constraint(r, pltpu.VMEM) for r in results])


def fused(activations, output_gradient, tenants, live_count, entry_of, weight, down_maps, up_maps, factors):
    rows, depth = activations.shape
    width = output_gradient.shape[1]
    owned, _, rank = down_maps.shape
    span = owned * rank
    chunks, quarter = 6, 4
    piece = width
    pieces = depth // piece + 1
    half = rows // 2
    any_spec = pl.BlockSpec(memory_space=pl.ANY)
    vmem = pl.BlockSpec(memory_space=pltpu.VMEM)
    dma = pltpu.SemaphoreType.DMA
    smem = pl.BlockSpec(memory_space=pltpu.SMEM)
    scratch = [
        pltpu.VMEM((rows, 128), jnp.int32),
        pltpu.VMEM((1, rows), jnp.int32),
        pltpu.VMEM((4, rows, width), bf16),
        pltpu.VMEM((4, depth, width), bf16),
        pltpu.VMEM((4, span, depth), bf16),
        pltpu.VMEM((4, span, width), bf16),
        pltpu.VMEM((rows, depth), f32),
        pltpu.VMEM((rows, 2 * rank), f32),
        pltpu.VMEM((half, 2 * rank), f32),
        pltpu.VMEM((half, 2 * rank), f32),
        pltpu.VMEM((half, 2 * rank), f32),
        pltpu.VMEM((rows, 2 * rank), bf16),
        pltpu.VMEM((2 * rank, rows), bf16),
        pltpu.VMEM((2, 2, span, rows), bf16),
        pltpu.VMEM((rows // 4, 4 * span), bf16),
        pltpu.VMEM((pieces, span, piece), f32),
        pltpu.VMEM((pieces, span, piece), f32),
        pltpu.VMEM((pieces, span, piece), bf16),
        pltpu.VMEM((pieces, span, piece), bf16),
        pltpu.VMEM((4, 8, span), f32),
        dma((8,)),
        dma((5, chunks)),
        dma((3, chunks)),
        dma((2,)),
        dma((2,)),
        dma((quarter, 2)),
        dma((quarter, 2)),
        dma((quarter, 2)),
        dma((quarter, 2)),
        dma((2, quarter, 2)),
        dma((2, quarter, 2)),
        dma((6,)),
        dma((5,)),
        dma((2, pieces)),
        dma((2, pieces)),
        dma((pieces,)),
        dma((pieces,)),
        dma((3,)),
        dma((3,)),
        pltpu.SemaphoreType.REGULAR,
    ]
    results = pl.pallas_call(
        functools.partial(fused_kernel, rank),
        out_shape=(
            pltpu.VMEM((rows, depth), bf16),
            pltpu.VMEM((owned, depth), f32),
            pltpu.VMEM((owned, width), f32),
            pltpu.VMEM((owned, rank), f32),
            pltpu.VMEM((owned, rank), f32),
            pltpu.VMEM((span, depth), f32),
            pltpu.VMEM((span, width), f32),
        ),
        in_specs=[any_spec] * 5 + [vmem, smem, smem] + [vmem] * 4,
        out_specs=(vmem,) * 7,
        scratch_shapes=scratch,
        compiler_params=pltpu.CompilerParams(
            collective_id=0, has_side_effects=True, vmem_limit_bytes=VMEM_LIMIT
        ),
        name="fused",
    )(
        activations,
        output_gradient,
        weight,
        down_maps.transpose(0, 2, 1).reshape(span, depth),
        up_maps.reshape(span, width),
        tenants,
        live_count,
        entry_of,
        *factors,
    )
    return hand_over(results)


def fits(activations, output_gradient, down_maps):
    rows, depth = activations.shape
    width = output_gradient.shape[1]
    owned, _, rank = down_maps.shape
    return (
        lax.axis_size("tensor") == 4
        and lax.axis_size("dp") == 4
        and lax.axis_size("rep") == 2
        and rank == 64
        and owned % 2 == 0
        and owned * rank // 8 % 16 == 0
        and rows % 768 == 0
        and width % 128 == 0
        and depth % width == 0
    )


def dot(a, b, ca, cb):
    return lax.dot_general(a, b, (((ca,), (cb,)), ((), ())), preferred_element_type=f32)


def chip_shift(value, groups, step):
    chips = groups // CORES
    pairs = [(d, (d // CORES + step) % chips * CORES + d % CORES) for d in range(groups)]
    return lax.ppermute(value, "dp", pairs)


def core_swap(value, groups):
    return lax.ppermute(value, "dp", [(d, d ^ 1) for d in range(groups)])


def ring_shift(value, size, step):
    return lax.ppermute(value, "tensor", [(t, (t + step) % size) for t in range(size)])


def total_small(value, size):
    if size > 8:
        return lax.psum(value, "tensor")
    me = lax.axis_index("tensor")
    parts = jnp.zeros((size,) + value.shape, value.dtype)
    parts = lax.dynamic_update_index_in_dim(parts, value, me, 0)
    for step in range(1, size):
        got = ring_shift(value, size, step)
        parts = lax.dynamic_update_index_in_dim(parts, got, (me - step) % size, 0)
    return jnp.sum(parts, axis=0)


def total_rows(value, size):
    if size > 8:
        return lax.psum(value, "tensor").astype(bf16)
    me = lax.axis_index("tensor")
    rows = value.shape[0] // size

    def piece(index):
        return lax.dynamic_slice_in_dim(value, index % size * rows, rows, 0)

    total = piece(me)
    for step in range(1, size):
        total = total + ring_shift(piece(me + step), size, step)
    mine = total.astype(bf16)
    out = jnp.zeros(value.shape, bf16)
    out = lax.dynamic_update_slice_in_dim(out, mine, me * rows, 0)
    for step in range(1, size):
        got = ring_shift(mine, size, step)
        out = lax.dynamic_update_slice_in_dim(out, got, (me - step) % size * rows, 0)
    return out


def shards(
    activations,
    output_gradient,
    row_tenant,
    group_row_count,
    tenant_storage_entry,
    key_value_weight,
    adapter_down_maps,
    adapter_up_maps,
    down_row_factor,
    down_column_factor,
    up_row_factor,
    up_column_factor,
):
    groups = lax.axis_size("dp")
    size = lax.axis_size("tensor")
    chips = groups // CORES
    owned, depth, rank = adapter_down_maps.shape
    width = adapter_up_maps.shape[2]
    entries = owned * groups
    count_rows = activations.shape[0]
    full_width = depth * size
    pair_width = key_value_weight.shape[1]
    here = lax.axis_index("dp")
    chip, core = here // CORES, here % CORES
    if fits(activations, output_gradient, adapter_down_maps):
        input_grad, down_rows, up_cols, down_cols, up_rows, down_update, up_update = fused(
            activations,
            output_gradient,
            row_tenant.reshape(1, count_rows),
            group_row_count,
            tenant_storage_entry,
            key_value_weight,
            adapter_down_maps,
            adapter_up_maps,
            (down_row_factor, up_column_factor, down_column_factor, up_row_factor),
        )
        return (
            input_grad,
            down_rows,
            down_cols,
            up_rows,
            up_cols,
            down_update.reshape(owned, rank, depth).transpose(0, 2, 1),
            up_update.reshape(owned, rank, width),
        )
    gathered = lax.all_gather(output_gradient, "tensor", axis=1, tiled=True)
    own_maps = jnp.concatenate(
        [adapter_down_maps.transpose(0, 2, 1), adapter_up_maps], axis=2
    ).reshape(owned * rank, depth + width)
    blocks = []
    for s in range(chips):
        column = own_maps if s == 0 else chip_shift(own_maps, groups, s)
        blocks.append(jnp.concatenate([column, core_swap(column, groups)], axis=0))
    live = jnp.arange(count_rows, dtype=jnp.int32)[:, None] < group_row_count[0]
    masked = jnp.where(live, output_gradient, jnp.zeros_like(output_gradient))
    tse = tenant_storage_entry
    owner = tse // owned
    place = (
        (chip - owner // CORES) % chips * CORES + (owner % CORES != core).astype(jnp.int32)
    ) * owned + tse % owned
    tenants = row_tenant[:, 0]
    place_of = jnp.sum(
        jnp.where(
            tenants[:, None] == jnp.arange(entries, dtype=jnp.int32)[None, :], place[None, :], 0
        ),
        axis=1,
    )
    span = CORES * owned * rank
    pair = 2 * rank
    lanes = jnp.arange(span, dtype=jnp.int32)[None, :] // rank

    def wide(s):
        return place_of[:, None] == lanes + s * CORES * owned

    def pick(s, product):
        kept = jnp.where(wide(s), product, 0.0)
        both = kept[:, :pair]
        for i in range(1, span // pair):
            both = both + kept[:, i * pair : (i + 1) * pair]
        return both

    picked_down = picked_up = 0.0
    for s in range(chips):
        picked_down += pick(s, dot(activations, blocks[s][:, :depth], 1, 1))
        picked_up += pick(s, dot(masked, blocks[s][:, depth:], 1, 1))
    partial = jnp.concatenate(
        [
            picked_down[:, :rank] + picked_down[:, rank:],
            picked_up[:, :rank] + picked_up[:, rank:],
        ],
        axis=1,
    )
    rounded = total_rows(partial, size)
    zero = jnp.zeros((), bf16)
    repeat_down = jnp.tile(rounded[:, :rank], (1, span // rank))
    repeat_up = jnp.tile(rounded[:, rank:], (1, span // rank))
    half = owned * rank
    spreads = [jnp.where(wide(s), repeat_up, zero) for s in range(chips)]
    pieces = []
    for s in list(range(1, chips)) + [0]:
        spread_down = jnp.where(wide(s), repeat_down, zero)
        terms = [
            adapter_scale
            * jnp.concatenate(
                [
                    dot(spreads[s][:, k : k + half], activations, 0, 0),
                    dot(spread_down[:, k : k + half], masked, 0, 0),
                ],
                axis=1,
            )
            for k in (half, 0)
        ]
        summed = terms[1] + core_swap(terms[0], groups)
        pieces.append(chip_shift(summed.astype(bf16), groups, -s) if s else summed)
    side = lax.optimization_barrier(
        (
            adapter_scale
            * dot(
                jnp.concatenate(spreads, axis=1),
                jnp.concatenate([b[:, :depth] for b in blocks], axis=0),
                1,
                0,
            )
        ).astype(bf16)
    )
    frozen = jnp.where(live, dot(gathered, key_value_weight, 1, 1), 0.0)
    input_grad = (frozen + side.astype(f32)).astype(bf16)
    pieces, input_grad = lax.optimization_barrier((pieces, input_grad))
    grads = sum(p.astype(f32) for p in pieces)
    grads = grads.reshape(owned, rank, depth + width)
    down_gradient, up_gradient = grads[:, :, :depth], grads[:, :, depth:]
    square_down = down_gradient * down_gradient + tiny_floor
    square_up = up_gradient * up_gradient + tiny_floor
    down_rows = decay_rate * down_row_factor + (1.0 - decay_rate) * jnp.mean(square_down, axis=1)
    up_cols = decay_rate * up_column_factor + (1.0 - decay_rate) * jnp.mean(square_up, axis=1)
    stats = jnp.concatenate(
        [
            jnp.sum(square_down, axis=2),
            jnp.sum(square_up, axis=2),
            jnp.broadcast_to(jnp.sum(down_rows, axis=1)[:, None], (owned, pair)),
        ],
        axis=1,
    )
    stats = total_small(stats, size)
    column_total, row_total = stats[:, :rank], stats[:, rank:pair]
    rows_sum = stats[:, pair]
    down_cols = decay_rate * down_column_factor + (1.0 - decay_rate) * (column_total / full_width)
    up_rows = decay_rate * up_row_factor + (1.0 - decay_rate) * (row_total / pair_width)
    second_down = (
        down_rows[:, None, :] * down_cols[:, :, None] / (rows_sum / full_width)[:, None, None]
    )
    second_up = up_rows[:, :, None] * up_cols[:, None, :] / jnp.mean(up_rows, axis=1)[:, None, None]
    down_update = (down_gradient * lax.rsqrt(second_down)).transpose(0, 2, 1)
    up_update = up_gradient * lax.rsqrt(second_up)
    return (input_grad, down_rows, down_cols, up_rows, up_cols, down_update, up_update)


def solution(mesh):
    in_specs = (
        P(("rep", "dp"), "tensor"),
        P(("rep", "dp"), "tensor"),
        P(("rep", "dp"), None),
        P(("rep", "dp")),
        P(),
        P("tensor", None),
        P("dp", "tensor", None),
        P("dp", None, "tensor"),
        P("dp", "tensor"),
        P("dp", None),
        P("dp", None),
        P("dp", "tensor"),
    )
    out_specs = (
        P(("rep", "dp"), "tensor"),
        P(("rep", "dp"), "tensor"),
        P(("rep", "dp"), None),
        P(("rep", "dp"), None),
        P(("rep", "dp"), "tensor"),
        P(("rep", "dp"), "tensor", None),
        P(("rep", "dp"), None, "tensor"),
    )
    return jax.shard_map(shards, mesh=mesh, in_specs=in_specs, out_specs=out_specs, check_vma=False)
```

```python
import functools

import jax
import jax.numpy as jnp
from jax import lax
from jax.experimental import pallas as pl
from jax.experimental.pallas import tpu as pltpu
from jax.sharding import PartitionSpec as P

HAND_LIMIT = 4_000_000
adapter_scale = 0.25
decay_rate = 0.9
tiny_floor = 1e-30
f32 = jnp.float32
bf16 = jnp.bfloat16
CORES = 2
VMEM_LIMIT = 57_000_000
MESH = pl.DeviceIdType.MESH
EARLY = 3
BEFORE = 3
HEADS = 2


def dot_nt(a, b):
    return lax.dot_general(a, b, (((1,), (1,)), ((), ())), preferred_element_type=jnp.float32)


def dot_nn(a, b):
    return lax.dot_general(a, b, (((1,), (0,)), ((), ())), preferred_element_type=jnp.float32)


def fused_kernel(
    rank,
    x_hbm,
    g_hbm,
    w_hbm,
    down_hbm,
    up_hbm,
    tenants_hbm,
    live_hbm,
    entry_hbm,
    row_hbm,
    column_hbm,
    line_hbm,
    upper_hbm,
    xv,
    new_rows,
    new_columns,
    new_line,
    new_upper,
    total_down,
    total_up,
    place_col,
    place_row,
    tenants,
    live_count,
    entry_of,
    row_factor,
    column_factor,
    line_factor,
    upper_factor,
    gv,
    wv,
    bd,
    bu,
    acc,
    part,
    far_in,
    near_in,
    cross_in,
    rounded,
    turned,
    spread,
    side_lhs,
    pair_out,
    pair_in,
    far_out,
    far_got,
    stat_all,
    load_sem,
    ag_send,
    ag_recv,
    own_send,
    own_recv,
    x_send,
    x_recv,
    y_send,
    y_recv,
    c_send,
    c_recv,
    rs_send,
    rs_recv,
    pair_send,
    pair_recv,
    far_send,
    far_recv,
    stat_send,
    stat_recv,
    credit,
):
    z = lax.axis_index("tensor")
    d = lax.axis_index("dp")
    rep = lax.axis_index("rep")
    middle = (z == 1) | (z == 2)
    end = (z == 0) | (z == 3)
    rows, depth = xv.shape
    width = gv.shape[2]
    span = bd.shape[1]
    owned = span // rank
    chunks = ag_recv.shape[1]
    size = rows // (chunks - 1)
    bounds = [i * size for i in range(chunks - 1)] + [rows - size // 2, rows]
    half = rows // 2
    tile = rows // 4
    cols = 512 if depth % 512 == 0 else depth
    wide = depth // cols
    piece = width
    pieces = depth // piece + 1
    quarter = x_recv.shape[0]
    step = span // 2 // quarter
    near_at = pl.multiple_of(z // 2 * half, half)
    far_at = pl.multiple_of((1 - z // 2) * half, half)

    def total_part(j):
        if j < pieces - 1:
            return total_down.at[:, j * piece : (j + 1) * piece]
        return total_up

    def remote(src, dst, ss, rs, **where):
        return pltpu.make_async_remote_copy(
            src_ref=src, dst_ref=dst, send_sem=ss, recv_sem=rs, device_id=where, device_id_type=MESH
        )

    def local(src, dst, sem):
        return pltpu.make_async_copy(src, dst, sem)

    barrier = pltpu.get_barrier_semaphore()
    peers = [
        {"tensor": z ^ 1},
        {"tensor": z ^ 2},
        {"tensor": z ^ 3},
        {"dp": d ^ 1},
        {"dp": d ^ 2},
        {"rep": rep ^ 1},
    ]
    for peer in peers:
        pl.semaphore_signal(barrier, inc=1, device_id=peer, device_id_type=MESH)
    loads = [
        local(g_hbm, gv.at[0], load_sem.at[0]),
        local(down_hbm, bd.at[0], load_sem.at[1]),
        local(up_hbm, bu.at[0], load_sem.at[2]),
        local(x_hbm, xv, load_sem.at[3]),
    ]
    for k in range(4):
        at = pl.multiple_of((z ^ k) * width, width)
        loads.append(local(w_hbm.at[:, pl.ds(at, width)], wv.at[k], load_sem.at[4 + k]))
    smalls = [
        local(tenants_hbm, tenants, load_sem.at[8]),
        local(live_hbm, live_count, load_sem.at[9]),
        local(entry_hbm, entry_of, load_sem.at[10]),
        local(row_hbm, row_factor, load_sem.at[11]),
        local(column_hbm, column_factor, load_sem.at[12]),
        local(line_hbm, line_factor, load_sem.at[13]),
        local(upper_hbm, upper_factor, load_sem.at[14]),
    ]
    for copy in smalls + loads:
        copy.start()

    pl.semaphore_wait(barrier, len(peers))

    def chunk(i):
        return pl.ds(bounds[i], bounds[i + 1] - bounds[i])

    def to_pair(i):
        return remote(
            g_hbm.at[chunk(i)], gv.at[1, chunk(i)], ag_send.at[0], ag_recv.at[0, i], tensor=z ^ 1
        )

    def to_cross(i):
        return remote(
            g_hbm.at[chunk(i)], gv.at[3, chunk(i)], ag_send.at[1], ag_recv.at[2, i], tensor=z ^ 3
        )

    def relay_cross(i):
        return remote(
            gv.at[1, chunk(i)], gv.at[2, chunk(i)], ag_send.at[2], ag_recv.at[1, i], tensor=z ^ 3
        )

    def relay_end(i):
        return remote(
            gv.at[3, chunk(i)], gv.at[2, chunk(i)], ag_send.at[3], ag_recv.at[1, i], tensor=z ^ 1
        )

    def relay_last(i):
        return remote(
            gv.at[2, chunk(i)], gv.at[3, chunk(i)], ag_send.at[4], ag_recv.at[2, i], tensor=z ^ 1
        )

    def arrive(slot, i):
        remote(
            gv.at[slot, chunk(i)], gv.at[slot, chunk(i)], ag_send.at[0], ag_recv.at[slot - 1, i], tensor=z ^ 1
        ).wait_recv()

    for i in range(chunks - 2):
        to_pair(i).start()

    @pl.when(middle)
    def _():
        for i in range(chunks - 2, chunks):
            to_pair(i).start()
        for i in range(chunks):
            to_cross(i).start()

    maps = ((down_hbm, bd), (up_hbm, bu))

    def own(m):
        src, dst = maps[m]
        return remote(src, dst.at[1], own_send.at[m], own_recv.at[m], dp=d ^ 1)

    mine = rep * (span // 2)
    other = (1 - rep) * (span // 2)

    def part_rows(base, q):
        return pl.ds(pl.multiple_of(base + q * step, step), step)

    def over_x(q, m):
        src, dst = maps[m]
        at = part_rows(mine, q)
        return remote(src.at[at], dst.at[2, at], x_send.at[m], x_recv.at[q, m], dp=d ^ 2)

    def over_y(q, m):
        dst = maps[m][1]
        at = part_rows(mine, q)
        return remote(dst.at[2, at], dst.at[2, at], y_send.at[m], y_recv.at[q, m], rep=rep ^ 1)

    def over_core(q, m, base, k):
        dst = maps[m][1]
        at = part_rows(base, q)
        return remote(dst.at[2, at], dst.at[3, at], c_send.at[m], c_recv.at[m], dp=d ^ 1)

    for q in range(quarter):
        for m in range(2):
            over_x(q, m).start()
    for m in range(2):
        own(m).start()

    for copy in smalls:
        copy.wait()
    named = tenants[...]
    entry = entry_of[...]
    owner = sum((entry >= k * owned).astype(jnp.int32) for k in range(1, 4))
    chip = (owner >= 2).astype(jnp.int32)
    away = (chip != d // 2).astype(jnp.int32) * 2 + (owner - 2 * chip != d % 2).astype(jnp.int32)
    spot = away * owned + (entry - owner * owned)
    found = jnp.zeros((1, rows), jnp.int32)
    for t in range(entry_of.shape[1]):
        found = jnp.where(named == t, jnp.broadcast_to(spot[:, t : t + 1], (1, rows)), found)
    alive = lax.broadcasted_iota(jnp.int32, (1, rows), 1) < live_count[...]
    place_row[...] = jnp.where(alive, found, -1)

    def stand(i, _):
        at = pl.ds(pl.multiple_of(i * 128, 128), 128)
        lines = jnp.broadcast_to(place_row[:, at].astype(jnp.float32), (128, 128))
        place_col[at, :] = lines.T.astype(jnp.int32)
        return 0

    lax.fori_loop(0, rows // 128, stand, 0)

    def place_wide(at, lanes):
        return jnp.concatenate([place_col[at, :]] * (lanes // 128), axis=1)

    lane = lax.broadcasted_iota(jnp.int32, (tile, span), 1) // rank
    low = lax.broadcasted_iota(jnp.int32, (tile, 2 * rank), 1) < rank

    def project(b, base=0, count=rows // tile):
        def body(i, _):
            at = pl.ds(pl.multiple_of(base + i * tile, tile), tile)
            hit = place_wide(at, span) == lane + b * owned

            def fold(product):
                kept = jnp.where(hit, product, 0.0)
                both = kept[:, : 2 * rank]
                for j in range(1, span // (2 * rank)):
                    both = both + kept[:, j * 2 * rank : (j + 1) * 2 * rank]
                return both + pltpu.roll(both, rank, axis=1)

            new = jnp.where(
                low,
                fold(dot_nt(xv[at, :], bd[b])),
                fold(dot_nt(gv[0, at, :], bu[b])),
            )
            part[at, :] = new if b == 0 else part[at, :] + new
            return 0

        lax.fori_loop(0, count, body, 0)

    def frozen(k, first, start, count):
        def body(t, _):
            i, j = t // wide, t % wide
            at = pl.ds(pl.multiple_of(i * tile, tile), tile)
            over = pl.ds(pl.multiple_of(j * cols, cols), cols)
            new = dot_nt(gv[k, at, :], wv[k, over, :])
            acc[at, over] = new if first else acc[at, over] + new
            return 0

        lax.fori_loop(start * wide, (start + count) * wide, body, 0)

    for k in range(4):
        loads[k].wait()
    project(0)
    for m in range(2):
        own(m).wait_recv()
    loads[4].wait()
    for q in range(quarter):
        if q == quarter - 2:
            project(1)
        else:
            frozen(0, True, min(q, 2), 1)
        for m in range(2):
            over_x(q, m).wait_recv()
            over_y(q, m).start()
            over_core(q, m, mine, 0).start()
    for q in range(quarter):
        for m in range(2):
            dst = maps[m][1]
            at = part_rows(other, q)
            remote(dst.at[2, at], dst.at[2, at], y_send.at[m], y_recv.at[q, m], rep=rep ^ 1).wait_recv()
            over_core(q, m, other, 1).start()
        if q == 0:
            frozen(0, True, 3, 1)
    project(2)
    for m in range(2):
        dst = maps[m][1]
        remote(dst.at[2], dst.at[3], c_send.at[m], c_recv.at[m], dp=d ^ 1).wait_recv()
    project(3, far_at, rows // tile // 2)

    near = pl.ds(near_at, half)
    far = pl.ds(far_at, half)
    send_far = remote(part.at[far], far_in, rs_send.at[0], rs_recv.at[0], tensor=z ^ 1)
    send_near = remote(part.at[near], near_in, rs_send.at[1], rs_recv.at[1], tensor=z ^ 1)
    send_cross = remote(far_in, cross_in, rs_send.at[2], rs_recv.at[2], tensor=z ^ 3)
    near_end = remote(rounded.at[near], rounded.at[near], rs_send.at[3], rs_recv.at[3], tensor=z ^ 1)
    near_cross = remote(rounded.at[near], rounded.at[near], rs_send.at[4], rs_recv.at[4], tensor=z ^ 3)
    far_end = remote(rounded.at[far], rounded.at[far], rs_send.at[5], rs_recv.at[4], tensor=z ^ 1)

    def seen(t):
        return sum(b < t * tile for b in bounds[:-1])

    def outward(i):
        arrive(3, i)
        relay_end(i).start()

    def across(i):
        arrive(1, i)
        relay_cross(i).start()

    @pl.when(end)
    def _():
        send_far.start()

    project(3, near_at, rows // tile // 2)

    def gather(slot, tiles):
        for t in tiles:
            for i in range(seen(t), seen(t + 1)):
                arrive(slot, i)

    for k in (5, 6, 7):
        loads[k].wait()

    @pl.when(end)
    def _():
        send_near.start()
        for i in range(chunks - 2, chunks):
            to_pair(i).start()
        gather(1, range(4))
        frozen(1, False, 0, 4)
        for t in range(HEADS):
            gather(2, (t,))
            frozen(2, False, t, 1)
        remote(rounded.at[near], rounded.at[near], rs_send.at[3], rs_recv.at[3], tensor=z ^ 1).wait_recv()
        remote(rounded.at[far], rounded.at[far], rs_send.at[4], rs_recv.at[4], tensor=z ^ 1).wait_recv()

    @pl.when(middle)
    def _():
        for i in range(EARLY):
            outward(i)
        across(0)
        send_far.wait_recv()
        far_in[...] = part[far, :] + far_in[...]
        send_cross.start()
        for i in range(1, seen(3)):
            arrive(1, i)
        frozen(1, False, 0, 3)
        send_near.wait_recv()
        send_cross.wait_recv()
        rounded[near, :] = ((part[near, :] + near_in[...]) + cross_in[...]).astype(jnp.bfloat16)
        near_cross.start()
        near_end.start()
        for i in range(seen(3), chunks):
            arrive(1, i)
        for i in range(1, chunks):
            relay_cross(i).start()
        remote(rounded.at[far], rounded.at[far], rs_send.at[4], rs_recv.at[4], tensor=z ^ 3).wait_recv()
        far_end.start()
        for i in range(EARLY, chunks):
            outward(i)

    def turn(i, _):
        at = pl.ds(pl.multiple_of(i * 128, 128), 128)
        turned[:, at] = rounded[at, :].astype(jnp.float32).T.astype(jnp.bfloat16)
        return 0

    lax.fori_loop(0, rows // 128, turn, 0)

    head = lax.broadcasted_iota(jnp.int32, (span, 128), 0) // rank

    def fill(b, put_in):
        def body(i, _):
            at = pl.ds(pl.multiple_of(i * 128, 128), 128)
            hit = place_row[:, at] == head + b * owned
            both = turned[:, at].astype(jnp.float32)
            for which, lines in ((0, both[rank:]), (1, both[:rank])):
                lines = jnp.concatenate([lines] * owned, axis=0)
                spread[put_in, which, :, at] = jnp.where(hit, lines, 0.0).astype(jnp.bfloat16)
            return 0

        lax.fori_loop(0, rows // 128, body, 0)

    def product(j, taken):
        if j < pieces - 1:
            return 0.25 * dot_nn(spread[taken, 0], xv[:, j * piece : (j + 1) * piece])
        return 0.25 * dot_nn(spread[taken, 1], gv[0])

    def to_core(k, j):
        return remote(
            pair_out.at[j], pair_in.at[j], pair_send.at[k, j], pair_recv.at[k, j], dp=d ^ 1
        )

    def to_chip(j):
        return remote(far_out.at[j], far_got.at[j], far_send.at[0], far_recv.at[j], dp=d ^ 2)

    def last(i):
        @pl.when(middle)
        def _():
            arrive(2, i)
            relay_last(i).start()

    def last(i):
        @pl.when(middle)
        def _():
            arrive(2, i)
            relay_last(i).start()

    def exchange(k, use):
        def offer(j):
            if k == 1:
                to_core(0, j).wait_send()
            pair_out[j] = product(j, 0)
            to_core(k, j).start()

        offer(0)
        for j in range(pieces):
            if j + 1 < pieces:
                offer(j + 1)
            ours = product(j, 1)
            to_core(k, j).wait_recv()
            use(j, ours + pair_in[j])

    def send_chip(j, value):
        far_out[j] = value.astype(jnp.bfloat16)
        to_chip(j).start()

    def keep(j, value):
        total_part(j)[...] = value

    fill(3, 0)
    fill(2, 1)
    with jax.named_scope("EX0"):
        exchange(0, send_chip)
    pl.semaphore_signal(credit, inc=1, device_id={"dp": d ^ 1}, device_id_type=MESH)
    for i in range(chunks // 3):
        last(i)
    fill(1, 0)
    fill(0, 1)
    pl.semaphore_wait(credit, 1)
    with jax.named_scope("EX1"):
        exchange(1, keep)
    for i in range(chunks // 3, chunks - 2):
        last(i)

    @pl.when(end)
    def _():
        for t in range(HEADS, 4):
            gather(2, (t,))
            frozen(2, False, t, 1)

    @pl.when(middle)
    def _():
        frozen(1, False, 3, 1)

    lane_side = lax.broadcasted_iota(jnp.int32, (tile, 2 * rank), 1) // rank

    def add_side(i, _):
        at = pl.ds(pl.multiple_of(i * tile, tile), tile)
        both = rounded[at, :].astype(jnp.float32)
        both = jnp.where(low, pltpu.roll(both, rank, axis=1), both)
        owner = place_col[at, :]
        for t in range(side_lhs.shape[1] // (2 * rank)):
            side_lhs[:, t * 2 * rank : (t + 1) * 2 * rank] = jnp.where(
                owner == lane_side + 2 * t, both, 0.0
            ).astype(jnp.bfloat16)

        def column(j, _):
            over = pl.ds(pl.multiple_of(j * cols, cols), cols)
            right = bd[:, :, over].reshape(4 * span, cols)
            acc[at, over] = acc[at, over] + 0.25 * dot_nn(side_lhs[...], right)
            return 0

        lax.fori_loop(0, wide, column, 0)
        return 0

    lax.fori_loop(0, rows // tile, add_side, 0)
    @pl.when(middle)
    def _():
        for i in range(chunks - 2, chunks):
            arrive(2, i)
        frozen(2, False, 0, 4)


    def finish(i):
        @pl.when(end)
        def _():
            arrive(3, i)

        at = chunk(i)
        alive = place_wide(at, cols) >= 0

        def column(j, _):
            over = pl.ds(pl.multiple_of(j * cols, cols), cols)
            value = acc[at, over] + dot_nt(gv[3, at, :], wv[3, over, :])
            xv[at, over] = jnp.where(alive, value, 0.0).astype(jnp.bfloat16)
            return 0

        lax.fori_loop(0, wide, column, 0)

    for i in range(BEFORE):
        finish(i)

    share = 1.0 - decay_rate
    line = jnp.zeros((span, 1), jnp.float32)
    upper = jnp.zeros((span, 1), jnp.float32)
    rows_sum = jnp.zeros((owned, 1), jnp.float32)
    for j in range(pieces):
        to_chip(j).wait_recv()
        value = total_part(j)[...] + far_got[j].astype(jnp.float32)
        total_part(j)[...] = value
        square = value * value + tiny_floor
        mean = jnp.sum(square.reshape(owned, rank, piece), axis=1) / rank
        if j < pieces - 1:
            over = slice(j * piece, (j + 1) * piece)
            fresh = decay_rate * row_factor[:, over] + share * mean
            new_rows[:, over] = fresh
            rows_sum = rows_sum + jnp.sum(fresh, axis=1, keepdims=True)
            line = line + jnp.sum(square, axis=1, keepdims=True)
        else:
            new_columns[...] = decay_rate * column_factor[...] + share * mean
            upper = jnp.sum(square, axis=1, keepdims=True)
    place = lax.broadcasted_iota(jnp.int32, (span, 128), 1)
    spread_sum = jnp.broadcast_to(rows_sum[:, None, :], (owned, rank, 1)).reshape(span, 1)
    packed = jnp.where(place == 0, line, jnp.where(place == 1, upper, spread_sum))
    stat_all[z] = packed.T[:8, :]

    def to_line(k):
        return remote(
            stat_all.at[z], stat_all.at[z], stat_send.at[k - 1], stat_recv.at[k - 1], tensor=z ^ k
        )

    for k in (1, 2, 3):
        to_line(k).start()

    @pl.when(middle)
    def _():
        for i in range(chunks - 2, chunks):
            relay_last(i).start()

    for i in range(BEFORE, chunks - 3):
        finish(i)
    for k in (1, 2, 3):
        remote(
            stat_all.at[z ^ k], stat_all.at[z ^ k], stat_send.at[k - 1], stat_recv.at[k - 1], tensor=z ^ k
        ).wait_recv()
    summed = (stat_all[0] + stat_all[1]) + (stat_all[2] + stat_all[3])
    full_width = depth * 4
    pair_width = width * 4

    def in_line(ref):
        return jnp.concatenate([ref[e : e + 1, :] for e in range(owned)], axis=1)

    down_cols = decay_rate * in_line(line_factor) + share * (summed[0:1, :] / full_width)
    up_rows = decay_rate * in_line(upper_factor) + share * (summed[1:2, :] / pair_width)
    for e in range(owned):
        new_line[e : e + 1, :] = down_cols[:, e * rank : (e + 1) * rank]
        new_upper[e : e + 1, :] = up_rows[:, e * rank : (e + 1) * rank]
    ratio = down_cols / (summed[2:3, :] / full_width)
    index = lax.broadcasted_iota(jnp.int32, (128, span), 0)
    back = jnp.where(index == 0, ratio, up_rows).T
    down_scale = lax.rsqrt(back[:, 0:1])
    up_column = back[:, 1:2].reshape(owned, rank, 1)
    up_mean = jnp.sum(up_column, axis=1, keepdims=True) / rank
    up_scale = lax.rsqrt(up_column / up_mean).reshape(span, 1)

    for j in range(pieces):
        if j < pieces - 1:
            row_scale = lax.rsqrt(new_rows[:, j * piece : (j + 1) * piece])
            column_scale = down_scale
        else:
            row_scale = lax.rsqrt(new_columns[...])
            column_scale = up_scale
        row_scale = jnp.broadcast_to(row_scale[:, None, :], (owned, rank, piece)).reshape(span, piece)
        total_part(j)[...] = total_part(j)[...] * row_scale * column_scale

    for i in range(chunks - 3, chunks):
        finish(i)

    def sent(src, dst, ss, **where):
        remote(src, dst, ss, ag_recv.at[0, 0], **where).wait_send()

    sent(gv.at[0], gv.at[1], ag_send.at[0], tensor=z ^ 1)

    @pl.when(middle)
    def _():
        sent(gv.at[0], gv.at[3], ag_send.at[1], tensor=z ^ 3)
        sent(gv.at[1], gv.at[2], ag_send.at[2], tensor=z ^ 3)
        sent(gv.at[3], gv.at[2], ag_send.at[3], tensor=z ^ 1)
        sent(gv.at[2], gv.at[3], ag_send.at[4], tensor=z ^ 1)

    for m in range(2):
        own(m).wait_send()
        dst = maps[m][1]
        lines = pl.ds(0, span // 2)
        sent(dst.at[2, lines], dst.at[2, lines], x_send.at[m], dp=d ^ 2)
        sent(dst.at[2, lines], dst.at[2, lines], y_send.at[m], rep=rep ^ 1)
        sent(dst.at[2], dst.at[3], c_send.at[m], dp=d ^ 1)

    @pl.when(end)
    def _():
        send_far.wait_send()
        send_near.wait_send()

    @pl.when(middle)
    def _():
        send_cross.wait_send()
        near_end.wait_send()
        near_cross.wait_send()
        far_end.wait_send()

    for j in range(pieces):
        to_core(1, j).wait_send()
    sent(far_out, far_got, far_send.at[0], dp=d ^ 2)
    for k in (1, 2, 3):
        to_line(k).wait_send()


def hand_over_kernel(count, steps, *refs):
    sources, targets, sem = refs[:count], refs[count : 2 * count], refs[2 * count]
    copies = []
    for k in range(count):
        rows = sources[k].shape[0] // steps[k]
        for i in range(steps[k]):
            at = pl.ds(i * rows, rows)
            copies.append(
                pltpu.make_async_copy(sources[k].at[at], targets[k].at[at], sem.at[len(copies)])
            )
    for copy in copies:
        copy.start()
    for copy in copies:
        copy.wait()


def hand_over(results):
    count = len(results)
    steps = [4 if r.shape[0] % 64 == 0 else 1 for r in results]
    return pl.pallas_call(
        functools.partial(hand_over_kernel, count, steps),
        out_shape=tuple(jax.ShapeDtypeStruct(r.shape, r.dtype) for r in results),
        in_specs=[pl.BlockSpec(memory_space=pltpu.VMEM)] * count,
        out_specs=(pl.BlockSpec(memory_space=pl.ANY),) * count,
        scratch_shapes=[pltpu.SemaphoreType.DMA((sum(steps),))],
        compiler_params=pltpu.CompilerParams(vmem_limit_bytes=HAND_LIMIT),
        name="hand_over",
    )(*[pltpu.with_memory_space_constraint(r, pltpu.VMEM) for r in results])


def fused(activations, output_gradient, tenants, live_count, entry_of, weight, down_maps, up_maps, factors):
    rows, depth = activations.shape
    width = output_gradient.shape[1]
    owned, _, rank = down_maps.shape
    span = owned * rank
    chunks, quarter = 7, 4
    piece = width
    pieces = depth // piece + 1
    half = rows // 2
    any_spec = pl.BlockSpec(memory_space=pl.ANY)
    vmem = pl.BlockSpec(memory_space=pltpu.VMEM)
    dma = pltpu.SemaphoreType.DMA
    scratch = [
        pltpu.VMEM((rows, 128), jnp.int32),
        pltpu.VMEM((1, rows), jnp.int32),
        pltpu.VMEM((1, rows), jnp.int32),
        pltpu.VMEM((1, 1), jnp.int32),
        pltpu.VMEM((1, 4 * owned), jnp.int32),
        pltpu.VMEM((owned, depth), f32),
        pltpu.VMEM((owned, width), f32),
        pltpu.VMEM((owned, rank), f32),
        pltpu.VMEM((owned, rank), f32),
        pltpu.VMEM((4, rows, width), bf16),
        pltpu.VMEM((4, depth, width), bf16),
        pltpu.VMEM((4, span, depth), bf16),
        pltpu.VMEM((4, span, width), bf16),
        pltpu.VMEM((rows, depth), f32),
        pltpu.VMEM((rows, 2 * rank), f32),
        pltpu.VMEM((half, 2 * rank), f32),
        pltpu.VMEM((half, 2 * rank), f32),
        pltpu.VMEM((half, 2 * rank), f32),
        pltpu.VMEM((rows, 2 * rank), bf16),
        pltpu.VMEM((2 * rank, rows), bf16),
        pltpu.VMEM((2, 2, span, rows), bf16),
        pltpu.VMEM((rows // 4, 4 * span), bf16),
        pltpu.VMEM((pieces, span, piece), f32),
        pltpu.VMEM((pieces, span, piece), f32),
        pltpu.VMEM((pieces, span, piece), bf16),
        pltpu.VMEM((pieces, span, piece), bf16),
        pltpu.VMEM((4, 8, span), f32),
        dma((15,)),
        dma((5,)),
        dma((3, chunks)),
        dma((2,)),
        dma((2,)),
        dma((2,)),
        dma((quarter, 2)),
        dma((2,)),
        dma((quarter, 2)),
        dma((2,)),
        dma((2,)),
        dma((6,)),
        dma((5,)),
        dma((2, pieces)),
        dma((2, pieces)),
        dma((1,)),
        dma((pieces,)),
        dma((3,)),
        dma((3,)),
        pltpu.SemaphoreType.REGULAR,
    ]
    results = pl.pallas_call(
        functools.partial(fused_kernel, rank),
        out_shape=(
            pltpu.VMEM((rows, depth), bf16),
            pltpu.VMEM((owned, depth), f32),
            pltpu.VMEM((owned, width), f32),
            pltpu.VMEM((owned, rank), f32),
            pltpu.VMEM((owned, rank), f32),
            pltpu.VMEM((span, depth), f32),
            pltpu.VMEM((span, width), f32),
        ),
        in_specs=[any_spec] * 12,
        out_specs=(vmem,) * 7,
        scratch_shapes=scratch,
        compiler_params=pltpu.CompilerParams(
            collective_id=0, has_side_effects=True, vmem_limit_bytes=VMEM_LIMIT
        ),
        name="fused",
    )(
        activations,
        output_gradient,
        weight,
        down_maps.transpose(0, 2, 1).reshape(span, depth),
        up_maps.reshape(span, width),
        tenants,
        live_count.reshape(1, 1),
        entry_of.reshape(1, 4 * owned),
        *factors,
    )
    return hand_over(results)


def fits(activations, output_gradient, down_maps):
    rows, depth = activations.shape
    width = output_gradient.shape[1]
    owned, _, rank = down_maps.shape
    return (
        lax.axis_size("tensor") == 4
        and lax.axis_size("dp") == 4
        and lax.axis_size("rep") == 2
        and rank == 64
        and owned % 2 == 0
        and owned * rank // 8 % 16 == 0
        and rows % 768 == 0
        and width % 128 == 0
        and depth % width == 0
    )


def dot(a, b, ca, cb):
    return lax.dot_general(a, b, (((ca,), (cb,)), ((), ())), preferred_element_type=f32)


def chip_shift(value, groups, step):
    chips = groups // CORES
    pairs = [(d, (d // CORES + step) % chips * CORES + d % CORES) for d in range(groups)]
    return lax.ppermute(value, "dp", pairs)


def core_swap(value, groups):
    return lax.ppermute(value, "dp", [(d, d ^ 1) for d in range(groups)])


def ring_shift(value, size, step):
    return lax.ppermute(value, "tensor", [(t, (t + step) % size) for t in range(size)])


def total_small(value, size):
    if size > 8:
        return lax.psum(value, "tensor")
    me = lax.axis_index("tensor")
    parts = jnp.zeros((size,) + value.shape, value.dtype)
    parts = lax.dynamic_update_index_in_dim(parts, value, me, 0)
    for step in range(1, size):
        got = ring_shift(value, size, step)
        parts = lax.dynamic_update_index_in_dim(parts, got, (me - step) % size, 0)
    return jnp.sum(parts, axis=0)


def total_rows(value, size):
    if size > 8:
        return lax.psum(value, "tensor").astype(bf16)
    me = lax.axis_index("tensor")
    rows = value.shape[0] // size

    def piece(index):
        return lax.dynamic_slice_in_dim(value, index % size * rows, rows, 0)

    total = piece(me)
    for step in range(1, size):
        total = total + ring_shift(piece(me + step), size, step)
    mine = total.astype(bf16)
    out = jnp.zeros(value.shape, bf16)
    out = lax.dynamic_update_slice_in_dim(out, mine, me * rows, 0)
    for step in range(1, size):
        got = ring_shift(mine, size, step)
        out = lax.dynamic_update_slice_in_dim(out, got, (me - step) % size * rows, 0)
    return out


def shards(
    activations,
    output_gradient,
    row_tenant,
    group_row_count,
    tenant_storage_entry,
    key_value_weight,
    adapter_down_maps,
    adapter_up_maps,
    down_row_factor,
    down_column_factor,
    up_row_factor,
    up_column_factor,
):
    groups = lax.axis_size("dp")
    size = lax.axis_size("tensor")
    chips = groups // CORES
    owned, depth, rank = adapter_down_maps.shape
    width = adapter_up_maps.shape[2]
    entries = owned * groups
    count_rows = activations.shape[0]
    full_width = depth * size
    pair_width = key_value_weight.shape[1]
    here = lax.axis_index("dp")
    chip, core = here // CORES, here % CORES
    if fits(activations, output_gradient, adapter_down_maps):
        input_grad, down_rows, up_cols, down_cols, up_rows, down_update, up_update = fused(
            activations,
            output_gradient,
            row_tenant.reshape(1, count_rows),
            group_row_count,
            tenant_storage_entry,
            key_value_weight,
            adapter_down_maps,
            adapter_up_maps,
            (down_row_factor, up_column_factor, down_column_factor, up_row_factor),
        )
        return (
            input_grad,
            down_rows,
            down_cols,
            up_rows,
            up_cols,
            down_update.reshape(owned, rank, depth).transpose(0, 2, 1),
            up_update.reshape(owned, rank, width),
        )
    gathered = lax.all_gather(output_gradient, "tensor", axis=1, tiled=True)
    own_maps = jnp.concatenate(
        [adapter_down_maps.transpose(0, 2, 1), adapter_up_maps], axis=2
    ).reshape(owned * rank, depth + width)
    blocks = []
    for s in range(chips):
        column = own_maps if s == 0 else chip_shift(own_maps, groups, s)
        blocks.append(jnp.concatenate([column, core_swap(column, groups)], axis=0))
    live = jnp.arange(count_rows, dtype=jnp.int32)[:, None] < group_row_count[0]
    masked = jnp.where(live, output_gradient, jnp.zeros_like(output_gradient))
    tse = tenant_storage_entry
    owner = tse // owned
    place = (
        (chip - owner // CORES) % chips * CORES + (owner % CORES != core).astype(jnp.int32)
    ) * owned + tse % owned
    tenants = row_tenant[:, 0]
    place_of = jnp.sum(
        jnp.where(
            tenants[:, None] == jnp.arange(entries, dtype=jnp.int32)[None, :], place[None, :], 0
        ),
        axis=1,
    )
    span = CORES * owned * rank
    pair = 2 * rank
    lanes = jnp.arange(span, dtype=jnp.int32)[None, :] // rank

    def wide(s):
        return place_of[:, None] == lanes + s * CORES * owned

    def pick(s, product):
        kept = jnp.where(wide(s), product, 0.0)
        both = kept[:, :pair]
        for i in range(1, span // pair):
            both = both + kept[:, i * pair : (i + 1) * pair]
        return both

    picked_down = picked_up = 0.0
    for s in range(chips):
        picked_down += pick(s, dot(activations, blocks[s][:, :depth], 1, 1))
        picked_up += pick(s, dot(masked, blocks[s][:, depth:], 1, 1))
    partial = jnp.concatenate(
        [
            picked_down[:, :rank] + picked_down[:, rank:],
            picked_up[:, :rank] + picked_up[:, rank:],
        ],
        axis=1,
    )
    rounded = total_rows(partial, size)
    zero = jnp.zeros((), bf16)
    repeat_down = jnp.tile(rounded[:, :rank], (1, span // rank))
    repeat_up = jnp.tile(rounded[:, rank:], (1, span // rank))
    half = owned * rank
    spreads = [jnp.where(wide(s), repeat_up, zero) for s in range(chips)]
    pieces = []
    for s in list(range(1, chips)) + [0]:
        spread_down = jnp.where(wide(s), repeat_down, zero)
        terms = [
            adapter_scale
            * jnp.concatenate(
                [
                    dot(spreads[s][:, k : k + half], activations, 0, 0),
                    dot(spread_down[:, k : k + half], masked, 0, 0),
                ],
                axis=1,
            )
            for k in (half, 0)
        ]
        summed = terms[1] + core_swap(terms[0], groups)
        pieces.append(chip_shift(summed.astype(bf16), groups, -s) if s else summed)
    side = lax.optimization_barrier(
        (
            adapter_scale
            * dot(
                jnp.concatenate(spreads, axis=1),
                jnp.concatenate([b[:, :depth] for b in blocks], axis=0),
                1,
                0,
            )
        ).astype(bf16)
    )
    frozen = jnp.where(live, dot(gathered, key_value_weight, 1, 1), 0.0)
    input_grad = (frozen + side.astype(f32)).astype(bf16)
    pieces, input_grad = lax.optimization_barrier((pieces, input_grad))
    grads = sum(p.astype(f32) for p in pieces)
    grads = grads.reshape(owned, rank, depth + width)
    down_gradient, up_gradient = grads[:, :, :depth], grads[:, :, depth:]
    square_down = down_gradient * down_gradient + tiny_floor
    square_up = up_gradient * up_gradient + tiny_floor
    down_rows = decay_rate * down_row_factor + (1.0 - decay_rate) * jnp.mean(square_down, axis=1)
    up_cols = decay_rate * up_column_factor + (1.0 - decay_rate) * jnp.mean(square_up, axis=1)
    stats = jnp.concatenate(
        [
            jnp.sum(square_down, axis=2),
            jnp.sum(square_up, axis=2),
            jnp.broadcast_to(jnp.sum(down_rows, axis=1)[:, None], (owned, pair)),
        ],
        axis=1,
    )
    stats = total_small(stats, size)
    column_total, row_total = stats[:, :rank], stats[:, rank:pair]
    rows_sum = stats[:, pair]
    down_cols = decay_rate * down_column_factor + (1.0 - decay_rate) * (column_total / full_width)
    up_rows = decay_rate * up_row_factor + (1.0 - decay_rate) * (row_total / pair_width)
    second_down = (
        down_rows[:, None, :] * down_cols[:, :, None] / (rows_sum / full_width)[:, None, None]
    )
    second_up = up_rows[:, :, None] * up_cols[:, None, :] / jnp.mean(up_rows, axis=1)[:, None, None]
    down_update = (down_gradient * lax.rsqrt(second_down)).transpose(0, 2, 1)
    up_update = up_gradient * lax.rsqrt(second_up)
    return (input_grad, down_rows, down_cols, up_rows, up_cols, down_update, up_update)


def solution(mesh):
    in_specs = (
        P(("rep", "dp"), "tensor"),
        P(("rep", "dp"), "tensor"),
        P(("rep", "dp"), None),
        P(("rep", "dp")),
        P(),
        P("tensor", None),
        P("dp", "tensor", None),
        P("dp", None, "tensor"),
        P("dp", "tensor"),
        P("dp", None),
        P("dp", None),
        P("dp", "tensor"),
    )
    out_specs = (
        P(("rep", "dp"), "tensor"),
        P(("rep", "dp"), "tensor"),
        P(("rep", "dp"), None),
        P(("rep", "dp"), None),
        P(("rep", "dp"), "tensor"),
        P(("rep", "dp"), "tensor", None),
        P(("rep", "dp"), None, "tensor"),
    )
    return jax.shard_map(shards, mesh=mesh, in_specs=in_specs, out_specs=out_specs, check_vma=False)
```

```python
import functools

import jax
import jax.numpy as jnp
from jax import lax
from jax.experimental import pallas as pl
from jax.experimental.pallas import tpu as pltpu
from jax.sharding import PartitionSpec as P

HAND_LIMIT = 4_000_000
adapter_scale = 0.25
decay_rate = 0.9
tiny_floor = 1e-30
f32 = jnp.float32
bf16 = jnp.bfloat16
CORES = 2
VMEM_LIMIT = 57_000_000
MESH = pl.DeviceIdType.MESH
EARLY = 3
BEFORE = 3
HEADS = 2


def dot_nt(a, b):
    return lax.dot_general(a, b, (((1,), (1,)), ((), ())), preferred_element_type=jnp.float32)


def dot_nn(a, b):
    return lax.dot_general(a, b, (((1,), (0,)), ((), ())), preferred_element_type=jnp.float32)


def fused_kernel(
    rank,
    x_hbm,
    g_hbm,
    w_hbm,
    down_hbm,
    up_hbm,
    tenants_hbm,
    live_hbm,
    entry_hbm,
    row_hbm,
    column_hbm,
    line_hbm,
    upper_hbm,
    xv,
    new_rows,
    new_columns,
    new_line,
    new_upper,
    total_down,
    total_up,
    place_col,
    place_row,
    tenants,
    live_count,
    entry_of,
    row_factor,
    column_factor,
    line_factor,
    upper_factor,
    gv,
    wv,
    bd,
    bu,
    acc,
    part,
    far_in,
    near_in,
    cross_in,
    rounded,
    turned,
    spread,
    side_lhs,
    pair_out,
    pair_in,
    far_out,
    far_got,
    stat_all,
    load_sem,
    ag_send,
    ag_recv,
    own_send,
    own_recv,
    x_send,
    x_recv,
    y_send,
    y_recv,
    c_send,
    c_recv,
    rs_send,
    rs_recv,
    pair_send,
    pair_recv,
    far_send,
    far_recv,
    stat_send,
    stat_recv,
    credit,
):
    z = lax.axis_index("tensor")
    d = lax.axis_index("dp")
    rep = lax.axis_index("rep")
    middle = (z == 1) | (z == 2)
    end = (z == 0) | (z == 3)
    rows, depth = xv.shape
    width = gv.shape[2]
    span = bd.shape[1]
    owned = span // rank
    chunks = ag_recv.shape[1]
    size = rows // (chunks - 1)
    bounds = [i * size for i in range(chunks - 1)] + [rows - size // 2, rows]
    half = rows // 2
    tile = rows // 4
    cols = 512 if depth % 512 == 0 else depth
    wide = depth // cols
    piece = width
    pieces = depth // piece + 1
    quarter = x_recv.shape[0]
    step = span // 2 // quarter
    near_at = pl.multiple_of(z // 2 * half, half)
    far_at = pl.multiple_of((1 - z // 2) * half, half)

    def total_part(j):
        if j < pieces - 1:
            return total_down.at[:, j * piece : (j + 1) * piece]
        return total_up

    def remote(src, dst, ss, rs, **where):
        return pltpu.make_async_remote_copy(
            src_ref=src, dst_ref=dst, send_sem=ss, recv_sem=rs, device_id=where, device_id_type=MESH
        )

    def local(src, dst, sem):
        return pltpu.make_async_copy(src, dst, sem)

    barrier = pltpu.get_barrier_semaphore()
    peers = [
        {"tensor": z ^ 1},
        {"tensor": z ^ 2},
        {"tensor": z ^ 3},
        {"dp": d ^ 1},
        {"dp": d ^ 2},
        {"rep": rep ^ 1},
    ]
    for peer in peers:
        pl.semaphore_signal(barrier, inc=1, device_id=peer, device_id_type=MESH)
    loads = [
        local(g_hbm, gv.at[0], load_sem.at[0]),
        local(down_hbm, bd.at[0], load_sem.at[1]),
        local(up_hbm, bu.at[0], load_sem.at[2]),
        local(x_hbm, xv, load_sem.at[3]),
    ]
    for k in range(4):
        at = pl.multiple_of((z ^ k) * width, width)
        loads.append(local(w_hbm.at[:, pl.ds(at, width)], wv.at[k], load_sem.at[4 + k]))
    smalls = [
        local(tenants_hbm, tenants, load_sem.at[8]),
        local(live_hbm, live_count, load_sem.at[9]),
        local(entry_hbm, entry_of, load_sem.at[10]),
        local(row_hbm, row_factor, load_sem.at[11]),
        local(column_hbm, column_factor, load_sem.at[12]),
        local(line_hbm, line_factor, load_sem.at[13]),
        local(upper_hbm, upper_factor, load_sem.at[14]),
    ]
    for copy in smalls + loads:
        copy.start()

    pl.semaphore_wait(barrier, len(peers))

    def chunk(i):
        return pl.ds(bounds[i], bounds[i + 1] - bounds[i])

    def to_pair(i):
        return remote(
            g_hbm.at[chunk(i)], gv.at[1, chunk(i)], ag_send.at[0], ag_recv.at[0, i], tensor=z ^ 1
        )

    def to_cross(i):
        return remote(
            g_hbm.at[chunk(i)], gv.at[3, chunk(i)], ag_send.at[1], ag_recv.at[2, i], tensor=z ^ 3
        )

    def relay_cross(i):
        return remote(
            gv.at[1, chunk(i)], gv.at[2, chunk(i)], ag_send.at[2], ag_recv.at[1, i], tensor=z ^ 3
        )

    def relay_end(i):
        return remote(
            gv.at[3, chunk(i)], gv.at[2, chunk(i)], ag_send.at[3], ag_recv.at[1, i], tensor=z ^ 1
        )

    def relay_last(i):
        return remote(
            gv.at[2, chunk(i)], gv.at[3, chunk(i)], ag_send.at[4], ag_recv.at[2, i], tensor=z ^ 1
        )

    def arrive(slot, i):
        remote(
            gv.at[slot, chunk(i)], gv.at[slot, chunk(i)], ag_send.at[0], ag_recv.at[slot - 1, i], tensor=z ^ 1
        ).wait_recv()

    for i in range(chunks - 2):
        to_pair(i).start()

    @pl.when(middle)
    def _():
        for i in range(chunks - 2, chunks):
            to_pair(i).start()
        for i in range(chunks):
            to_cross(i).start()

    maps = ((down_hbm, bd), (up_hbm, bu))

    def own(m):
        src, dst = maps[m]
        return remote(src, dst.at[1], own_send.at[m], own_recv.at[m], dp=d ^ 1)

    mine = rep * (span // 2)
    other = (1 - rep) * (span // 2)

    def part_rows(base, q):
        return pl.ds(pl.multiple_of(base + q * step, step), step)

    def over_x(q, m):
        src, dst = maps[m]
        at = part_rows(mine, q)
        return remote(src.at[at], dst.at[2, at], x_send.at[m], x_recv.at[q, m], dp=d ^ 2)

    def over_y(q, m):
        dst = maps[m][1]
        at = part_rows(mine, q)
        return remote(dst.at[2, at], dst.at[2, at], y_send.at[m], y_recv.at[q, m], rep=rep ^ 1)

    def over_core(q, m, base, k):
        dst = maps[m][1]
        at = part_rows(base, q)
        return remote(dst.at[2, at], dst.at[3, at], c_send.at[m], c_recv.at[m], dp=d ^ 1)

    for q in range(quarter):
        for m in range(2):
            over_x(q, m).start()
    for m in range(2):
        own(m).start()

    for copy in smalls:
        copy.wait()
    named = tenants[...]
    entry = entry_of[...]
    owner = sum((entry >= k * owned).astype(jnp.int32) for k in range(1, 4))
    chip = (owner >= 2).astype(jnp.int32)
    away = (chip != d // 2).astype(jnp.int32) * 2 + (owner - 2 * chip != d % 2).astype(jnp.int32)
    spot = away * owned + (entry - owner * owned)
    found = jnp.zeros((1, rows), jnp.int32)
    for t in range(entry_of.shape[1]):
        found = jnp.where(named == t, jnp.broadcast_to(spot[:, t : t + 1], (1, rows)), found)
    alive = lax.broadcasted_iota(jnp.int32, (1, rows), 1) < live_count[0]
    place_row[...] = jnp.where(alive, found, -1)

    def stand(i, _):
        at = pl.ds(pl.multiple_of(i * 128, 128), 128)
        lines = jnp.broadcast_to(place_row[:, at].astype(jnp.float32), (128, 128))
        place_col[at, :] = lines.T.astype(jnp.int32)
        return 0

    lax.fori_loop(0, rows // 128, stand, 0)

    def place_wide(at, lanes):
        return jnp.concatenate([place_col[at, :]] * (lanes // 128), axis=1)

    lane = lax.broadcasted_iota(jnp.int32, (tile, span), 1) // rank
    low = lax.broadcasted_iota(jnp.int32, (tile, 2 * rank), 1) < rank

    def project(b, base=0, count=rows // tile):
        def body(i, _):
            at = pl.ds(pl.multiple_of(base + i * tile, tile), tile)
            hit = place_wide(at, span) == lane + b * owned

            def fold(product):
                kept = jnp.where(hit, product, 0.0)
                both = kept[:, : 2 * rank]
                for j in range(1, span // (2 * rank)):
                    both = both + kept[:, j * 2 * rank : (j + 1) * 2 * rank]
                return both + pltpu.roll(both, rank, axis=1)

            new = jnp.where(
                low,
                fold(dot_nt(xv[at, :], bd[b])),
                fold(dot_nt(gv[0, at, :], bu[b])),
            )
            part[at, :] = new if b == 0 else part[at, :] + new
            return 0

        lax.fori_loop(0, count, body, 0)

    def frozen(k, first, start, count):
        def body(t, _):
            i, j = t // wide, t % wide
            at = pl.ds(pl.multiple_of(i * tile, tile), tile)
            over = pl.ds(pl.multiple_of(j * cols, cols), cols)
            new = dot_nt(gv[k, at, :], wv[k, over, :])
            acc[at, over] = new if first else acc[at, over] + new
            return 0

        lax.fori_loop(start * wide, (start + count) * wide, body, 0)

    for k in range(4):
        loads[k].wait()
    project(0)
    for m in range(2):
        own(m).wait_recv()
    loads[4].wait()
    for q in range(quarter):
        if q == quarter - 2:
            project(1)
        else:
            frozen(0, True, min(q, 2), 1)
        for m in range(2):
            over_x(q, m).wait_recv()
            over_y(q, m).start()
            over_core(q, m, mine, 0).start()
    for q in range(quarter):
        for m in range(2):
            dst = maps[m][1]
            at = part_rows(other, q)
            remote(dst.at[2, at], dst.at[2, at], y_send.at[m], y_recv.at[q, m], rep=rep ^ 1).wait_recv()
            over_core(q, m, other, 1).start()
        if q == 0:
            frozen(0, True, 3, 1)
    project(2)
    for m in range(2):
        dst = maps[m][1]
        remote(dst.at[2], dst.at[3], c_send.at[m], c_recv.at[m], dp=d ^ 1).wait_recv()
    project(3, far_at, rows // tile // 2)

    near = pl.ds(near_at, half)
    far = pl.ds(far_at, half)
    send_far = remote(part.at[far], far_in, rs_send.at[0], rs_recv.at[0], tensor=z ^ 1)
    send_near = remote(part.at[near], near_in, rs_send.at[1], rs_recv.at[1], tensor=z ^ 1)
    send_cross = remote(far_in, cross_in, rs_send.at[2], rs_recv.at[2], tensor=z ^ 3)
    near_end = remote(rounded.at[near], rounded.at[near], rs_send.at[3], rs_recv.at[3], tensor=z ^ 1)
    near_cross = remote(rounded.at[near], rounded.at[near], rs_send.at[4], rs_recv.at[4], tensor=z ^ 3)
    far_end = remote(rounded.at[far], rounded.at[far], rs_send.at[5], rs_recv.at[4], tensor=z ^ 1)

    def seen(t):
        return sum(b < t * tile for b in bounds[:-1])

    def outward(i):
        arrive(3, i)
        relay_end(i).start()

    def across(i):
        arrive(1, i)
        relay_cross(i).start()

    @pl.when(end)
    def _():
        send_far.start()

    project(3, near_at, rows // tile // 2)

    def gather(slot, tiles):
        for t in tiles:
            for i in range(seen(t), seen(t + 1)):
                arrive(slot, i)

    for k in (5, 6, 7):
        loads[k].wait()

    @pl.when(end)
    def _():
        send_near.start()
        for i in range(chunks - 2, chunks):
            to_pair(i).start()
        gather(1, range(4))
        frozen(1, False, 0, 4)
        for t in range(HEADS):
            gather(2, (t,))
            frozen(2, False, t, 1)
        remote(rounded.at[near], rounded.at[near], rs_send.at[3], rs_recv.at[3], tensor=z ^ 1).wait_recv()
        remote(rounded.at[far], rounded.at[far], rs_send.at[4], rs_recv.at[4], tensor=z ^ 1).wait_recv()

    @pl.when(middle)
    def _():
        for i in range(EARLY):
            outward(i)
        across(0)
        send_far.wait_recv()
        far_in[...] = part[far, :] + far_in[...]
        send_cross.start()
        outward(chunks - 1)
        for i in range(1, seen(3)):
            arrive(1, i)
        frozen(1, False, 0, 3)
        send_near.wait_recv()
        send_cross.wait_recv()
        rounded[near, :] = ((part[near, :] + near_in[...]) + cross_in[...]).astype(jnp.bfloat16)
        near_cross.start()
        near_end.start()
        for i in range(seen(3), chunks):
            arrive(1, i)
        for i in range(1, chunks):
            relay_cross(i).start()
        remote(rounded.at[far], rounded.at[far], rs_send.at[4], rs_recv.at[4], tensor=z ^ 3).wait_recv()
        far_end.start()
        for i in range(EARLY, chunks - 1):
            outward(i)

    def turn(i, _):
        at = pl.ds(pl.multiple_of(i * 128, 128), 128)
        turned[:, at] = rounded[at, :].astype(jnp.float32).T.astype(jnp.bfloat16)
        return 0

    lax.fori_loop(0, rows // 128, turn, 0)

    head = lax.broadcasted_iota(jnp.int32, (span, 128), 0) // rank

    def fill(b, put_in):
        def body(i, _):
            at = pl.ds(pl.multiple_of(i * 128, 128), 128)
            hit = place_row[:, at] == head + b * owned
            both = turned[:, at].astype(jnp.float32)
            for which, lines in ((0, both[rank:]), (1, both[:rank])):
                lines = jnp.concatenate([lines] * owned, axis=0)
                spread[put_in, which, :, at] = jnp.where(hit, lines, 0.0).astype(jnp.bfloat16)
            return 0

        lax.fori_loop(0, rows // 128, body, 0)

    def product(j, taken):
        if j < pieces - 1:
            return 0.25 * dot_nn(spread[taken, 0], xv[:, j * piece : (j + 1) * piece])
        return 0.25 * dot_nn(spread[taken, 1], gv[0])

    def to_core(k, j):
        return remote(
            pair_out.at[j], pair_in.at[j], pair_send.at[k, j], pair_recv.at[k, j], dp=d ^ 1
        )

    def to_chip(j):
        return remote(far_out.at[j], far_got.at[j], far_send.at[0], far_recv.at[j], dp=d ^ 2)

    def last(i):
        @pl.when(middle)
        def _():
            arrive(2, i)
            relay_last(i).start()

    def last(i):
        @pl.when(middle)
        def _():
            arrive(2, i)
            relay_last(i).start()

    def exchange(k, use):
        def offer(j):
            if k == 1:
                to_core(0, j).wait_send()
            pair_out[j] = product(j, 0)
            to_core(k, j).start()

        offer(0)
        for j in range(pieces):
            if j + 1 < pieces:
                offer(j + 1)
            ours = product(j, 1)
            to_core(k, j).wait_recv()
            use(j, ours + pair_in[j])

    def send_chip(j, value):
        far_out[j] = value.astype(jnp.bfloat16)
        to_chip(j).start()

    def keep(j, value):
        total_part(j)[...] = value

    fill(3, 0)
    fill(2, 1)
    with jax.named_scope("EX0"):
        exchange(0, send_chip)
    pl.semaphore_signal(credit, inc=1, device_id={"dp": d ^ 1}, device_id_type=MESH)
    for i in range(chunks // 3):
        last(i)
    fill(1, 0)
    fill(0, 1)
    pl.semaphore_wait(credit, 1)
    with jax.named_scope("EX1"):
        exchange(1, keep)
    @pl.when(end)
    def _():
        for t in range(HEADS, 4):
            gather(2, (t,))
            frozen(2, False, t, 1)

    @pl.when(middle)
    def _():
        frozen(1, False, 3, 1)

    lane_side = lax.broadcasted_iota(jnp.int32, (tile, 2 * rank), 1) // rank

    def add_side(i, _):
        at = pl.ds(pl.multiple_of(i * tile, tile), tile)
        both = rounded[at, :].astype(jnp.float32)
        both = jnp.where(low, pltpu.roll(both, rank, axis=1), both)
        owner = place_col[at, :]
        for t in range(side_lhs.shape[1] // (2 * rank)):
            side_lhs[:, t * 2 * rank : (t + 1) * 2 * rank] = jnp.where(
                owner == lane_side + 2 * t, both, 0.0
            ).astype(jnp.bfloat16)

        def column(j, _):
            over = pl.ds(pl.multiple_of(j * cols, cols), cols)
            right = bd[:, :, over].reshape(4 * span, cols)
            acc[at, over] = acc[at, over] + 0.25 * dot_nn(side_lhs[...], right)
            return 0

        lax.fori_loop(0, wide, column, 0)
        return 0

    lax.fori_loop(0, rows // tile, add_side, 0)
    for i in range(chunks // 3, chunks - 2):
        last(i)

    @pl.when(middle)
    def _():
        for i in range(chunks - 2, chunks):
            arrive(2, i)
        frozen(2, False, 0, 4)


    def finish(i):
        @pl.when(end)
        def _():
            arrive(3, i)

        at = chunk(i)
        alive = place_wide(at, cols) >= 0

        def column(j, _):
            over = pl.ds(pl.multiple_of(j * cols, cols), cols)
            value = acc[at, over] + dot_nt(gv[3, at, :], wv[3, over, :])
            xv[at, over] = jnp.where(alive, value, 0.0).astype(jnp.bfloat16)
            return 0

        lax.fori_loop(0, wide, column, 0)

    for i in range(BEFORE):
        finish(i)

    share = 1.0 - decay_rate
    line = jnp.zeros((span, 1), jnp.float32)
    upper = jnp.zeros((span, 1), jnp.float32)
    rows_sum = jnp.zeros((owned, 1), jnp.float32)
    for j in range(pieces):
        to_chip(j).wait_recv()
        value = total_part(j)[...] + far_got[j].astype(jnp.float32)
        total_part(j)[...] = value
        square = value * value + tiny_floor
        mean = jnp.sum(square.reshape(owned, rank, piece), axis=1) / rank
        if j < pieces - 1:
            over = slice(j * piece, (j + 1) * piece)
            fresh = decay_rate * row_factor[:, over] + share * mean
            new_rows[:, over] = fresh
            rows_sum = rows_sum + jnp.sum(fresh, axis=1, keepdims=True)
            line = line + jnp.sum(square, axis=1, keepdims=True)
        else:
            new_columns[...] = decay_rate * column_factor[...] + share * mean
            upper = jnp.sum(square, axis=1, keepdims=True)
    place = lax.broadcasted_iota(jnp.int32, (span, 128), 1)
    spread_sum = jnp.broadcast_to(rows_sum[:, None, :], (owned, rank, 1)).reshape(span, 1)
    packed = jnp.where(place == 0, line, jnp.where(place == 1, upper, spread_sum))
    stat_all[z] = packed.T[:8, :]

    def to_line(k):
        return remote(
            stat_all.at[z], stat_all.at[z], stat_send.at[k - 1], stat_recv.at[k - 1], tensor=z ^ k
        )

    for k in (1, 2, 3):
        to_line(k).start()

    @pl.when(middle)
    def _():
        for i in range(chunks - 2, chunks):
            relay_last(i).start()

    for i in range(BEFORE, chunks - 3):
        finish(i)
    for k in (1, 2, 3):
        remote(
            stat_all.at[z ^ k], stat_all.at[z ^ k], stat_send.at[k - 1], stat_recv.at[k - 1], tensor=z ^ k
        ).wait_recv()
    summed = (stat_all[0] + stat_all[1]) + (stat_all[2] + stat_all[3])
    full_width = depth * 4
    pair_width = width * 4

    def in_line(ref):
        return jnp.concatenate([ref[e : e + 1, :] for e in range(owned)], axis=1)

    down_cols = decay_rate * in_line(line_factor) + share * (summed[0:1, :] / full_width)
    up_rows = decay_rate * in_line(upper_factor) + share * (summed[1:2, :] / pair_width)
    for e in range(owned):
        new_line[e : e + 1, :] = down_cols[:, e * rank : (e + 1) * rank]
        new_upper[e : e + 1, :] = up_rows[:, e * rank : (e + 1) * rank]
    ratio = down_cols / (summed[2:3, :] / full_width)
    index = lax.broadcasted_iota(jnp.int32, (128, span), 0)
    back = jnp.where(index == 0, ratio, up_rows).T
    down_scale = lax.rsqrt(back[:, 0:1])
    up_column = back[:, 1:2].reshape(owned, rank, 1)
    up_mean = jnp.sum(up_column, axis=1, keepdims=True) / rank
    up_scale = lax.rsqrt(up_column / up_mean).reshape(span, 1)

    for j in range(pieces):
        if j < pieces - 1:
            row_scale = lax.rsqrt(new_rows[:, j * piece : (j + 1) * piece])
            column_scale = down_scale
        else:
            row_scale = lax.rsqrt(new_columns[...])
            column_scale = up_scale
        row_scale = jnp.broadcast_to(row_scale[:, None, :], (owned, rank, piece)).reshape(span, piece)
        total_part(j)[...] = total_part(j)[...] * row_scale * column_scale

    for i in range(chunks - 3, chunks):
        finish(i)

    def sent(src, dst, ss, **where):
        remote(src, dst, ss, ag_recv.at[0, 0], **where).wait_send()

    sent(gv.at[0], gv.at[1], ag_send.at[0], tensor=z ^ 1)

    @pl.when(middle)
    def _():
        sent(gv.at[0], gv.at[3], ag_send.at[1], tensor=z ^ 3)
        sent(gv.at[1], gv.at[2], ag_send.at[2], tensor=z ^ 3)
        sent(gv.at[3], gv.at[2], ag_send.at[3], tensor=z ^ 1)
        sent(gv.at[2], gv.at[3], ag_send.at[4], tensor=z ^ 1)

    for m in range(2):
        own(m).wait_send()
        dst = maps[m][1]
        lines = pl.ds(0, span // 2)
        sent(dst.at[2, lines], dst.at[2, lines], x_send.at[m], dp=d ^ 2)
        sent(dst.at[2, lines], dst.at[2, lines], y_send.at[m], rep=rep ^ 1)
        sent(dst.at[2], dst.at[3], c_send.at[m], dp=d ^ 1)

    @pl.when(end)
    def _():
        send_far.wait_send()
        send_near.wait_send()

    @pl.when(middle)
    def _():
        send_cross.wait_send()
        near_end.wait_send()
        near_cross.wait_send()
        far_end.wait_send()

    for j in range(pieces):
        to_core(1, j).wait_send()
    sent(far_out, far_got, far_send.at[0], dp=d ^ 2)
    for k in (1, 2, 3):
        to_line(k).wait_send()


def hand_over_kernel(count, steps, *refs):
    sources, targets, sem = refs[:count], refs[count : 2 * count], refs[2 * count]
    copies = []
    for k in range(count):
        rows = sources[k].shape[0] // steps[k]
        for i in range(steps[k]):
            at = pl.ds(i * rows, rows)
            copies.append(
                pltpu.make_async_copy(sources[k].at[at], targets[k].at[at], sem.at[len(copies)])
            )
    for copy in copies:
        copy.start()
    for copy in copies:
        copy.wait()


def hand_over(results):
    count = len(results)
    steps = [4 if r.shape[0] % 64 == 0 else 1 for r in results]
    return pl.pallas_call(
        functools.partial(hand_over_kernel, count, steps),
        out_shape=tuple(jax.ShapeDtypeStruct(r.shape, r.dtype) for r in results),
        in_specs=[pl.BlockSpec(memory_space=pltpu.VMEM)] * count,
        out_specs=(pl.BlockSpec(memory_space=pl.ANY),) * count,
        scratch_shapes=[pltpu.SemaphoreType.DMA((sum(steps),))],
        compiler_params=pltpu.CompilerParams(vmem_limit_bytes=HAND_LIMIT),
        name="hand_over",
    )(*[pltpu.with_memory_space_constraint(r, pltpu.VMEM) for r in results])


def fused(activations, output_gradient, tenants, live_count, entry_of, weight, down_maps, up_maps, factors):
    rows, depth = activations.shape
    width = output_gradient.shape[1]
    owned, _, rank = down_maps.shape
    span = owned * rank
    chunks, quarter = 7, 4
    piece = width
    pieces = depth // piece + 1
    half = rows // 2
    any_spec = pl.BlockSpec(memory_space=pl.ANY)
    vmem = pl.BlockSpec(memory_space=pltpu.VMEM)
    dma = pltpu.SemaphoreType.DMA
    scratch = [
        pltpu.VMEM((rows, 128), jnp.int32),
        pltpu.VMEM((1, rows), jnp.int32),
        pltpu.VMEM((1, rows), jnp.int32),
        pltpu.SMEM((1,), jnp.int32),
        pltpu.VMEM((1, 4 * owned), jnp.int32),
        pltpu.VMEM((owned, depth), f32),
        pltpu.VMEM((owned, width), f32),
        pltpu.VMEM((owned, rank), f32),
        pltpu.VMEM((owned, rank), f32),
        pltpu.VMEM((4, rows, width), bf16),
        pltpu.VMEM((4, depth, width), bf16),
        pltpu.VMEM((4, span, depth), bf16),
        pltpu.VMEM((4, span, width), bf16),
        pltpu.VMEM((rows, depth), f32),
        pltpu.VMEM((rows, 2 * rank), f32),
        pltpu.VMEM((half, 2 * rank), f32),
        pltpu.VMEM((half, 2 * rank), f32),
        pltpu.VMEM((half, 2 * rank), f32),
        pltpu.VMEM((rows, 2 * rank), bf16),
        pltpu.VMEM((2 * rank, rows), bf16),
        pltpu.VMEM((2, 2, span, rows), bf16),
        pltpu.VMEM((rows // 4, 4 * span), bf16),
        pltpu.VMEM((pieces, span, piece), f32),
        pltpu.VMEM((pieces, span, piece), f32),
        pltpu.VMEM((pieces, span, piece), bf16),
        pltpu.VMEM((pieces, span, piece), bf16),
        pltpu.VMEM((4, 8, span), f32),
        dma((15,)),
        dma((5,)),
        dma((3, chunks)),
        dma((2,)),
        dma((2,)),
        dma((2,)),
        dma((quarter, 2)),
        dma((2,)),
        dma((quarter, 2)),
        dma((2,)),
        dma((2,)),
        dma((6,)),
        dma((5,)),
        dma((2, pieces)),
        dma((2, pieces)),
        dma((1,)),
        dma((pieces,)),
        dma((3,)),
        dma((3,)),
        pltpu.SemaphoreType.REGULAR,
    ]
    results = pl.pallas_call(
        functools.partial(fused_kernel, rank),
        out_shape=(
            pltpu.VMEM((rows, depth), bf16),
            pltpu.VMEM((owned, depth), f32),
            pltpu.VMEM((owned, width), f32),
            pltpu.VMEM((owned, rank), f32),
            pltpu.VMEM((owned, rank), f32),
            pltpu.VMEM((span, depth), f32),
            pltpu.VMEM((span, width), f32),
        ),
        in_specs=[any_spec] * 12,
        out_specs=(vmem,) * 7,
        scratch_shapes=scratch,
        compiler_params=pltpu.CompilerParams(
            collective_id=0, has_side_effects=True, vmem_limit_bytes=VMEM_LIMIT
        ),
        name="fused",
    )(
        activations,
        output_gradient,
        weight,
        down_maps.transpose(0, 2, 1).reshape(span, depth),
        up_maps.reshape(span, width),
        tenants,
        live_count,
        entry_of.reshape(1, 4 * owned),
        *factors,
    )
    return hand_over(results)


def fits(activations, output_gradient, down_maps):
    rows, depth = activations.shape
    width = output_gradient.shape[1]
    owned, _, rank = down_maps.shape
    return (
        lax.axis_size("tensor") == 4
        and lax.axis_size("dp") == 4
        and lax.axis_size("rep") == 2
        and rank == 64
        and owned % 2 == 0
        and owned * rank // 8 % 16 == 0
        and rows % 768 == 0
        and width % 128 == 0
        and depth % width == 0
    )


def dot(a, b, ca, cb):
    return lax.dot_general(a, b, (((ca,), (cb,)), ((), ())), preferred_element_type=f32)


def chip_shift(value, groups, step):
    chips = groups // CORES
    pairs = [(d, (d // CORES + step) % chips * CORES + d % CORES) for d in range(groups)]
    return lax.ppermute(value, "dp", pairs)


def core_swap(value, groups):
    return lax.ppermute(value, "dp", [(d, d ^ 1) for d in range(groups)])


def ring_shift(value, size, step):
    return lax.ppermute(value, "tensor", [(t, (t + step) % size) for t in range(size)])


def total_small(value, size):
    if size > 8:
        return lax.psum(value, "tensor")
    me = lax.axis_index("tensor")
    parts = jnp.zeros((size,) + value.shape, value.dtype)
    parts = lax.dynamic_update_index_in_dim(parts, value, me, 0)
    for step in range(1, size):
        got = ring_shift(value, size, step)
        parts = lax.dynamic_update_index_in_dim(parts, got, (me - step) % size, 0)
    return jnp.sum(parts, axis=0)


def total_rows(value, size):
    if size > 8:
        return lax.psum(value, "tensor").astype(bf16)
    me = lax.axis_index("tensor")
    rows = value.shape[0] // size

    def piece(index):
        return lax.dynamic_slice_in_dim(value, index % size * rows, rows, 0)

    total = piece(me)
    for step in range(1, size):
        total = total + ring_shift(piece(me + step), size, step)
    mine = total.astype(bf16)
    out = jnp.zeros(value.shape, bf16)
    out = lax.dynamic_update_slice_in_dim(out, mine, me * rows, 0)
    for step in range(1, size):
        got = ring_shift(mine, size, step)
        out = lax.dynamic_update_slice_in_dim(out, got, (me - step) % size * rows, 0)
    return out


def shards(
    activations,
    output_gradient,
    row_tenant,
    group_row_count,
    tenant_storage_entry,
    key_value_weight,
    adapter_down_maps,
    adapter_up_maps,
    down_row_factor,
    down_column_factor,
    up_row_factor,
    up_column_factor,
):
    groups = lax.axis_size("dp")
    size = lax.axis_size("tensor")
    chips = groups // CORES
    owned, depth, rank = adapter_down_maps.shape
    width = adapter_up_maps.shape[2]
    entries = owned * groups
    count_rows = activations.shape[0]
    full_width = depth * size
    pair_width = key_value_weight.shape[1]
    here = lax.axis_index("dp")
    chip, core = here // CORES, here % CORES
    if fits(activations, output_gradient, adapter_down_maps):
        input_grad, down_rows, up_cols, down_cols, up_rows, down_update, up_update = fused(
            activations,
            output_gradient,
            row_tenant.reshape(1, count_rows),
            group_row_count,
            tenant_storage_entry,
            key_value_weight,
            adapter_down_maps,
            adapter_up_maps,
            (down_row_factor, up_column_factor, down_column_factor, up_row_factor),
        )
        return (
            input_grad,
            down_rows,
            down_cols,
            up_rows,
            up_cols,
            down_update.reshape(owned, rank, depth).transpose(0, 2, 1),
            up_update.reshape(owned, rank, width),
        )
    gathered = lax.all_gather(output_gradient, "tensor", axis=1, tiled=True)
    own_maps = jnp.concatenate(
        [adapter_down_maps.transpose(0, 2, 1), adapter_up_maps], axis=2
    ).reshape(owned * rank, depth + width)
    blocks = []
    for s in range(chips):
        column = own_maps if s == 0 else chip_shift(own_maps, groups, s)
        blocks.append(jnp.concatenate([column, core_swap(column, groups)], axis=0))
    live = jnp.arange(count_rows, dtype=jnp.int32)[:, None] < group_row_count[0]
    masked = jnp.where(live, output_gradient, jnp.zeros_like(output_gradient))
    tse = tenant_storage_entry
    owner = tse // owned
    place = (
        (chip - owner // CORES) % chips * CORES + (owner % CORES != core).astype(jnp.int32)
    ) * owned + tse % owned
    tenants = row_tenant[:, 0]
    place_of = jnp.sum(
        jnp.where(
            tenants[:, None] == jnp.arange(entries, dtype=jnp.int32)[None, :], place[None, :], 0
        ),
        axis=1,
    )
    span = CORES * owned * rank
    pair = 2 * rank
    lanes = jnp.arange(span, dtype=jnp.int32)[None, :] // rank

    def wide(s):
        return place_of[:, None] == lanes + s * CORES * owned

    def pick(s, product):
        kept = jnp.where(wide(s), product, 0.0)
        both = kept[:, :pair]
        for i in range(1, span // pair):
            both = both + kept[:, i * pair : (i + 1) * pair]
        return both

    picked_down = picked_up = 0.0
    for s in range(chips):
        picked_down += pick(s, dot(activations, blocks[s][:, :depth], 1, 1))
        picked_up += pick(s, dot(masked, blocks[s][:, depth:], 1, 1))
    partial = jnp.concatenate(
        [
            picked_down[:, :rank] + picked_down[:, rank:],
            picked_up[:, :rank] + picked_up[:, rank:],
        ],
        axis=1,
    )
    rounded = total_rows(partial, size)
    zero = jnp.zeros((), bf16)
    repeat_down = jnp.tile(rounded[:, :rank], (1, span // rank))
    repeat_up = jnp.tile(rounded[:, rank:], (1, span // rank))
    half = owned * rank
    spreads = [jnp.where(wide(s), repeat_up, zero) for s in range(chips)]
    pieces = []
    for s in list(range(1, chips)) + [0]:
        spread_down = jnp.where(wide(s), repeat_down, zero)
        terms = [
            adapter_scale
            * jnp.concatenate(
                [
                    dot(spreads[s][:, k : k + half], activations, 0, 0),
                    dot(spread_down[:, k : k + half], masked, 0, 0),
                ],
                axis=1,
            )
            for k in (half, 0)
        ]
        summed = terms[1] + core_swap(terms[0], groups)
        pieces.append(chip_shift(summed.astype(bf16), groups, -s) if s else summed)
    side = lax.optimization_barrier(
        (
            adapter_scale
            * dot(
                jnp.concatenate(spreads, axis=1),
                jnp.concatenate([b[:, :depth] for b in blocks], axis=0),
                1,
                0,
            )
        ).astype(bf16)
    )
    frozen = jnp.where(live, dot(gathered, key_value_weight, 1, 1), 0.0)
    input_grad = (frozen + side.astype(f32)).astype(bf16)
    pieces, input_grad = lax.optimization_barrier((pieces, input_grad))
    grads = sum(p.astype(f32) for p in pieces)
    grads = grads.reshape(owned, rank, depth + width)
    down_gradient, up_gradient = grads[:, :, :depth], grads[:, :, depth:]
    square_down = down_gradient * down_gradient + tiny_floor
    square_up = up_gradient * up_gradient + tiny_floor
    down_rows = decay_rate * down_row_factor + (1.0 - decay_rate) * jnp.mean(square_down, axis=1)
    up_cols = decay_rate * up_column_factor + (1.0 - decay_rate) * jnp.mean(square_up, axis=1)
    stats = jnp.concatenate(
        [
            jnp.sum(square_down, axis=2),
            jnp.sum(square_up, axis=2),
            jnp.broadcast_to(jnp.sum(down_rows, axis=1)[:, None], (owned, pair)),
        ],
        axis=1,
    )
    stats = total_small(stats, size)
    column_total, row_total = stats[:, :rank], stats[:, rank:pair]
    rows_sum = stats[:, pair]
    down_cols = decay_rate * down_column_factor + (1.0 - decay_rate) * (column_total / full_width)
    up_rows = decay_rate * up_row_factor + (1.0 - decay_rate) * (row_total / pair_width)
    second_down = (
        down_rows[:, None, :] * down_cols[:, :, None] / (rows_sum / full_width)[:, None, None]
    )
    second_up = up_rows[:, :, None] * up_cols[:, None, :] / jnp.mean(up_rows, axis=1)[:, None, None]
    down_update = (down_gradient * lax.rsqrt(second_down)).transpose(0, 2, 1)
    up_update = up_gradient * lax.rsqrt(second_up)
    return (input_grad, down_rows, down_cols, up_rows, up_cols, down_update, up_update)


def solution(mesh):
    in_specs = (
        P(("rep", "dp"), "tensor"),
        P(("rep", "dp"), "tensor"),
        P(("rep", "dp"), None),
        P(("rep", "dp")),
        P(),
        P("tensor", None),
        P("dp", "tensor", None),
        P("dp", None, "tensor"),
        P("dp", "tensor"),
        P("dp", None),
        P("dp", None),
        P("dp", "tensor"),
    )
    out_specs = (
        P(("rep", "dp"), "tensor"),
        P(("rep", "dp"), "tensor"),
        P(("rep", "dp"), None),
        P(("rep", "dp"), None),
        P(("rep", "dp"), "tensor"),
        P(("rep", "dp"), "tensor", None),
        P(("rep", "dp"), None, "tensor"),
    )
    return jax.shard_map(shards, mesh=mesh, in_specs=in_specs, out_specs=out_specs, check_vma=False)
```
